128 devices in a mesh: dp: 16 (over y, x), section: 2 (over core), tensor: 4 (over z).
Axes of the slice: x: 4, y: 4, z: 4, core: 2. Of those that a mesh axis runs over, the one named last changes fastest.
Arguments:
- fwd_state: bfloat16 [2, 2048, 4096], P('section', ('dp', 'tensor')), may hold values from -6 to 6
- bwd_state: bfloat16 [2, 2048, 4096], P('section', ('dp', 'tensor')), may hold values from -6 to 6
- stash: bfloat16 [2, 2, 2048, 4096], P('section', None, ('dp', 'tensor')), may hold values from -6 to 6
- gains: bfloat16 [2, 2, 4096], P('section'), may hold values from 0.25 to 1.75
- w_query: bfloat16 [2, 2, 4096, 4096], P('section', None, 'dp', 'tensor'), may hold values from -0.09375 to 0.09375
- w_key: bfloat16 [2, 2, 4096, 1024], P('section', None, 'dp', 'tensor'), may hold values from -0.09375 to 0.09375
- w_value: bfloat16 [2, 2, 4096, 1024], P('section', None, 'dp', 'tensor'), may hold values from -0.09375 to 0.09375
- w_out: bfloat16 [2, 2, 4096, 4096], P('section', None, 'tensor', 'dp'), may hold values from -0.09375 to 0.09375
- fwd_segments: int32 [2, 16, 128], P(None, 'dp'), may hold values from 0 to 3, never falling along the last dimension, each value on 1 to 64 neighbouring positions
- bwd_segments: int32 [2, 16, 128], P(None, 'dp'), may hold values from 0 to 3, never falling along the last dimension, each value on 1 to 64 neighbouring positions
Outputs:
- fwd_out: bfloat16 [2, 2048, 4096], P('section', ('dp', 'tensor'))
- bwd_out: bfloat16 [2, 2048, 4096], P('section', ('dp', 'tensor'))
- gain_grad: float32 [2, 2, 4096], P('section')
The draws below stay inside these ranges and needn't reach their ends.
Inputs may be any that keep to these rules, and one draw needn't show every extreme that they name: `fwd_segments`: in each replica's rows of each micro-batch the document ids never fall; each document has at most 64 rows and one has exactly that many. `bwd_segments`: in each replica's rows of each micro-batch the document ids never fall; each document has at most 64 rows and one has exactly that many.
All inputs are finite; a program needn't handle non-finite values.
Results may differ from the reference program's by a relative error of at most 0.02.
Values may be sent and summed in bfloat16 or wider, within the bound.
No kernel may reach another device: no remote copies, remote signals or barrier semaphores. Data moves between devices by JAX's collectives and lax.ppermute only.
A program may use at most 192 MiB of HBM per device.

```python
import math
import jax
import jax.numpy as jnp
import numpy as np
from jax import lax

D = 4096
HEADS = 32
KV = 8
HD = 128
R = 128
TICKS = 2
SECTIONS = 2
REPLICAS = 16
ROWS = 2048
N_DP = 16
N_SECTION = 2
N_TENSOR = 4


def steps_of(rng, extent, shards, least, largest):
    def one(axis_at, blocks):
        steps = jax.random.uniform(jax.random.fold_in(jax.random.fold_in(rng, 6), axis_at), (blocks,), jnp.float32, least / len(shards), largest / len(shards))
        return jnp.repeat(jnp.exp(steps), extent[axis_at] // blocks).reshape((-1,) + (1,) * (len(extent) - axis_at - 1))

    level = one(*shards[0])
    for cut in shards[1:]:
        level = level * one(*cut)
    return level


def profile(amount, total, limit, lean):
    loads = [(1 << 20) // math.isqrt(rank ** lean) + 1 for rank in range(2, amount + 1)]
    rest, counts = total - limit - (amount - 1), [1] * (amount - 1)
    while rest > 0:
        movable = [i for i in range(amount - 1) if counts[i] < limit]
        pool, budget = sum([loads[i] for i in movable]), rest
        for i in movable:
            more = min(limit - counts[i], max(1, budget * loads[i] // pool), rest)
            counts[i] = counts[i] + more
            rest = rest - more
    return np.array([limit] + counts)


def ragged(own_key, count, total, reach, skew):
    if count == 2:
        one = jax.random.randint(own_key, (), max(1, total - reach), min(reach, total - 1) + 1)
        return jnp.stack([one, total - one])
    lengths = jnp.asarray(profile(count, total, reach, skew), jnp.int32)
    twos = (count - 1) // 2
    giver, taker = lengths[1:1 + 2 * twos:2], lengths[2:2 + 2 * twos:2]
    room = jnp.minimum(giver - 1, reach - taker)
    passed = jax.random.randint(jax.random.fold_in(own_key, 1), (twos,), 0, 1 << 20) % (room + 1)
    lengths = lengths.at[1:1 + 2 * twos:2].set(giver - passed).at[2:2 + 2 * twos:2].set(taker + passed)
    return lengths[jax.random.permutation(jax.random.fold_in(own_key, 2), count)]


def normal_values(key, extent, spread, reach, shards=(), kind=jnp.bfloat16):
    factor_of = steps_of(key, extent, shards, -0.22, 0.18) if shards else 1.0
    result = jax.random.normal(key, extent, jnp.float32) * spread * factor_of
    return jnp.minimum(jnp.maximum(result, -reach), reach).astype(kind)


def setup_inputs(seed: int = 0) -> dict:
    keys = jax.random.split(jax.random.key(seed), 11)
    return {
        "fwd_state": normal_values(keys[0], (SECTIONS, ROWS, D), 1.0, 6.0, ((0, 2), (1, 64))),
        "bwd_state": normal_values(keys[1], (SECTIONS, ROWS, D), 1.0, 6.0, ((0, 2), (1, 64))),
        "stash": normal_values(keys[2], (SECTIONS, TICKS, ROWS, D), 1.0, 6.0, ((0, 2), (2, 64))),
        "gains": jnp.clip(1.0 + 0.15 * jax.random.normal(keys[3], (SECTIONS, 2, D), jnp.float32), 0.25, 1.75).astype(jnp.bfloat16),
        "w_query": normal_values(keys[4], (SECTIONS, 2, D, HEADS * HD), D ** -0.5, 0.09375, ((0, 2), (2, 16), (3, 4))),
        "w_key": normal_values(keys[5], (SECTIONS, 2, D, KV * HD), D ** -0.5, 0.09375, ((0, 2), (2, 16), (3, 4))),
        "w_value": normal_values(keys[6], (SECTIONS, 2, D, KV * HD), D ** -0.5, 0.09375, ((0, 2), (2, 16), (3, 4))),
        "w_out": normal_values(keys[7], (SECTIONS, 2, HEADS * HD, D), (HEADS * HD) ** -0.5, 0.09375, ((0, 2), (2, 4), (3, 16))),
        "fwd_segments": jax.vmap(lambda own: jnp.searchsorted(jnp.cumsum(ragged(own, 4, R, R // 2, 0)), jnp.arange(R), side="right"))(jax.random.split(keys[8], SECTIONS * REPLICAS)).reshape((SECTIONS, REPLICAS, R)).astype(jnp.int32),
        "bwd_segments": jax.vmap(lambda own: jnp.searchsorted(jnp.cumsum(ragged(own, 4, R, R // 2, 0)), jnp.arange(R), side="right"))(jax.random.split(keys[9], SECTIONS * REPLICAS)).reshape((SECTIONS, REPLICAS, R)).astype(jnp.int32),
    }


ROPE_BASE = 1000000.0

def rope_tables(segments):
    count_rows = segments.shape[0]
    row_index = jnp.arange(count_rows, dtype=jnp.int32)
    previous = jnp.concatenate([segments[:1] - 1, segments[:-1]])
    doc_starts = lax.cummax(jnp.where(segments != previous, row_index, 0), axis=0)
    positions = (row_index - doc_starts).astype(jnp.float32)
    halfway = HD // 2
    frequency = jnp.exp(jnp.arange(halfway, dtype=jnp.float32) * (-2.0 * math.log(ROPE_BASE) / HD))
    angles = positions[:, None] * frequency[None, :]
    cosine = jnp.concatenate([jnp.cos(angles), jnp.cos(angles)], axis=1)
    sine_table = jnp.concatenate([jnp.sin(angles), jnp.sin(angles)], axis=1)
    allowed = (segments[:, None] == segments[None, :]) & (row_index[:, None] >= row_index[None, :])
    return (cosine[:, None, :], sine_table[:, None, :], allowed)

def rotate(vectors, cosine, sine_table):
    halfway = vectors.shape[-1] // 2
    turned = jnp.concatenate([-vectors[..., halfway:], vectors[..., :halfway]], axis=-1)
    return vectors * cosine + turned * sine_table

def partial_layer(state_rows, gain_vector, w_query, w_key, w_value, w_out, segments):
    count_rows = state_rows.shape[0]
    cosine, sine_table, allowed = rope_tables(segments)
    variance = lax.optimization_barrier(jnp.mean(state_rows * state_rows, axis=1, keepdims=True))
    normed = (state_rows * lax.rsqrt(variance + 1e-06) * gain_vector).astype(jnp.bfloat16)
    query_rows = jnp.dot(normed, w_query, preferred_element_type=jnp.float32).reshape(count_rows, -1, HD)
    key_rows = jnp.dot(normed, w_key, preferred_element_type=jnp.float32).reshape(count_rows, -1, HD)
    value_rows = jnp.dot(normed, w_value, preferred_element_type=jnp.float32).astype(jnp.bfloat16)
    value_rows = value_rows.reshape(count_rows, -1, HD)
    query_rows = rotate(query_rows, cosine, sine_table).astype(jnp.bfloat16)
    key_rows = rotate(key_rows, cosine, sine_table).astype(jnp.bfloat16)
    key_heads = key_rows.shape[1]
    grouped = query_rows.reshape(count_rows, key_heads, -1, HD)
    scores = jnp.einsum('qkgd,skd->kgqs', grouped.astype(jnp.float32), key_rows.astype(jnp.float32))
    scores = scores * (1.0 / math.sqrt(HD))
    scores = jnp.where(allowed[None, None], scores, -1e+30)
    exponents = jnp.exp(scores)
    soft_weights = (exponents / lax.optimization_barrier(jnp.sum(exponents, axis=-1, keepdims=True))).astype(jnp.bfloat16)
    mixed_heads = jnp.einsum('kgqs,skd->qkgd', soft_weights.astype(jnp.float32), value_rows.astype(jnp.float32))
    mixed_heads = mixed_heads.astype(jnp.bfloat16).reshape(count_rows, -1)
    return jnp.dot(mixed_heads, w_out, preferred_element_type=jnp.float32)

def round_trip(terms):
    return lax.optimization_barrier(terms.astype(jnp.bfloat16)).astype(jnp.float32)

def pick_span(table, span):
    return lax.dynamic_index_in_dim(table, span, 0, keepdims=False)

def split_groups(w_query, w_key, w_value, w_out, span):
    query_pick = pick_span(w_query, span)
    key_pick = pick_span(w_key, span)
    value_pick = pick_span(w_value, span)
    out_pick = pick_span(w_out, span)
    model_width = query_pick.shape[0]
    return (query_pick.reshape(model_width, N_TENSOR, -1).transpose(1, 0, 2), key_pick.reshape(model_width, N_TENSOR, -1).transpose(1, 0, 2), value_pick.reshape(model_width, N_TENSOR, -1).transpose(1, 0, 2), out_pick.reshape(N_TENSOR, -1, model_width))

def phase_forward(operands):
    state_block, gains, w_query, w_key, w_value, w_out, span, segments = operands
    gain_vector = pick_span(gains, span).astype(jnp.float32)
    group_query, group_key, group_value, group_out = split_groups(w_query, w_key, w_value, w_out, span)

    def one_replica(rows_in, segment_row):

        def one_group(query_part, key_part, value_part, out_part):
            return partial_layer(rows_in.astype(jnp.float32), gain_vector, query_part, key_part, value_part, out_part, segment_row)
        terms = jax.vmap(one_group)(group_query, group_key, group_value, group_out)
        return lax.optimization_barrier(jnp.sum(round_trip(terms), axis=0))
    summed = jax.vmap(one_replica)(state_block, segments)
    return (state_block.astype(jnp.float32) + summed).astype(jnp.bfloat16)

def phase_backward(operands):
    stash_block, cotangent, gains, w_query, w_key, w_value, w_out, span, segments = operands
    gain_vector = pick_span(gains, span).astype(jnp.float32)
    group_query, group_key, group_value, group_out = split_groups(w_query, w_key, w_value, w_out, span)

    def one_replica(rows_in, cot_rows, segment_row):

        def one_group(query_part, key_part, value_part, out_part):

            def local(state_in, gain_in):
                return partial_layer(state_in, gain_in, query_part, key_part, value_part, out_part, segment_row)
            unused, pull = jax.vjp(local, rows_in.astype(jnp.float32), gain_vector)
            return pull(cot_rows.astype(jnp.float32))
        state_terms, gain_terms = jax.vmap(one_group)(group_query, group_key, group_value, group_out)
        return (lax.optimization_barrier(jnp.sum(round_trip(state_terms), axis=0)), lax.optimization_barrier(jnp.sum(gain_terms, axis=0)))
    row_terms, gain_terms = jax.vmap(one_replica)(stash_block, cotangent, segments)
    returned = (cotangent.astype(jnp.float32) + row_terms).astype(jnp.bfloat16)
    return (returned, lax.optimization_barrier(jnp.sum(gain_terms, axis=0)))

def reference(fwd_state, bwd_state, stash, gains, w_query, w_key, w_value, w_out, fwd_segments, bwd_segments):
    model_width = fwd_state.shape[2]
    forward_blocks = fwd_state.reshape(N_SECTION, N_DP, R, model_width)
    backward_blocks = bwd_state.reshape(N_SECTION, N_DP, R, model_width)
    stash_blocks = stash.reshape(N_SECTION, TICKS, N_DP, R, model_width)
    phase_ids = jnp.arange(N_SECTION, dtype=jnp.int32)
    span_ids = jnp.arange(2, dtype=jnp.int32)
    gain_grad = jnp.zeros((N_SECTION, 2, model_width), jnp.float32)
    for tick_index in range(TICKS):
        fwd_span = jnp.where(phase_ids < tick_index, 1, 0).astype(jnp.int32)
        fwd_rows = fwd_segments[(phase_ids - tick_index) % N_SECTION]
        advanced = lax.map(phase_forward, (forward_blocks, gains, w_query, w_key, w_value, w_out, fwd_span, fwd_rows))
        bwd_span = jnp.where(phase_ids > N_SECTION - 1 - tick_index, 0, 1).astype(jnp.int32)
        bwd_rows = bwd_segments[(phase_ids + tick_index) % N_SECTION]
        returned, gain_terms = lax.map(phase_backward, (stash_blocks[:, tick_index], backward_blocks, gains, w_query, w_key, w_value, w_out, bwd_span, bwd_rows))
        chosen = (span_ids[None, :] == bwd_span[:, None]).astype(jnp.float32)
        gain_grad = gain_grad + chosen[:, :, None] * gain_terms[:, None, :]
        forward_blocks = jnp.roll(advanced, 1, axis=0)
        backward_blocks = jnp.roll(returned, -1, axis=0)
    return (forward_blocks.reshape(N_SECTION, N_DP * R, model_width), backward_blocks.reshape(N_SECTION, N_DP * R, model_width), gain_grad)
```

```python
import math

import jax
import jax.numpy as jnp
from jax import lax
from jax.sharding import Mesh, PartitionSpec as P

HD = 128
ROPE_BASE = 1000000.0
BF = jnp.bfloat16
F32 = jnp.float32

CHIP = ("xh", "xl", "s")


def spot(xh, xl, core):
    return (xh * 2 + xl) * 2 + core


PLACES = [(xh, xl, core) for xh in (0, 1) for xl in (0, 1) for core in (0, 1)]
SIBLING = [(spot(a, l, c), spot(a, l, 1 - c)) for a, l, c in PLACES]
ACROSS = [(spot(a, l, c), spot(1 - a, 1 - l, c)) for a, l, c in PLACES]
BESIDE = [(spot(a, l, c), spot(a, 1 - l, c)) for a, l, c in PLACES]
HOME = [
    (spot(a, l, c), spot(a, l, 1 - c) if c == a else spot(1 - a, 1 - l, c)) for a, l, c in PLACES
]
GUEST = [(spot(a, l, c), spot(1 - a, 1 - l, 1 - c)) for a, l, c in PLACES if c != a]


def chip_move(value, pairs):
    return lax.ppermute(value, CHIP, pairs)


def shift(value, axis, steps):
    count = lax.axis_size(axis)
    return lax.ppermute(value, axis, [(i, (i + steps) % count) for i in range(count)])


RING = (0, 3, 1, 2)
RING_BACK = (0, 2, 3, 1)


def take(value, order, axis):
    parts = [lax.index_in_dim(value, k, axis, keepdims=True) for k in order]
    return jnp.concatenate(parts, axis=axis)


def flip_if(flag, value, axis):
    return jnp.where(flag, jnp.flip(value, axis), value)


def to_relative(value):
    y, a, l = lax.axis_index("y"), lax.axis_index("xh"), lax.axis_index("xl")
    lead, width = value.shape[:-1], value.shape[-1]
    n = len(lead)
    v = value.reshape(lead + (4, width // 4))
    v = take(jnp.roll(v, -y, axis=n), RING, n)
    v = v.reshape(lead + (4, 2, 2, width // 16))
    v = flip_if(l == 1, flip_if(a == 1, v, n + 1), n + 2)
    v = take(v.reshape(lead + (4, 4, width // 16)), RING, n + 1)
    return v.reshape(value.shape)


def to_absolute(value):
    y, a, l = lax.axis_index("y"), lax.axis_index("xh"), lax.axis_index("xl")
    lead, width = value.shape[:-1], value.shape[-1]
    n = len(lead)
    v = take(value.reshape(lead + (4, 4, width // 16)), RING_BACK, n + 1)
    v = v.reshape(lead + (4, 2, 2, width // 16))
    v = flip_if(l == 1, flip_if(a == 1, v, n + 1), n + 2)
    v = take(v.reshape(lead + (4, width // 4)), RING_BACK, n)
    return jnp.roll(v, y, axis=n).reshape(value.shape)


def to_partner(value):
    lead, width = value.shape[:-1], value.shape[-1]
    v = value.reshape(lead + (4, 2, 2, width // 16))
    return jnp.flip(v, len(lead) + 2).reshape(value.shape)


def gather_rows(value):
    half = value.shape[1] // 2
    before, after = shift(value, "z", 1), shift(value, "z", -1)
    top, bottom = shift(before[:, :half], "z", 1), shift(after[:, half:], "z", -1)
    mine = jnp.concatenate([value, before, after, top, bottom], axis=1)
    return jnp.concatenate([mine, chip_move(mine, SIBLING)], axis=1)


def scatter_rows(terms):
    rows = terms.shape[0] // 2
    block = rows // 4
    mine = terms[:rows] + chip_move(terms[rows:].astype(BF), SIBLING).astype(F32)
    parts = [mine[k * block : (k + 1) * block] for k in range(4)]
    total = parts[0]
    total = total + shift(parts[1].astype(BF), "z", -1).astype(F32)
    total = total + shift(parts[2].astype(BF), "z", 1).astype(F32)
    return total + shift(parts[3].astype(BF), "z", 2).astype(F32)


def rms_scale(rows):
    return lax.rsqrt(jnp.mean(rows * rows, axis=1, keepdims=True) + 1e-06)


def both_slots(halves, match, a):
    kept = lax.dynamic_index_in_dim(halves, a, 0, keepdims=False)
    home = chip_move(lax.dynamic_index_in_dim(halves, 1 - a, 0, keepdims=False), HOME)
    guest = chip_move(kept, GUEST)
    return jnp.concatenate(
        [jnp.where(match, kept, home), jnp.where(match, home, guest)], axis=0
    )


def gather_beside_first(base):
    both = jnp.concatenate([base, chip_move(base, BESIDE)], axis=0)
    half = base.shape[0]
    before, after = shift(both, "y", 1), shift(both, "y", -1)
    top, bottom = shift(before[:half], "y", 1), shift(after[half:], "y", -1)
    return [both, before, after, top, bottom]


def gather_ring_first(base):
    half = base.shape[0] // 2
    before, after = shift(base, "y", 1), shift(base, "y", -1)
    top, bottom = shift(before[:half], "y", 1), shift(after[half:], "y", -1)
    opposite = jnp.concatenate([top, bottom], axis=0)
    parts = []
    for part in (base, before, after, opposite):
        parts += [part, chip_move(part, BESIDE)]
    return parts


def times(rows, parts):
    total, at = None, 0
    for part in parts:
        term = jnp.dot(rows[:, at : at + part.shape[0]], part, preferred_element_type=F32)
        total = term if total is None else total + term
        at += part.shape[0]
    return total


def times_turned(rows, parts):
    return jnp.concatenate(
        [
            lax.dot_general(rows, part, (((1,), (1,)), ((), ())), preferred_element_type=F32)
            for part in parts
        ],
        axis=1,
    )


def tables(segments, z):
    count = segments.shape[1]
    block = count // 4
    index = jnp.broadcast_to(jnp.arange(count, dtype=jnp.int32), segments.shape)
    starts = jnp.sum((segments[:, None, :] < segments[:, :, None]).astype(jnp.int32), axis=2)

    def relative(v):
        v = v.reshape(2, 4, block)
        return take(jnp.roll(v, -z, axis=1), RING, 1).reshape(2, count)

    positions = relative(index - starts).astype(F32)
    ids, index = relative(segments), relative(index)
    halfway = HD // 2
    frequency = jnp.exp(jnp.arange(halfway, dtype=F32) * (-2.0 * math.log(ROPE_BASE) / HD))
    angles = positions[:, :, None] * frequency
    cosine, sine = jnp.cos(angles), jnp.sin(angles)
    cosine = jnp.concatenate([cosine, cosine], axis=2)
    sine = jnp.concatenate([sine, sine], axis=2)
    allowed = (ids[:, :, None] == ids[:, None, :]) & (index[:, :, None] >= index[:, None, :])
    return cosine[:, :, None], sine[:, :, None], allowed[:, None]


def turn(v):
    halfway = HD // 2
    return jnp.concatenate([-v[..., halfway:], v[..., :halfway]], axis=-1)


def heads_of(projected, table):
    cosine, sine, unused = table
    width = projected.shape[1]
    query = projected[:, : width - 2 * HD].reshape(2, -1, width // HD - 2, HD)
    key = projected[:, width - 2 * HD : width - HD].reshape(2, -1, 1, HD)
    value = projected[:, width - HD :].astype(BF).reshape(2, -1, HD)
    query = (query * cosine + turn(query) * sine).astype(BF)
    key = (key * cosine + turn(key) * sine).astype(BF)[:, :, 0]
    return query, key, value


def probabilities(query, key, allowed):
    scores = jnp.einsum("bqgd,bkd->bgqk", query, key, preferred_element_type=F32)
    scores = jnp.where(allowed, scores * (1.0 / math.sqrt(HD)), -1e30)
    exponents = jnp.exp(scores)
    return exponents / jnp.sum(exponents, axis=-1, keepdims=True)


def layer_terms(normed, qkv, out, table):
    query, key, value = heads_of(times(normed, qkv), table)
    probs = probabilities(query, key, table[2]).astype(BF)
    mixed = jnp.einsum("bgqk,bkd->bqgd", probs, value, preferred_element_type=F32)
    mixed = mixed.astype(BF).reshape(normed.shape[0], -1)
    return times_turned(mixed, out)


def backward_saved(normed, qkv, table):
    query, key, value = heads_of(times(normed, qkv), table)
    return query, key, value, probabilities(query, key, table[2])


def backward_terms(saved, cotangent, qkv, out, table):
    query, key, value, probs = saved
    cosine, sine, unused = table
    d_mixed = times(cotangent, out).astype(BF).reshape(query.shape)
    d_value = jnp.einsum("bgqk,bqgd->bkd", probs.astype(BF), d_mixed, preferred_element_type=F32)
    d_probs = jnp.einsum("bqgd,bkd->bgqk", d_mixed, value, preferred_element_type=F32)
    centre = jnp.sum(d_probs * probs, axis=-1, keepdims=True)
    d_scores = (probs * (d_probs - centre) * (1.0 / math.sqrt(HD))).astype(BF)
    d_query = jnp.einsum("bgqk,bkd->bqgd", d_scores, key, preferred_element_type=F32)
    d_key = jnp.einsum("bgqk,bqgd->bkd", d_scores, query, preferred_element_type=F32)
    d_key = d_key[:, :, None]
    d_query = (d_query * cosine - turn(d_query) * sine).astype(BF)
    d_key = (d_key * cosine - turn(d_key) * sine).astype(BF)
    rows = cotangent.shape[0]
    d_projected = jnp.concatenate(
        [d_query.reshape(rows, -1), d_key.reshape(rows, -1), d_value.astype(BF).reshape(rows, -1)],
        axis=1,
    )
    return times_turned(d_projected, qkv)


def sum_gains(part):
    part = part + shift(part, "z", 1) + shift(part, "z", -1) + shift(part, "z", 2)
    part = part + shift(part, "y", 1) + shift(part, "y", -1) + shift(part, "y", 2)
    part = part + chip_move(part, SIBLING)
    part = part + chip_move(part, BESIDE)
    other = chip_move(part, ACROSS)
    return jnp.where(lax.axis_index("s") == lax.axis_index("xh"), part, other)


def per_device(
    fwd_state, bwd_state, stash, gains, w_query, w_key, w_value, w_out, fwd_segments, bwd_segments
):
    a, core, z = lax.axis_index("xh"), lax.axis_index("s"), lax.axis_index("z")
    match = core == a
    width = fwd_state.shape[2]

    local = jnp.concatenate([fwd_state, bwd_state, stash[0]], axis=0)
    rows = to_relative(jnp.where(match, local, chip_move(local, GUEST)))
    state, grad, stash_rows = rows[0], rows[1], rows[2:].astype(F32)
    gain = to_relative(
        jnp.where(match, gains[0], chip_move(gains[0], SIBLING))
    ).astype(F32)
    gain_fwd = [gain[0], jnp.where(a == 0, gain[1], gain[0])]
    gain_bwd = [gain[1], jnp.where(a == 0, gain[1], gain[0])]

    qkv_parts, out_parts = [], []
    block = w_query.shape[2]
    for span in range(2):
        halves = [
            w[0, span].reshape(block, 2, -1).transpose(1, 0, 2) for w in (w_query, w_key, w_value)
        ]
        out_halves = w_out[0, span].reshape(2, -1, block).transpose(0, 2, 1)
        qkv_parts.append(
            gather_beside_first(both_slots(jnp.concatenate(halves, axis=2), match, a))
        )
        out_parts.append(gather_ring_first(both_slots(out_halves, match, a)))
    qkv_late = [jnp.where(a == 0, v, u) for u, v in zip(*qkv_parts)]
    out_late = [jnp.where(a == 0, v, u) for u, v in zip(*out_parts)]

    own_ids = jnp.stack([fwd_segments[:, 0], bwd_segments[:, 0]])
    partner_ids = chip_move(own_ids, ACROSS)
    ids = jnp.stack(
        [jnp.where(match, own_ids, partner_ids), jnp.where(match, partner_ids, own_ids)], axis=2
    )
    straight = [jnp.where(a == 0, ids[k, 0], ids[k, 1]) for k in range(2)]
    crossed = [jnp.where(a == 0, ids[k, 1], ids[k, 0]) for k in range(2)]
    fwd_tables = [tables(straight[0], z), tables(crossed[0], z)]
    bwd_tables = [tables(straight[1], z), tables(crossed[1], z)]

    def normed(rows, gain_row):
        rows = rows.astype(F32)
        return (rows * rms_scale(rows) * gain_row).astype(BF)

    stash_scale = [rms_scale(stash_rows[t]) for t in range(2)]
    first = gather_rows(
        jnp.stack([normed(state, gain_fwd[0]), normed(stash_rows[0], gain_bwd[0])])
    )
    second = gather_rows(jnp.stack([grad, normed(stash_rows[1], gain_bwd[1])]))
    fwd_in, cotangent = first[0], second[0]
    stash_in = [first[1], second[1]]

    gain_sum = jnp.zeros((2, width), F32)
    for tick in range(2):
        qkv_fwd, out_fwd = (qkv_parts[0], out_parts[0]) if tick == 0 else (qkv_late, out_late)
        qkv_bwd, out_bwd = (qkv_parts[1], out_parts[1]) if tick == 0 else (qkv_late, out_late)
        fwd_terms = layer_terms(fwd_in, qkv_fwd, out_fwd, fwd_tables[tick])
        saved = backward_saved(stash_in[tick], qkv_bwd, bwd_tables[tick])
        bwd_terms = backward_terms(saved, cotangent, qkv_bwd, out_bwd, bwd_tables[tick])
        gain_part = jnp.sum(bwd_terms * stash_in[tick].astype(F32), axis=0) / gain_bwd[tick]
        on_first = jnp.where((a == 1) if tick == 1 else False, 1.0, 0.0)
        gain_sum = gain_sum + jnp.stack([gain_part * on_first, gain_part * (1.0 - on_first)])

        state = (state.astype(F32) + scatter_rows(fwd_terms)).astype(BF)
        d_normed = scatter_rows(bwd_terms) * gain_bwd[tick]
        own, scale = stash_rows[tick], stash_scale[tick]
        lean = jnp.mean(own * d_normed, axis=1, keepdims=True) * (scale * scale * scale)
        grad = (grad.astype(F32) + d_normed * scale - own * lean).astype(BF)
        if tick == 0:
            state = to_partner(chip_move(state, ACROSS))
            grad = to_partner(chip_move(grad, ACROSS))
            fwd_in = gather_rows(normed(state, gain_fwd[1])[None])[0]
            cotangent = gather_rows(grad[None])[0]

    state_out = chip_move(to_absolute(state), HOME)
    grad_out = chip_move(to_absolute(grad), HOME)
    gain_total = sum_gains(to_absolute(gain_sum))
    return (state_out[None], grad_out[None], gain_total[None])


def solution(mesh):
    grid = Mesh(mesh.devices.reshape(4, 2, 2, 2, 4), ("y", "xh", "xl", "s", "z"))
    dp = ("y", "xh", "xl")
    in_specs = (
        P("s", dp + ("z",), None),
        P("s", dp + ("z",), None),
        P("s", None, dp + ("z",), None),
        P("s", None, None),
        P("s", None, dp, "z"),
        P("s", None, dp, "z"),
        P("s", None, dp, "z"),
        P("s", None, "z", dp),
        P(None, dp, None),
        P(None, dp, None),
    )
    out_specs = (
        P("s", dp + ("z",), None),
        P("s", dp + ("z",), None),
        P("s", None, None),
    )
    return jax.shard_map(
        per_device, mesh=grid, in_specs=in_specs, out_specs=out_specs, check_vma=False
    )
```

```python
import math

import jax
import jax.numpy as jnp
from jax import lax
from jax.experimental import pallas as pl
from jax.experimental.pallas import tpu as pltpu
from jax.sharding import Mesh, PartitionSpec as P

HD = 128
ROPE_BASE = 1000000.0
BF = jnp.bfloat16
F32 = jnp.float32

CHIP = ("xh", "xl", "s")


def spot(xh, xl, core):
    return (xh * 2 + xl) * 2 + core


PLACES = [(xh, xl, core) for xh in (0, 1) for xl in (0, 1) for core in (0, 1)]
SIBLING = [(spot(a, l, c), spot(a, l, 1 - c)) for a, l, c in PLACES]
ACROSS = [(spot(a, l, c), spot(1 - a, 1 - l, c)) for a, l, c in PLACES]
BESIDE = [(spot(a, l, c), spot(a, 1 - l, c)) for a, l, c in PLACES]
HOME = [
    (spot(a, l, c), spot(a, l, 1 - c) if c == a else spot(1 - a, 1 - l, c)) for a, l, c in PLACES
]
GUEST = [(spot(a, l, c), spot(1 - a, 1 - l, 1 - c)) for a, l, c in PLACES if c != a]


def chip_move(value, pairs):
    return lax.ppermute(value, CHIP, pairs)


def shift(value, axis, steps):
    count = lax.axis_size(axis)
    return lax.ppermute(value, axis, [(i, (i + steps) % count) for i in range(count)])


RING = (0, 3, 1, 2)
RING_BACK = (0, 2, 3, 1)


NEAR = (0, 3, 1, 2)
GROUP = [
    [(spot(c, l ^ i, a ^ j), spot(a, l, c)) for a, l, c in PLACES] for i in (0, 1) for j in (0, 1)
]
VM = pl.BlockSpec(memory_space=pltpu.VMEM)
SM = pl.BlockSpec(memory_space=pltpu.SMEM)
HB = pl.BlockSpec(memory_space=pl.ANY)
CHUNKS = 8


def shape(dims, kind=BF):
    return jax.ShapeDtypeStruct(dims, kind)


def kernel_call(body, outs, in_specs, scratch=(), flops=0, moved=0):
    return pl.pallas_call(
        body,
        out_shape=outs,
        in_specs=in_specs,
        out_specs=jax.tree.map(lambda unused: VM, outs),
        scratch_shapes=list(scratch),
        cost_estimate=pl.CostEstimate(flops=flops, bytes_accessed=moved, transcendentals=0),
        compiler_params=pltpu.CompilerParams(),
    )


def turned_dot(left, right):
    return lax.dot_general(left, right, (((1,), (1,)), ((), ())), preferred_element_type=F32)


def dot(left, right):
    return jnp.dot(left, right, preferred_element_type=F32)


def split_weights(a, w_query, w_key, w_value, w_out):
    block = w_query.shape[1]
    q_cols, k_cols, o_rows = w_query.shape[2] // 2, w_key.shape[2] // 2, w_out.shape[1] // 2
    wide = q_cols + 2 * k_cols + o_rows

    def body(a_ref, q_ref, k_ref, v_ref, o_ref, *outs):
        for span in range(2):
            for which in range(2):
                half = a_ref[0] if which == 0 else 1 - a_ref[0]
                out = outs[span * 2 + which]
                q_at = pl.multiple_of(half * q_cols, q_cols)
                k_at = pl.multiple_of(half * k_cols, k_cols)
                o_at = pl.multiple_of(half * o_rows, o_rows)
                out[:, :q_cols] = q_ref[span, :, pl.ds(q_at, q_cols)]
                out[:, q_cols : q_cols + k_cols] = k_ref[span, :, pl.ds(k_at, k_cols)]
                out[:, q_cols + k_cols : q_cols + 2 * k_cols] = v_ref[span, :, pl.ds(k_at, k_cols)]
                out[:, q_cols + 2 * k_cols :] = o_ref[span, pl.ds(o_at, o_rows), :].T

    outs = tuple(shape((block, wide)) for unused in range(4))
    return kernel_call(body, outs, [SM] + [VM] * 4, moved=10 << 20)(
        a, w_query, w_key, w_value, w_out
    )


def join_slots(match, kept, home, guest):
    block, wide = kept.shape
    cut = wide - wide * 2 // 5

    def body(match_ref, kept_ref, home_ref, guest_ref, qkv_ref, out_ref):
        def put(at, value_ref):
            qkv_ref[pl.ds(at, block), :] = value_ref[:, :cut]
            out_ref[pl.ds(at, block), :] = value_ref[:, cut:]

        @pl.when(match_ref[0] == 1)
        def own():
            put(0, kept_ref)
            put(block, home_ref)

        @pl.when(match_ref[0] == 0)
        def moved():
            put(0, home_ref)
            put(block, guest_ref)

    outs = (shape((2 * block, cut)), shape((2 * block, wide - cut)))
    return kernel_call(body, outs, [SM] + [VM] * 3, moved=3 << 20)(match, kept, home, guest)


def gather_beside_first(base):
    beside = chip_move(base, BESIDE)
    before, after = shift(base, "y", 1), shift(base, "y", -1)
    before_x, after_x = shift(beside, "y", 1), shift(beside, "y", -1)
    opposite, opposite_x = shift(before, "y", 1), shift(after_x, "y", -1)
    return [base, beside, before, before_x, after, after_x, opposite, opposite_x]


def gather_ring_first(base):
    half = base.shape[0] // 2
    before, after = shift(base, "y", 1), shift(base, "y", -1)
    top, bottom = shift(before[:half], "y", 1), shift(after[half:], "y", -1)
    parts = []
    for group in ((base,), (before,), (after,), (top, bottom)):
        parts += list(group) + [chip_move(part, BESIDE) for part in group]
    return parts


def reorder(order_ref, width, block, take_from, put_to):
    for k in range(width // block):
        at = pl.multiple_of(order_ref[k] * block, block)
        put_to(k * block, take_from(at))


def start_rows(scalars, order, local, guest, gains, gains_sibling):
    kinds, rows, width = local.shape
    block = width // 16

    def body(s_ref, order_ref, local_ref, guest_ref, g_ref, h_ref, first, second, keep, scale, gain):
        match, a = s_ref[0] == 1, s_ref[1]

        def take_gain(at):
            return jnp.where(match, g_ref[:, pl.ds(at, block)], h_ref[:, pl.ds(at, block)])

        def put_gain(at, value):
            gain[:, at : at + block] = value.astype(F32)

        reorder(order_ref, width, block, take_gain, put_gain)
        late = jnp.where(a == 0, gain[1:2, :], gain[0:1, :])
        for kind, (out, slot) in enumerate(((first, 0), (second, 0), (first, 1), (second, 1))):

            def take_rows(at):
                return jnp.where(
                    match, local_ref[kind, :, pl.ds(at, block)], guest_ref[kind, :, pl.ds(at, block)]
                )

            def put_rows(at, value):
                keep[kind, :, at : at + block] = value

            reorder(order_ref, width, block, take_rows, put_rows)
            value = keep[kind]
            if kind == 1:
                out[slot] = value
                continue
            value = value.astype(F32)
            by = lax.rsqrt(jnp.mean(value * value, axis=1, keepdims=True) + 1e-06)
            factor = (gain[0:1, :], None, gain[1:2, :], late)[kind]
            out[slot] = (value * by * factor).astype(BF)
            scale[kind] = jnp.broadcast_to(by, (rows, 128))

    outs = (
        shape((2, rows, width)),
        shape((2, rows, width)),
        shape((kinds, rows, width)),
        shape((kinds, rows, 128), F32),
        shape((2, width), F32),
    )
    return kernel_call(body, outs, [SM, SM] + [VM] * 4, moved=6 << 20)(
        scalars, order, local, guest, gains, gains_sibling
    )


def norm_rows(state, gain_row):
    def body(state_ref, gain_ref, out_ref):
        value = state_ref[...].astype(F32)
        by = lax.rsqrt(jnp.mean(value * value, axis=1, keepdims=True) + 1e-06)
        out_ref[...] = (value * by * gain_ref[...]).astype(BF)

    return kernel_call(body, shape(state.shape), [VM, VM], moved=1 << 19)(state, gain_row)


def gather_rows(value):
    half = value.shape[-2] // 2
    before, after = shift(value, "z", 1), shift(value, "z", -1)
    top, bottom = shift(before[..., :half, :], "z", 1), shift(after[..., half:, :], "z", -1)
    mine = jnp.concatenate([value, before, after, top, bottom], axis=-2)
    return mine, chip_move(mine, SIBLING)


def scatter_rows(mine, other):
    came = chip_move(other, SIBLING)
    rows, width = mine.shape
    block = rows // 4

    def body(mine_ref, came_ref, own, one, two, three):
        for k, out in enumerate((own, one, two, three)):
            at = pl.ds(k * block, block)
            total = mine_ref[at, :].astype(F32) + came_ref[at, :].astype(F32)
            out[...] = total.astype(out.dtype)

    outs = (shape((block, width), F32),) + (shape((block, width)),) * 3
    own, one, two, three = kernel_call(body, outs, [VM, VM], moved=4 << 20)(mine, came)
    return own, shift(one, "z", -1), shift(two, "z", 1), shift(three, "z", 2)


def finish_forward(order, parts, state):
    rows, width = state.shape
    block = width // 16

    def body(order_ref, own, one, two, three, state_ref, out_ref):
        def total(at):
            at = pl.ds(at, block)
            value = own[:, at] + one[:, at].astype(F32) + two[:, at].astype(F32)
            value = value + three[:, at].astype(F32) + state_ref[:, at].astype(F32)
            return value.astype(BF)

        def put(at, value):
            out_ref[:, at : at + block] = value

        reorder(order_ref, width, block, total, put)

    return kernel_call(body, shape((rows, width)), [SM] + [VM] * 5, moved=2 << 20)(
        order, *parts, state
    )


def finish_backward(order, parts, grad, kept, scale, gain_row):
    rows, width = grad.shape
    block = width // 16

    def body(order_ref, own, one, two, three, grad_ref, kept_ref, scale_ref, gain_ref, out_ref, hold):
        by = scale_ref[:, :1]
        pushed = own[...] + one[...].astype(F32) + two[...].astype(F32) + three[...].astype(F32)
        pushed = pushed * gain_ref[...]
        value = kept_ref[...].astype(F32)
        lean = jnp.mean(value * pushed, axis=1, keepdims=True) * (by * by * by)
        hold[...] = (grad_ref[...].astype(F32) + pushed * by - value * lean).astype(BF)

        def put(at, piece):
            out_ref[:, at : at + block] = piece

        reorder(order_ref, width, block, lambda at: hold[:, pl.ds(at, block)], put)

    return kernel_call(
        body,
        shape((rows, width)),
        [SM] + [VM] * 8,
        scratch=[pltpu.VMEM((rows, width), BF)],
        moved=2 << 20,
    )(order, *parts, grad, kept, scale, gain_row)


def stack_copies(parts, target, sems, at):
    copies, row = [], 0
    for k, part in enumerate(parts):
        rows = part.shape[0]
        copies.append(pltpu.make_async_copy(part, target.at[pl.ds(row, rows)], sems.at[at + k]))
        row += rows
    return copies


def start_copies(pick_ref, groups):
    if len(groups) == 1:
        for copy in groups[0]:
            copy.start()
        return
    for span, copies in enumerate(groups):

        @pl.when(pick_ref[0] == span)
        def begin():
            for copy in copies:
                copy.start()


def turn_heads(projected, cosine, sine, heads, back=False):
    outs = []
    for h in range(heads):
        v = projected[:, h * HD : (h + 1) * HD]
        turned = pltpu.roll(v, HD // 2, 1) * sine
        outs.append(v * cosine - turned if back else v * cosine + turned)
    return outs


def project(rows_ref, qkv, copies, cosine, sine, heads_ref, total):
    width = rows_ref.shape[1]
    step = width // CHUNKS
    for k in range(CHUNKS):
        copies[k].wait()
    total[...] = jnp.zeros_like(total)

    def add(k, carry):
        at = pl.ds(pl.multiple_of(k * step, step), step)
        total[...] += dot(rows_ref[:, at], qkv[at, :])
        return carry

    lax.fori_loop(0, CHUNKS, add, 0)
    count = total.shape[1] // HD
    turned = turn_heads(total, cosine[...], sine[...], count - 1)
    for h in range(count - 1):
        heads_ref[:, h * HD : (h + 1) * HD] = turned[h].astype(BF)
    heads_ref[:, (count - 1) * HD :] = total[:, (count - 1) * HD :].astype(BF)


def stack_query(ref, b, rows, groups):
    return jnp.concatenate(
        [ref[b * rows : (b + 1) * rows, g * HD : (g + 1) * HD] for g in range(groups)], axis=0
    )


def probabilities(query, key, keep):
    scores = turned_dot(query, key) * (1.0 / math.sqrt(HD))
    exponents = jnp.exp(jnp.where(keep > 0.0, scores, -1e30))
    return exponents / jnp.sum(exponents, axis=-1, keepdims=True)


def load_rows(index, mine, other, rows_ref, sems):
    half = rows_ref.shape[0] // 2
    return [
        pltpu.make_async_copy(
            src if index is None else src.at[index], rows_ref.at[pl.ds(k * half, half)], sems.at[k]
        )
        for k, src in enumerate((mine, other))
    ]


def layer_call(kind, rows_in, index, tables, pick, qkv_sets, out_sets, saved=None, normed=None):
    mine, other = rows_in
    half, width = mine.shape[-2:]
    rows = 2 * half
    spans = len(qkv_sets)
    q_wide = qkv_sets[0][0].shape[1]
    o_wide = out_sets[0][0].shape[1] if out_sets else 0
    groups = q_wide // HD - 2
    n_qkv = len(qkv_sets[0])
    n_out = len(out_sets[0]) if out_sets else 0
    step = width // CHUNKS

    def body(*refs):
        refs = list(refs)
        pick_ref, mine_ref, other_ref = refs[:3]
        cosine, sine, keep = refs[3:6]
        refs = refs[6:]
        qkv_refs = [refs[s * n_qkv : (s + 1) * n_qkv] for s in range(spans)]
        refs = refs[spans * n_qkv :]
        out_refs = [refs[s * n_out : (s + 1) * n_out] for s in range(spans)]
        refs = refs[spans * n_out :]
        if kind == "backward":
            heads, n_mine, n_other = refs[:3]
            refs = refs[3:]
        n_results = {"forward": 2, "project": 1, "backward": 3}[kind]
        results, refs = refs[:n_results], refs[n_results:]
        rows_ref, qkv, total, sems = refs[:4]
        refs = refs[4:]
        row_copies = load_rows(index, mine_ref, other_ref, rows_ref, sems)
        qkv_copies = [stack_copies(parts, qkv, sems, 4) for parts in qkv_refs]
        if n_out:
            out, mixed = refs[:2]
            out_copies = [stack_copies(parts, out, sems, 4 + n_qkv) for parts in out_refs]
        for copy in row_copies:
            copy.start()
        if kind == "backward":
            start_copies(pick_ref, out_copies)
            start_copies(pick_ref, qkv_copies)
            d_heads, normed_ref = refs[2:]
            more = load_rows(normed[1], n_mine, n_other, normed_ref, sems.at[pl.ds(2, 2)])
            for copy in more:
                copy.start()
        else:
            start_copies(pick_ref, qkv_copies)
            if n_out:
                start_copies(pick_ref, out_copies)
        for copy in row_copies:
            copy.wait()

        if kind == "project":
            project(rows_ref, qkv, qkv_copies[0], cosine, sine, results[0], total)
            return

        if kind == "forward":
            heads = refs[2]
            project(rows_ref, qkv, qkv_copies[0], cosine, sine, heads, total)
            for b in range(2):
                at = slice(b * half, (b + 1) * half)
                query = stack_query(heads, b, half, groups)
                kept = jnp.concatenate([keep[at, :]] * groups, axis=0)
                probs = probabilities(query, heads[at, groups * HD : (groups + 1) * HD], kept)
                got = dot(probs.astype(BF), heads[at, (groups + 1) * HD :]).astype(BF)
                for g in range(groups):
                    mixed[at, g * HD : (g + 1) * HD] = got[g * half : (g + 1) * half]
            for copy in out_copies[0]:
                copy.wait()

            def give(k, carry):
                at = pl.ds(pl.multiple_of(k * step, step), step)
                term = turned_dot(mixed[...], out[at, :]).astype(BF)
                results[0][:, at] = term[:half]
                results[1][:, at] = term[half:]
                return carry

            lax.fori_loop(0, CHUNKS, give, 0)
            return

        for copy in out_copies[0]:
            copy.wait()
        total[:, :o_wide] = jnp.zeros((rows, o_wide), F32)

        def add(k, carry):
            at = pl.ds(pl.multiple_of(k * step, step), step)
            total[:, :o_wide] += dot(rows_ref[:, at], out[at, :])
            return carry

        lax.fori_loop(0, CHUNKS, add, 0)
        mixed[...] = total[:, :o_wide].astype(BF)
        for b in range(2):
            at = slice(b * half, (b + 1) * half)
            query = stack_query(heads, b, half, groups)
            push = stack_query(mixed, b, half, groups)
            key = heads[at, groups * HD : (groups + 1) * HD]
            value = heads[at, (groups + 1) * HD :]
            kept = jnp.concatenate([keep[at, :]] * groups, axis=0)
            probs = probabilities(query, key, kept)
            d_probs = turned_dot(push, value)
            centre = jnp.sum(d_probs * probs, axis=-1, keepdims=True)
            d_scores = (probs * (d_probs - centre) * (1.0 / math.sqrt(HD))).astype(BF)
            over_rows = (((0,), (0,)), ((), ()))
            d_value = lax.dot_general(probs.astype(BF), push, over_rows, preferred_element_type=F32)
            d_key = lax.dot_general(d_scores, query, over_rows, preferred_element_type=F32)
            d_query = dot(d_scores, key)
            c, s = cosine[at, :], sine[at, :]
            for g in range(groups):
                piece = d_query[g * half : (g + 1) * half]
                d_heads[at, g * HD : (g + 1) * HD] = turn_heads(piece, c, s, 1, True)[0].astype(BF)
            d_heads[at, groups * HD : (groups + 1) * HD] = turn_heads(d_key, c, s, 1, True)[0].astype(BF)
            d_heads[at, (groups + 1) * HD :] = d_value.astype(BF)
        for copy in qkv_copies[0]:
            copy.wait()
        for copy in more:
            copy.wait()

        def give_back(k, carry):
            at = pl.ds(pl.multiple_of(k * step, step), step)
            term = turned_dot(d_heads[...], qkv[at, :])
            results[2][:, at] = jnp.sum(
                term * normed_ref[:, at].astype(F32), axis=0, keepdims=True
            )
            term = term.astype(BF)
            results[0][:, at] = term[:half]
            results[1][:, at] = term[half:]
            return carry

        lax.fori_loop(0, CHUNKS, give_back, 0)

    outs = {
        "forward": (shape((half, width)),) * 2,
        "project": shape((rows, q_wide)),
        "backward": (shape((half, width)),) * 2 + (shape((1, width), F32),),
    }[kind]
    scratch = [
        pltpu.VMEM((rows, width), BF),
        pltpu.VMEM((width, q_wide), BF),
        pltpu.VMEM((rows, q_wide), F32),
        pltpu.SemaphoreType.DMA((4 + n_qkv + n_out,)),
    ]
    if n_out:
        scratch += [pltpu.VMEM((width, o_wide), BF), pltpu.VMEM((rows, o_wide), BF)]
        scratch += [pltpu.VMEM((rows, q_wide), BF)]
    args = [pick, mine, other, *tables]
    specs = [SM, HB, HB, VM, VM, VM]
    for parts in list(qkv_sets) + list(out_sets):
        args += parts
        specs += [HB] * len(parts)
    if kind == "backward":
        args += [saved, *normed[0]]
        specs += [VM, HB, HB]
        scratch += [pltpu.VMEM((rows, width), BF)]
    flops = 2 * rows * width * (q_wide + o_wide)
    return kernel_call(body, outs, specs, scratch, flops=flops, moved=14 << 20)(*args)


def all_tables(ids, z):
    count = ids.shape[-1]
    block = count // 4
    row = jnp.arange(count, dtype=jnp.int32)
    own = (z + jnp.array(RING, jnp.int32)) % 4
    index = (own[:, None] * block + jnp.arange(block, dtype=jnp.int32)).reshape(count)
    picked = (index[:, None] == row).astype(F32)
    ids = ids.astype(F32)
    relative = jnp.sum(ids[:, :, None, :] * picked, axis=-1)
    starts = jnp.sum((ids[:, :, None, :] < relative[:, :, :, None]).astype(F32), axis=-1)
    positions = index.astype(F32) - starts
    halfway = HD // 2
    frequency = jnp.exp(jnp.arange(halfway, dtype=F32) * (-2.0 * math.log(ROPE_BASE) / HD))
    angles = positions[..., None] * frequency
    cosine, sine = jnp.cos(angles), jnp.sin(angles)
    cosine = jnp.concatenate([cosine, cosine], axis=-1).reshape(4, 2 * count, HD)
    sine = jnp.concatenate([-sine, sine], axis=-1).reshape(4, 2 * count, HD)
    kept = (relative[..., :, None] == relative[..., None, :]) & (index[:, None] >= index[None, :])
    return cosine, sine, kept.astype(F32).reshape(4, 2 * count, count)


def sum_gains(part):
    order = chip_order()[1]
    part = part + shift(part, "z", 1) + shift(part, "z", -1) + shift(part, "z", 2)
    block = part.shape[1] // 16
    part = jnp.take(part.reshape(2, 16, block), order, axis=1).reshape(part.shape)
    part = part + shift(part, "y", 1) + shift(part, "y", -1) + shift(part, "y", 2)
    parts = [chip_move(part, pairs) for pairs in GROUP]
    return (parts[0] + parts[1]) + (parts[2] + parts[3])


def chip_order():
    y, x = lax.axis_index("y"), lax.axis_index("xh") * 2 + lax.axis_index("xl")
    ring, near = jnp.array(RING, jnp.int32), jnp.array(NEAR, jnp.int32)
    place = ((y + ring) % 4)[:, None] * 4 + jnp.bitwise_xor(x, near)[None, :]
    every = jnp.arange(4, dtype=jnp.int32)
    ring_back, near_back = jnp.array(RING_BACK, jnp.int32), jnp.array(RING_BACK, jnp.int32)
    back_y = jnp.sum(
        jnp.where(((every - y) % 4)[:, None] == every[None, :], ring_back[None, :], 0), axis=1
    )
    back_x = jnp.sum(
        jnp.where(jnp.bitwise_xor(every, x)[:, None] == every[None, :], near_back[None, :], 0),
        axis=1,
    )
    back = back_y[:, None] * 4 + back_x[None, :]
    return place.reshape(16).astype(jnp.int32), back.reshape(16).astype(jnp.int32)


def per_device(
    fwd_state, bwd_state, stash, gains, w_query, w_key, w_value, w_out, fwd_segments, bwd_segments
):
    a, core, z = lax.axis_index("xh"), lax.axis_index("s"), lax.axis_index("z")
    match = core == a
    one = lambda v: v.astype(jnp.int32).reshape(1)
    width = fwd_state.shape[2]
    place, back = chip_order()
    across = jnp.array([4 * y + (x ^ 1) for y in range(4) for x in range(4)], jnp.int32)

    kept0, home0, kept1, home1 = split_weights(
        one(a), w_query[0], w_key[0], w_value[0], w_out[0]
    )
    qkv_parts, out_parts = [], []
    for kept, home in ((kept0, home0), (kept1, home1)):
        guest = chip_move(kept, GUEST)
        base_qkv, base_out = join_slots(one(match), kept, chip_move(home, HOME), guest)
        qkv_parts.append(gather_beside_first(base_qkv))
        out_parts.append(gather_ring_first(base_out))

    local = jnp.concatenate([fwd_state, bwd_state, stash[0]], axis=0)
    scalars = jnp.stack([match.astype(jnp.int32), a.astype(jnp.int32)])
    first, second, keep, scale, gain = start_rows(
        scalars, place, local, chip_move(local, GUEST), gains[0], chip_move(gains[0], SIBLING)
    )
    gain_late = jnp.where(a == 0, gain[1:2], gain[0:1])
    gain_bwd = (gain[1:2], gain_late)

    own_ids = jnp.stack([fwd_segments[:, 0], bwd_segments[:, 0]])
    partner_ids = chip_move(own_ids, ACROSS)
    ids = jnp.stack(
        [jnp.where(match, own_ids, partner_ids), jnp.where(match, partner_ids, own_ids)], axis=2
    )
    ids = jnp.where(a == 0, ids, ids[:, ::-1]).reshape(4, 2, -1)
    cosine, sine, kept_pairs = all_tables(ids, z)
    tables = [(cosine[k], sine[k], kept_pairs[k]) for k in range(4)]

    late = one(jnp.where(a == 0, 1, 0))
    state, grad = keep[0], keep[1]
    first, second = gather_rows(first), gather_rows(second)
    fwd_in, fwd_at = first, 0
    cotangent, cot_at = second, 0
    stash_in = ((first, 1), (second, 1))
    sets = (qkv_parts, out_parts)
    gain_sum = []
    for tick in range(2):
        spans_fwd, spans_bwd = (([0], [1]), ([0, 1], [0, 1]))[tick]
        qkv_fwd, out_fwd = ([table[s] for s in spans_fwd] for table in sets)
        qkv_bwd, out_bwd = ([table[s] for s in spans_bwd] for table in sets)
        mine, other = layer_call(
            "forward", fwd_in, fwd_at, tables[tick], late, qkv_fwd, out_fwd
        )
        stash_rows, stash_at = stash_in[tick]
        heads = layer_call("project", stash_rows, stash_at, tables[2 + tick], late, qkv_bwd, [])
        b_mine, b_other, gain_part = layer_call(
            "backward",
            cotangent,
            cot_at,
            tables[2 + tick],
            late,
            qkv_bwd,
            out_bwd,
            saved=heads,
            normed=stash_in[tick],
        )
        gain_sum.append(gain_part / gain_bwd[tick])
        order = across if tick == 0 else back
        state = finish_forward(order, scatter_rows(mine, other), state)
        grad = finish_backward(
            order, scatter_rows(b_mine, b_other), grad, keep[2 + tick], scale[2 + tick], gain_bwd[tick]
        )
        if tick == 0:
            state, grad = chip_move(state, ACROSS), chip_move(grad, ACROSS)
            fwd_in, fwd_at = gather_rows(norm_rows(state, gain_late)), None
            cotangent, cot_at = gather_rows(grad), None

    state_out, grad_out = chip_move(state, HOME), chip_move(grad, HOME)
    on_first = jnp.where(a == 1, 1.0, 0.0)
    gain_rows = jnp.concatenate(
        [gain_sum[1] * on_first, gain_sum[0] + gain_sum[1] * (1.0 - on_first)], axis=0
    )
    gain_total = sum_gains(gain_rows)
    return (state_out[None], grad_out[None], gain_total[None])


def solution(mesh):
    grid = Mesh(mesh.devices.reshape(4, 2, 2, 2, 4), ("y", "xh", "xl", "s", "z"))
    dp = ("y", "xh", "xl")
    in_specs = (
        P("s", dp + ("z",), None),
        P("s", dp + ("z",), None),
        P("s", None, dp + ("z",), None),
        P("s", None, None),
        P("s", None, dp, "z"),
        P("s", None, dp, "z"),
        P("s", None, dp, "z"),
        P("s", None, "z", dp),
        P(None, dp, None),
        P(None, dp, None),
    )
    out_specs = (
        P("s", dp + ("z",), None),
        P("s", dp + ("z",), None),
        P("s", None, None),
    )
    return jax.shard_map(
        per_device, mesh=grid, in_specs=in_specs, out_specs=out_specs, check_vma=False
    )
```

```python
import math

import jax
import jax.numpy as jnp
from jax import lax
from jax.experimental import pallas as pl
from jax.experimental.pallas import tpu as pltpu
from jax.sharding import Mesh, PartitionSpec as P

HD = 128
ROPE_BASE = 1000000.0
BF = jnp.bfloat16
F32 = jnp.float32


CHIP = ("xh", "xl", "s")


def spot(xh, xl, core):
    return (xh * 2 + xl) * 2 + core


PLACES = [(xh, xl, core) for xh in (0, 1) for xl in (0, 1) for core in (0, 1)]
SIBLING = [(spot(a, l, c), spot(a, l, 1 - c)) for a, l, c in PLACES]
ACROSS = [(spot(a, l, c), spot(1 - a, 1 - l, c)) for a, l, c in PLACES]
BESIDE = [(spot(a, l, c), spot(a, 1 - l, c)) for a, l, c in PLACES]
HOME = [
    (spot(a, l, c), spot(a, l, 1 - c) if c == a else spot(1 - a, 1 - l, c)) for a, l, c in PLACES
]
GUEST = [(spot(a, l, c), spot(1 - a, 1 - l, 1 - c)) for a, l, c in PLACES if c != a]


def chip_move(value, pairs):
    return lax.ppermute(value, CHIP, pairs)


def shift(value, axis, steps):
    count = lax.axis_size(axis)
    return lax.ppermute(value, axis, [(i, (i + steps) % count) for i in range(count)])


RING = (0, 3, 1, 2)
RING_BACK = (0, 2, 3, 1)


NEAR = (0, 3, 1, 2)
GROUP = [
    [(spot(c, l ^ i, a ^ j), spot(a, l, c)) for a, l, c in PLACES] for i in (0, 1) for j in (0, 1)
]
VM = pl.BlockSpec(memory_space=pltpu.VMEM)
SM = pl.BlockSpec(memory_space=pltpu.SMEM)
HB = pl.BlockSpec(memory_space=pl.ANY)
CHUNKS = 8


def shape(dims, kind=BF):
    return jax.ShapeDtypeStruct(dims, kind)


def kernel_call(body, outs, in_specs, scratch=(), flops=0, moved=0):
    return pl.pallas_call(
        body,
        out_shape=outs,
        in_specs=in_specs,
        out_specs=jax.tree.map(lambda unused: VM, outs),
        scratch_shapes=list(scratch),
        cost_estimate=pl.CostEstimate(flops=flops, bytes_accessed=moved, transcendentals=0),
    )


def turned_dot(left, right):
    return lax.dot_general(left, right, (((1,), (1,)), ((), ())), preferred_element_type=F32)


def dot(left, right):
    return jnp.dot(left, right, preferred_element_type=F32)


def split_weights(a, w_query, w_key, w_value, w_out):
    block = w_query.shape[1]
    q_cols, k_cols, o_rows = w_query.shape[2] // 2, w_key.shape[2] // 2, w_out.shape[1] // 2
    wide = q_cols + 2 * k_cols + o_rows

    def body(a_ref, q_ref, k_ref, v_ref, o_ref, *outs):
        for span in range(2):
            for which in range(2):
                half = a_ref[0] if which == 0 else 1 - a_ref[0]
                out = outs[span * 2 + which]
                q_at = pl.multiple_of(half * q_cols, q_cols)
                k_at = pl.multiple_of(half * k_cols, k_cols)
                o_at = pl.multiple_of(half * o_rows, o_rows)
                out[:, :q_cols] = q_ref[span, :, pl.ds(q_at, q_cols)]
                out[:, q_cols : q_cols + k_cols] = k_ref[span, :, pl.ds(k_at, k_cols)]
                out[:, q_cols + k_cols : q_cols + 2 * k_cols] = v_ref[span, :, pl.ds(k_at, k_cols)]
                out[:, q_cols + 2 * k_cols :] = o_ref[span, pl.ds(o_at, o_rows), :].T

    outs = tuple(shape((block, wide)) for _ in range(4))
    return kernel_call(body, outs, [SM] + [VM] * 4, moved=10 << 20)(
        a, w_query, w_key, w_value, w_out
    )


def join_slots(match, kept, home, guest):
    block, wide = kept.shape
    cut = wide - wide * 2 // 5

    def body(match_ref, kept_ref, home_ref, guest_ref, qkv_ref, out_ref):
        def put(at, value_ref):
            qkv_ref[pl.ds(at, block), :] = value_ref[:, :cut]
            out_ref[pl.ds(at, block), :] = value_ref[:, cut:]

        @pl.when(match_ref[0] == 1)
        def own():
            put(0, kept_ref)
            put(block, home_ref)

        @pl.when(match_ref[0] == 0)
        def moved():
            put(0, home_ref)
            put(block, guest_ref)

    outs = (shape((2 * block, cut)), shape((2 * block, wide - cut)))
    return kernel_call(body, outs, [SM] + [VM] * 3, moved=3 << 20)(match, kept, home, guest)


def after(value, *earlier):
    return lax.optimization_barrier((value, earlier))[0]


def y_both(value):
    return shift(value, "y", 1), shift(value, "y", -1)


def beside(value):
    return chip_move(value, BESIDE)


def y_halves(before, behind):
    half = before.shape[0] // 2
    return shift(before[:half], "y", 1), shift(behind[half:], "y", -1)


def reorder(order_ref, width, block, take_from, put_to):
    for k in range(width // block):
        at = pl.multiple_of(order_ref[k] * block, block)
        put_to(k * block, take_from(at))


def start_rows(scalars, order, local, guest, gains, gains_sibling):
    kinds, rows, width = local.shape
    block = width // 16

    def body(s_ref, order_ref, local_ref, guest_ref, g_ref, h_ref, out, keep, scale, gain):
        match, a = s_ref[0] == 1, s_ref[1]

        def take_gain(at):
            return jnp.where(match, g_ref[:, pl.ds(at, block)], h_ref[:, pl.ds(at, block)])

        def put_gain(at, value):
            gain[:, at : at + block] = value.astype(F32)

        reorder(order_ref, width, block, take_gain, put_gain)
        late = jnp.where(a == 0, gain[1:2, :], gain[0:1, :])
        for kind in range(4):

            def take_rows(at):
                return jnp.where(
                    match, local_ref[kind, :, pl.ds(at, block)], guest_ref[kind, :, pl.ds(at, block)]
                )

            def put_rows(at, value):
                keep[kind, :, at : at + block] = value

            reorder(order_ref, width, block, take_rows, put_rows)
            value = keep[kind]
            if kind == 1:
                out[kind] = value
                continue
            value = value.astype(F32)
            by = lax.rsqrt(jnp.mean(value * value, axis=1, keepdims=True) + 1e-06)
            factor = (gain[0:1, :], None, gain[1:2, :], late)[kind]
            out[kind] = (value * by * factor).astype(BF)
            scale[kind] = jnp.broadcast_to(by, (rows, 128))

    outs = (
        shape((kinds, rows, width)),
        shape((kinds, rows, width)),
        shape((kinds, rows, 128), F32),
        shape((2, width), F32),
    )
    return kernel_call(body, outs, [SM, SM] + [VM] * 4, moved=6 << 20)(
        scalars, order, local, guest, gains, gains_sibling
    )


def norm_rows(state, gain_row):
    def body(state_ref, gain_ref, out_ref):
        value = state_ref[...].astype(F32)
        by = lax.rsqrt(jnp.mean(value * value, axis=1, keepdims=True) + 1e-06)
        out_ref[...] = (value * by * gain_ref[...]).astype(BF)

    return kernel_call(body, shape(state.shape), [VM, VM], moved=1 << 19)(state, gain_row)


def gather_near(value):
    return shift(value, "z", 1), shift(value, "z", -1)


def gather_far(before, behind):
    half = before.shape[-2] // 2
    top = shift(before[..., :half, :], "z", 1)
    return top, shift(behind[..., half:, :], "z", -1)


def gather_rows(value):
    near = gather_near(value)
    mine = jnp.concatenate([value, *near, *gather_far(*near)], axis=-2)
    return mine, chip_move(mine, SIBLING)


def scatter_rows(mine, other):
    came = chip_move(other, SIBLING)
    rows, width = mine.shape
    block = rows // 4

    def body(mine_ref, came_ref, own, one, two, three):
        for k, out in enumerate((own, one, two, three)):
            at = pl.ds(k * block, block)
            total = mine_ref[at, :].astype(F32) + came_ref[at, :].astype(F32)
            out[...] = total.astype(out.dtype)

    outs = (shape((block, width), F32),) + (shape((block, width)),) * 3
    own, one, two, three = kernel_call(body, outs, [VM, VM], moved=4 << 20)(mine, came)
    return own, shift(one, "z", -1), shift(two, "z", 1), shift(three, "z", 2)


def finish_forward(order, parts, state):
    rows, width = state.shape
    block = width // 16

    def body(order_ref, own, one, two, three, state_ref, out_ref):
        def total(at):
            at = pl.ds(at, block)
            value = own[:, at] + one[:, at].astype(F32) + two[:, at].astype(F32)
            value = value + three[:, at].astype(F32) + state_ref[:, at].astype(F32)
            return value.astype(BF)

        def put(at, value):
            out_ref[:, at : at + block] = value

        reorder(order_ref, width, block, total, put)

    return kernel_call(body, shape((rows, width)), [SM] + [VM] * 5, moved=2 << 20)(
        order, *parts, state
    )


def finish_backward(order, parts, grad, kept, scale, gain_row):
    rows, width = grad.shape
    block = width // 16

    def body(order_ref, own, one, two, three, grad_ref, kept_ref, scale_ref, gain_ref, out_ref, hold):
        by = scale_ref[:, :1]
        pushed = own[...] + one[...].astype(F32) + two[...].astype(F32) + three[...].astype(F32)
        pushed = pushed * gain_ref[...]
        value = kept_ref[...].astype(F32)
        lean = jnp.mean(value * pushed, axis=1, keepdims=True) * (by * by * by)
        hold[...] = (grad_ref[...].astype(F32) + pushed * by - value * lean).astype(BF)

        def put(at, piece):
            out_ref[:, at : at + block] = piece

        reorder(order_ref, width, block, lambda at: hold[:, pl.ds(at, block)], put)

    return kernel_call(
        body,
        shape((rows, width)),
        [SM] + [VM] * 8,
        scratch=[pltpu.VMEM((rows, width), BF)],
        moved=2 << 20,
    )(order, *parts, grad, kept, scale, gain_row)


def stack_copies(parts, target, sems, at):
    copies, row = [], 0
    for k, part in enumerate(parts):
        rows = part.shape[0]
        copies.append(pltpu.make_async_copy(part, target.at[pl.ds(row, rows)], sems.at[at + k]))
        row += rows
    return copies


def start_copies(pick_ref, groups):
    if len(groups) == 1:
        for copy in groups[0]:
            copy.start()
        return
    for span, copies in enumerate(groups):

        @pl.when(pick_ref[0] == span)
        def begin():
            for copy in copies:
                copy.start()


def turn_heads(projected, cosine, sine, heads, back=False):
    outs = []
    for h in range(heads):
        v = projected[:, h * HD : (h + 1) * HD]
        turned = pltpu.roll(v, HD // 2, 1) * sine
        outs.append(v * cosine - turned if back else v * cosine + turned)
    return outs


def project(rows_ref, qkv, copies, cosine, sine, heads_ref, total):
    width = rows_ref.shape[1]
    step = width // CHUNKS
    total[...] = jnp.zeros_like(total)
    for k in range(CHUNKS):
        copies[k].wait()
        at = pl.ds(k * step, step)
        total[...] += dot(rows_ref[:, at], qkv[at, :])
    count = total.shape[1] // HD
    turned = turn_heads(total, cosine[...], sine[...], count - 1)
    for h in range(count - 1):
        heads_ref[:, h * HD : (h + 1) * HD] = turned[h].astype(BF)
    heads_ref[:, (count - 1) * HD :] = total[:, (count - 1) * HD :].astype(BF)


def stack_query(ref, b, rows, groups):
    return jnp.concatenate(
        [ref[b * rows : (b + 1) * rows, g * HD : (g + 1) * HD] for g in range(groups)], axis=0
    )


def probabilities(query, key, keep):
    scores = turned_dot(query, key) * (1.0 / math.sqrt(HD))
    exponents = jnp.exp(jnp.where(keep > 0.0, scores, -1e30))
    return exponents / jnp.sum(exponents, axis=-1, keepdims=True)


def load_rows(index, mine, other, rows_ref, sems):
    half = rows_ref.shape[0] // 2
    return [
        pltpu.make_async_copy(
            src if index is None else src.at[index], rows_ref.at[pl.ds(k * half, half)], sems.at[k]
        )
        for k, src in enumerate((mine, other))
    ]


def layer_call(kind, rows_in, index, tables, pick, qkv_sets, out_sets, saved=None, normed=None):
    mine, other = rows_in
    half, width = mine.shape[-2:]
    rows = 2 * half
    spans = len(qkv_sets)
    q_wide = qkv_sets[0][0].shape[1]
    o_wide = out_sets[0][0].shape[1] if out_sets else 0
    groups = q_wide // HD - 2
    n_qkv = len(qkv_sets[0])
    n_out = len(out_sets[0]) if out_sets else 0
    step = width // CHUNKS

    def body(*refs):
        refs = list(refs)
        pick_ref, mine_ref, other_ref = refs[:3]
        cosine, sine, keep = refs[3:6]
        refs = refs[6:]
        qkv_refs = [refs[s * n_qkv : (s + 1) * n_qkv] for s in range(spans)]
        refs = refs[spans * n_qkv :]
        out_refs = [refs[s * n_out : (s + 1) * n_out] for s in range(spans)]
        refs = refs[spans * n_out :]
        if kind == "backward":
            heads, n_mine, n_other = refs[:3]
            refs = refs[3:]
        n_results = {"forward": 2, "project": 1, "backward": 3}[kind]
        results, refs = refs[:n_results], refs[n_results:]
        rows_ref, qkv, total, sems = refs[:4]
        refs = refs[4:]
        row_copies = load_rows(index, mine_ref, other_ref, rows_ref, sems)
        qkv_copies = [stack_copies(parts, qkv, sems, 4) for parts in qkv_refs]
        if n_out:
            out, mixed = refs[:2]
            out_copies = [stack_copies(parts, out, sems, 4 + n_qkv) for parts in out_refs]
        for copy in row_copies:
            copy.start()
        if kind == "backward":
            start_copies(pick_ref, out_copies)
            start_copies(pick_ref, qkv_copies)
            d_heads, normed_ref = refs[2:]
            more = load_rows(normed[1], n_mine, n_other, normed_ref, sems.at[pl.ds(2, 2)])
            for copy in more:
                copy.start()
        else:
            start_copies(pick_ref, qkv_copies)
            if n_out:
                start_copies(pick_ref, out_copies)
        for copy in row_copies:
            copy.wait()

        if kind == "project":
            project(rows_ref, qkv, qkv_copies[0], cosine, sine, results[0], total)
            return

        if kind == "forward":
            heads = refs[2]
            project(rows_ref, qkv, qkv_copies[0], cosine, sine, heads, total)
            for b in range(2):
                at = slice(b * half, (b + 1) * half)
                query = stack_query(heads, b, half, groups)
                kept = jnp.concatenate([keep[at, :]] * groups, axis=0)
                probs = probabilities(query, heads[at, groups * HD : (groups + 1) * HD], kept)
                got = dot(probs.astype(BF), heads[at, (groups + 1) * HD :]).astype(BF)
                for g in range(groups):
                    mixed[at, g * HD : (g + 1) * HD] = got[g * half : (g + 1) * half]
            for copy in out_copies[0]:
                copy.wait()

            def give(k, carry):
                at = pl.ds(pl.multiple_of(k * step, step), step)
                term = turned_dot(mixed[...], out[at, :]).astype(BF)
                results[0][:, at] = term[:half]
                results[1][:, at] = term[half:]
                return carry

            lax.fori_loop(0, CHUNKS, give, 0)
            return

        for copy in out_copies[0]:
            copy.wait()
        total[:, :o_wide] = jnp.zeros((rows, o_wide), F32)

        def add(k, carry):
            at = pl.ds(pl.multiple_of(k * step, step), step)
            total[:, :o_wide] += dot(rows_ref[:, at], out[at, :])
            return carry

        lax.fori_loop(0, CHUNKS, add, 0)
        mixed[...] = total[:, :o_wide].astype(BF)
        for b in range(2):
            at = slice(b * half, (b + 1) * half)
            query = stack_query(heads, b, half, groups)
            push = stack_query(mixed, b, half, groups)
            key = heads[at, groups * HD : (groups + 1) * HD]
            value = heads[at, (groups + 1) * HD :]
            kept = jnp.concatenate([keep[at, :]] * groups, axis=0)
            probs = probabilities(query, key, kept)
            d_probs = turned_dot(push, value)
            centre = jnp.sum(d_probs * probs, axis=-1, keepdims=True)
            d_scores = (probs * (d_probs - centre) * (1.0 / math.sqrt(HD))).astype(BF)
            over_rows = (((0,), (0,)), ((), ()))
            d_value = lax.dot_general(probs.astype(BF), push, over_rows, preferred_element_type=F32)
            d_key = lax.dot_general(d_scores, query, over_rows, preferred_element_type=F32)
            d_query = dot(d_scores, key)
            c, s = cosine[at, :], sine[at, :]
            for g in range(groups):
                piece = d_query[g * half : (g + 1) * half]
                d_heads[at, g * HD : (g + 1) * HD] = turn_heads(piece, c, s, 1, True)[0].astype(BF)
            d_heads[at, groups * HD : (groups + 1) * HD] = turn_heads(d_key, c, s, 1, True)[0].astype(BF)
            d_heads[at, (groups + 1) * HD :] = d_value.astype(BF)
        for copy in qkv_copies[0]:
            copy.wait()
        for copy in more:
            copy.wait()

        def give_back(k, carry):
            at = pl.ds(pl.multiple_of(k * step, step), step)
            term = turned_dot(d_heads[...], qkv[at, :])
            results[2][:, at] = jnp.sum(
                term * normed_ref[:, at].astype(F32), axis=0, keepdims=True
            )
            term = term.astype(BF)
            results[0][:, at] = term[:half]
            results[1][:, at] = term[half:]
            return carry

        lax.fori_loop(0, CHUNKS, give_back, 0)

    outs = {
        "forward": (shape((half, width)),) * 2,
        "project": shape((rows, q_wide)),
        "backward": (shape((half, width)),) * 2 + (shape((1, width), F32),),
    }[kind]
    scratch = [
        pltpu.VMEM((rows, width), BF),
        pltpu.VMEM((width, q_wide), BF),
        pltpu.VMEM((rows, q_wide), F32),
        pltpu.SemaphoreType.DMA((4 + n_qkv + n_out,)),
    ]
    if n_out:
        scratch += [pltpu.VMEM((width, o_wide), BF), pltpu.VMEM((rows, o_wide), BF)]
        scratch += [pltpu.VMEM((rows, q_wide), BF)]
    args = [pick, mine, other, *tables]
    specs = [SM, HB, HB, VM, VM, VM]
    for parts in list(qkv_sets) + list(out_sets):
        args += parts
        specs += [HB] * len(parts)
    if kind == "backward":
        args += [saved, *normed[0]]
        specs += [VM, HB, HB]
        scratch += [pltpu.VMEM((rows, width), BF)]
    flops = 2 * rows * width * (q_wide + o_wide)
    return kernel_call(body, outs, specs, scratch, flops=flops, moved=14 << 20)(*args)


def all_tables(ids, z):
    count = ids.shape[-1]
    block = count // 4
    row = jnp.arange(count, dtype=jnp.int32)
    own = (z + jnp.array(RING, jnp.int32)) % 4
    index = (own[:, None] * block + jnp.arange(block, dtype=jnp.int32)).reshape(count)
    picked = (index[:, None] == row).astype(F32)
    ids = ids.astype(F32)
    relative = jnp.sum(ids[:, :, None, :] * picked, axis=-1)
    starts = jnp.sum((ids[:, :, None, :] < relative[:, :, :, None]).astype(F32), axis=-1)
    positions = index.astype(F32) - starts
    halfway = HD // 2
    frequency = jnp.exp(jnp.arange(halfway, dtype=F32) * (-2.0 * math.log(ROPE_BASE) / HD))
    angles = positions[..., None] * frequency
    cosine, sine = jnp.cos(angles), jnp.sin(angles)
    cosine = jnp.concatenate([cosine, cosine], axis=-1).reshape(4, 2 * count, HD)
    sine = jnp.concatenate([-sine, sine], axis=-1).reshape(4, 2 * count, HD)
    kept = (relative[..., :, None] == relative[..., None, :]) & (index[:, None] >= index[None, :])
    return cosine, sine, kept.astype(F32).reshape(4, 2 * count, count)


def sum_gains(part):
    order = chip_order()[1]
    part = part + shift(part, "z", 1) + shift(part, "z", -1) + shift(part, "z", 2)
    block = part.shape[1] // 16
    part = jnp.take(part.reshape(2, 16, block), order, axis=1).reshape(part.shape)
    part = part + shift(part, "y", 1) + shift(part, "y", -1) + shift(part, "y", 2)
    parts = [chip_move(part, pairs) for pairs in GROUP]
    return (parts[0] + parts[1]) + (parts[2] + parts[3])


def chip_order():
    y, x = lax.axis_index("y"), lax.axis_index("xh") * 2 + lax.axis_index("xl")
    ring, near = jnp.array(RING, jnp.int32), jnp.array(NEAR, jnp.int32)
    place = ((y + ring) % 4)[:, None] * 4 + jnp.bitwise_xor(x, near)[None, :]
    every = jnp.arange(4, dtype=jnp.int32)
    ring_back, near_back = jnp.array(RING_BACK, jnp.int32), jnp.array(RING_BACK, jnp.int32)
    back_y = jnp.sum(
        jnp.where(((every - y) % 4)[:, None] == every[None, :], ring_back[None, :], 0), axis=1
    )
    back_x = jnp.sum(
        jnp.where(jnp.bitwise_xor(every, x)[:, None] == every[None, :], near_back[None, :], 0),
        axis=1,
    )
    back = back_y[:, None] * 4 + back_x[None, :]
    return place.reshape(16).astype(jnp.int32), back.reshape(16).astype(jnp.int32)


def per_device(
    fwd_state, bwd_state, stash, gains, w_query, w_key, w_value, w_out, fwd_segments, bwd_segments
):
    a, core, z = lax.axis_index("xh"), lax.axis_index("s"), lax.axis_index("z")
    match = core == a
    one = lambda v: v.astype(jnp.int32).reshape(1)
    place, back = chip_order()
    across = jnp.array([4 * y + (x ^ 1) for y in range(4) for x in range(4)], jnp.int32)

    kept0, home0, kept1, home1 = split_weights(
        one(a), w_query[0], w_key[0], w_value[0], w_out[0]
    )
    home1, guest1 = chip_move(home1, HOME), chip_move(kept1, GUEST)
    local = jnp.concatenate([fwd_state, bwd_state, stash[0]], axis=0)
    gains_sibling = chip_move(gains[0], SIBLING)
    own_ids = jnp.stack([fwd_segments[:, 0], bwd_segments[:, 0]])
    partner_ids = chip_move(own_ids, ACROSS)
    q1, o1 = join_slots(one(match), kept1, home1, guest1)

    came = (home1, guest1)
    guest_rows = chip_move(after(local, *came), GUEST)
    home0, guest0 = chip_move(after(home0, *came), HOME), chip_move(after(kept0, *came), GUEST)
    q1_x, o1_x = beside(q1), beside(o1)
    q1_b, q1_a = y_both(q1)
    o1_b, o1_a = y_both(o1)
    ids = jnp.stack(
        [jnp.where(match, own_ids, partner_ids), jnp.where(match, partner_ids, own_ids)], axis=2
    )
    ids = jnp.where(a == 0, ids, ids[:, ::-1]).reshape(4, 2, -1)
    all_cosines, all_sines, all_kept = all_tables(ids, z)

    came = (q1_x, o1_x, q1_b, q1_a, o1_b, o1_a, guest_rows, home0, guest0)
    scalars = jnp.stack([match.astype(jnp.int32), a.astype(jnp.int32)])
    rows, keep, scale, gain = start_rows(
        scalars, place, local, guest_rows, gains[0], gains_sibling
    )
    q1_xb, q1_xa = y_both(after(q1_x, *came))
    o1_t, o1_d = y_halves(after(o1_b, *came), after(o1_a, *came))
    o1_bx, o1_ax = beside(after(o1_b, *came)), beside(after(o1_a, *came))
    rows_near = gather_near(after(rows, *came))
    q0, o0 = join_slots(one(match), kept0, home0, guest0)

    came = (q1_xb, q1_xa, o1_t, o1_d, o1_bx, o1_ax, all_cosines, all_sines, all_kept) + rows_near
    q1_o, q1_ox = shift(after(q1_b, *came), "y", 1), shift(after(q1_xa, *came), "y", -1)
    o1_tx, o1_dx = beside(after(o1_t, *came)), beside(after(o1_d, *came))
    o0_b, o0_a = y_both(after(o0, *came))
    q0_x = beside(after(q0, *came))
    rows_far = gather_far(*(after(v, *came) for v in rows_near))

    came = (q1_o, q1_ox, o1_tx, o1_dx, o0_b, o0_a, q0_x) + rows_far
    q0_b, q0_a = y_both(after(q0, *came))
    q0_xb, q0_xa = y_both(after(q0_x, *came))
    o0_t, o0_d = y_halves(after(o0_b, *came), after(o0_a, *came))
    o0_x, o0_bx, o0_ax = (beside(after(v, *came)) for v in (o0, o0_b, o0_a))
    rows_mine = jnp.concatenate(
        [after(rows, *came), *rows_near, *(after(v, *came) for v in rows_far)], axis=-2
    )
    entering = rows_mine, chip_move(rows_mine, SIBLING)

    came = (q0_b, q0_a, q0_xb, q0_xa, o0_t, o0_d, o0_x, o0_bx, o0_ax)
    q0_o, q0_ox = shift(after(q0_b, *came), "y", 1), shift(after(q0_xa, *came), "y", -1)
    o0_tx, o0_dx = beside(after(o0_t, *came)), beside(after(o0_d, *came))

    qkv_parts = [
        [q0, q0_x, q0_b, q0_xb, q0_a, q0_xa, q0_o, q0_ox],
        [q1, q1_x, q1_b, q1_xb, q1_a, q1_xa, q1_o, q1_ox],
    ]
    out_parts = [
        [o0, o0_x, o0_b, o0_bx, o0_a, o0_ax, o0_t, o0_d, o0_tx, o0_dx],
        [o1, o1_x, o1_b, o1_bx, o1_a, o1_ax, o1_t, o1_d, o1_tx, o1_dx],
    ]
    gain_late = jnp.where(a == 0, gain[1:2], gain[0:1])
    gain_bwd = (gain[1:2], gain_late)

    tables = [(all_cosines[k], all_sines[k], all_kept[k]) for k in range(4)]

    late = one(jnp.where(a == 0, 1, 0))
    state, grad = keep[0], keep[1]
    fwd_in, fwd_at = entering, 0
    cotangent, cot_at = entering, 1
    stash_in = ((entering, 2), (entering, 3))
    sets = (qkv_parts, out_parts)
    gain_sum = []
    for tick in range(2):
        spans_fwd, spans_bwd = (([0], [1]), ([0, 1], [0, 1]))[tick]
        qkv_fwd, out_fwd = ([table[s] for s in spans_fwd] for table in sets)
        qkv_bwd, out_bwd = ([table[s] for s in spans_bwd] for table in sets)
        mine, other = layer_call(
            "forward", fwd_in, fwd_at, tables[tick], late, qkv_fwd, out_fwd
        )
        stash_rows, stash_at = stash_in[tick]
        heads = layer_call("project", stash_rows, stash_at, tables[2 + tick], late, qkv_bwd, [])
        b_mine, b_other, gain_part = layer_call(
            "backward",
            cotangent,
            cot_at,
            tables[2 + tick],
            late,
            qkv_bwd,
            out_bwd,
            saved=heads,
            normed=stash_in[tick],
        )
        gain_sum.append(gain_part / gain_bwd[tick])
        order = across if tick == 0 else back
        state = finish_forward(order, scatter_rows(mine, other), state)
        grad = finish_backward(
            order, scatter_rows(b_mine, b_other), grad, keep[2 + tick], scale[2 + tick], gain_bwd[tick]
        )
        if tick == 0:
            state, grad = chip_move(state, ACROSS), chip_move(grad, ACROSS)
            fwd_in, fwd_at = gather_rows(norm_rows(state, gain_late)), None
            cotangent, cot_at = gather_rows(grad), None

    state_out, grad_out = chip_move(state, HOME), chip_move(grad, HOME)
    on_first = jnp.where(a == 1, 1.0, 0.0)
    gain_rows = jnp.concatenate(
        [gain_sum[1] * on_first, gain_sum[0] + gain_sum[1] * (1.0 - on_first)], axis=0
    )
    gain_total = sum_gains(gain_rows)
    return (state_out[None], grad_out[None], gain_total[None])


def solution(mesh):
    grid = Mesh(mesh.devices.reshape(4, 2, 2, 2, 4), ("y", "xh", "xl", "s", "z"))
    dp = ("y", "xh", "xl")
    in_specs = (
        P("s", dp + ("z",), None),
        P("s", dp + ("z",), None),
        P("s", None, dp + ("z",), None),
        P("s", None, None),
        P("s", None, dp, "z"),
        P("s", None, dp, "z"),
        P("s", None, dp, "z"),
        P("s", None, "z", dp),
        P(None, dp, None),
        P(None, dp, None),
    )
    out_specs = (
        P("s", dp + ("z",), None),
        P("s", dp + ("z",), None),
        P("s", None, None),
    )

    return jax.shard_map(
        per_device, mesh=grid, in_specs=in_specs, out_specs=out_specs, check_vma=False
    )
```

```python
import math

import jax
import jax.numpy as jnp
from jax import lax
from jax.experimental import pallas as pl
from jax.experimental.pallas import tpu as pltpu
from jax.sharding import Mesh, PartitionSpec as P

HD = 128
ROPE_BASE = 1000000.0
BF = jnp.bfloat16
F32 = jnp.float32


CHIP = ("xh", "xl", "s")


def spot(xh, xl, core):
    return (xh * 2 + xl) * 2 + core


PLACES = [(xh, xl, core) for xh in (0, 1) for xl in (0, 1) for core in (0, 1)]
SIBLING = [(spot(a, l, c), spot(a, l, 1 - c)) for a, l, c in PLACES]
ACROSS = [(spot(a, l, c), spot(1 - a, 1 - l, c)) for a, l, c in PLACES]
BESIDE = [(spot(a, l, c), spot(a, 1 - l, c)) for a, l, c in PLACES]
HOME = [
    (spot(a, l, c), spot(a, l, 1 - c) if c == a else spot(1 - a, 1 - l, c)) for a, l, c in PLACES
]
GUEST = [(spot(a, l, c), spot(1 - a, 1 - l, 1 - c)) for a, l, c in PLACES if c != a]


def chip_move(value, pairs):
    return lax.ppermute(value, CHIP, pairs)


def shift(value, axis, steps):
    count = lax.axis_size(axis)
    return lax.ppermute(value, axis, [(i, (i + steps) % count) for i in range(count)])


RING = (0, 3, 1, 2)
RING_BACK = (0, 2, 3, 1)


NEAR = (0, 3, 1, 2)
VM = pl.BlockSpec(memory_space=pltpu.VMEM)
SM = pl.BlockSpec(memory_space=pltpu.SMEM)
HB = pl.BlockSpec(memory_space=pl.ANY)
CHUNKS = 8


def shape(dims, kind=BF):
    return jax.ShapeDtypeStruct(dims, kind)


def kernel_call(body, outs, in_specs, scratch=(), flops=0, moved=0):
    return pl.pallas_call(
        body,
        out_shape=outs,
        in_specs=in_specs,
        out_specs=jax.tree.map(lambda unused: VM, outs),
        scratch_shapes=list(scratch),
        cost_estimate=pl.CostEstimate(flops=flops, bytes_accessed=moved, transcendentals=0),
    )


def turned_dot(left, right):
    return lax.dot_general(left, right, (((1,), (1,)), ((), ())), preferred_element_type=F32)


def dot(left, right):
    return jnp.dot(left, right, preferred_element_type=F32)


def split_weights(a, w_query, w_key, w_value, w_out):
    block = w_query.shape[1]
    q_cols, k_cols, o_rows = w_query.shape[2] // 2, w_key.shape[2] // 2, w_out.shape[1] // 2
    wide = q_cols + 2 * k_cols + o_rows

    def body(a_ref, q_ref, k_ref, v_ref, o_ref, *outs):
        for span in range(2):
            for which in range(2):
                half = a_ref[0] if which == 0 else 1 - a_ref[0]
                out = outs[span * 2 + which]
                q_at = pl.multiple_of(half * q_cols, q_cols)
                k_at = pl.multiple_of(half * k_cols, k_cols)
                o_at = pl.multiple_of(half * o_rows, o_rows)
                out[:, :q_cols] = q_ref[span, :, pl.ds(q_at, q_cols)]
                out[:, q_cols : q_cols + k_cols] = k_ref[span, :, pl.ds(k_at, k_cols)]
                out[:, q_cols + k_cols : q_cols + 2 * k_cols] = v_ref[span, :, pl.ds(k_at, k_cols)]
                out[:, q_cols + 2 * k_cols :] = o_ref[span, pl.ds(o_at, o_rows), :].T

    outs = tuple(shape((block, wide)) for _ in range(4))
    return kernel_call(body, outs, [SM] + [VM] * 4, moved=10 << 20)(
        a, w_query, w_key, w_value, w_out
    )


def join_slots(match, kept, home, guest):
    block, wide = kept.shape
    cut = wide - wide * 2 // 5

    def body(match_ref, kept_ref, home_ref, guest_ref, qkv_ref, out_ref):
        def put(at, value_ref):
            qkv_ref[pl.ds(at, block), :] = value_ref[:, :cut]
            out_ref[pl.ds(at, block), :] = value_ref[:, cut:]

        @pl.when(match_ref[0] == 1)
        def own():
            put(0, kept_ref)
            put(block, home_ref)

        @pl.when(match_ref[0] == 0)
        def moved():
            put(0, home_ref)
            put(block, guest_ref)

    outs = (shape((2 * block, cut)), shape((2 * block, wide - cut)))
    return kernel_call(body, outs, [SM] + [VM] * 3, moved=3 << 20)(match, kept, home, guest)


def after(value, *earlier):
    return lax.optimization_barrier((value, earlier))[0]


def y_both(value):
    return shift(value, "y", 1), shift(value, "y", -1)


def beside(value):
    return chip_move(value, BESIDE)


def reorder(order_ref, width, block, take_from, put_to):
    for k in range(width // block):
        at = pl.multiple_of(order_ref[k] * block, block)
        put_to(k * block, take_from(at))


def start_rows(scalars, order, local, guest, gains, gains_sibling):
    kinds, rows, width = local.shape
    block = width // 16

    def body(s_ref, order_ref, local_ref, guest_ref, g_ref, h_ref, out, keep, scale, gain):
        match, a = s_ref[0] == 1, s_ref[1]

        def take_gain(at):
            return jnp.where(match, g_ref[:, pl.ds(at, block)], h_ref[:, pl.ds(at, block)])

        def put_gain(at, value):
            gain[:, at : at + block] = value.astype(F32)

        reorder(order_ref, width, block, take_gain, put_gain)
        late = jnp.where(a == 0, gain[1:2, :], gain[0:1, :])
        for kind in range(4):

            def take_rows(at):
                return jnp.where(
                    match, local_ref[kind, :, pl.ds(at, block)], guest_ref[kind, :, pl.ds(at, block)]
                )

            def put_rows(at, value):
                keep[kind, :, at : at + block] = value

            reorder(order_ref, width, block, take_rows, put_rows)
            value = keep[kind]
            if kind == 1:
                out[kind] = value
                continue
            value = value.astype(F32)
            by = lax.rsqrt(jnp.mean(value * value, axis=1, keepdims=True) + 1e-06)
            factor = (gain[0:1, :], None, gain[1:2, :], late)[kind]
            out[kind] = (value * by * factor).astype(BF)
            scale[kind] = jnp.broadcast_to(by, (rows, 128))

    outs = (
        shape((kinds, rows, width)),
        shape((kinds, rows, width)),
        shape((kinds, rows, 128), F32),
        shape((2, width), F32),
    )
    return kernel_call(body, outs, [SM, SM] + [VM] * 4, moved=6 << 20)(
        scalars, order, local, guest, gains, gains_sibling
    )


def norm_rows(state, gain_row):
    def body(state_ref, gain_ref, out_ref):
        value = state_ref[...].astype(F32)
        by = lax.rsqrt(jnp.mean(value * value, axis=1, keepdims=True) + 1e-06)
        out_ref[...] = (value * by * gain_ref[...]).astype(BF)

    return kernel_call(body, shape(state.shape), [VM, VM], moved=1 << 19)(state, gain_row)


def gather_near(value):
    return shift(value, "z", 1), shift(value, "z", -1)


def gather_rows(value):
    near = gather_near(value)
    parts = (value, *near, shift(near[0], "z", 1))
    return parts + tuple(chip_move(part, SIBLING) for part in parts)


def scatter_rows(mine, other):
    came = chip_move(other, SIBLING)
    rows, width = mine.shape
    block = rows // 4

    def body(mine_ref, came_ref, own, one, two, three):
        for k, out in enumerate((own, one, two, three)):
            at = pl.ds(k * block, block)
            total = mine_ref[at, :].astype(F32) + came_ref[at, :].astype(F32)
            out[...] = total.astype(out.dtype)

    outs = (shape((block, width), F32),) + (shape((block, width)),) * 3
    own, one, two, three = kernel_call(body, outs, [VM, VM], moved=4 << 20)(mine, came)
    return own, shift(one, "z", -1), shift(two, "z", 1), shift(three, "z", 2)


def finish_forward(order, parts, state):
    rows, width = state.shape
    block = width // 16

    def body(order_ref, own, one, two, three, state_ref, out_ref):
        def total(at):
            at = pl.ds(at, block)
            value = own[:, at] + one[:, at].astype(F32) + two[:, at].astype(F32)
            value = value + three[:, at].astype(F32) + state_ref[:, at].astype(F32)
            return value.astype(BF)

        def put(at, value):
            out_ref[:, at : at + block] = value

        reorder(order_ref, width, block, total, put)

    return kernel_call(body, shape((rows, width)), [SM] + [VM] * 5, moved=2 << 20)(
        order, *parts, state
    )


def finish_backward(order, parts, grad, kept, scale, gain_row):
    rows, width = grad.shape
    block = width // 16

    def body(order_ref, own, one, two, three, grad_ref, kept_ref, scale_ref, gain_ref, out_ref, hold):
        by = scale_ref[:, :1]
        pushed = own[...] + one[...].astype(F32) + two[...].astype(F32) + three[...].astype(F32)
        pushed = pushed * gain_ref[...]
        value = kept_ref[...].astype(F32)
        lean = jnp.mean(value * pushed, axis=1, keepdims=True) * (by * by * by)
        hold[...] = (grad_ref[...].astype(F32) + pushed * by - value * lean).astype(BF)

        def put(at, piece):
            out_ref[:, at : at + block] = piece

        reorder(order_ref, width, block, lambda at: hold[:, pl.ds(at, block)], put)

    return kernel_call(
        body,
        shape((rows, width)),
        [SM] + [VM] * 8,
        scratch=[pltpu.VMEM((rows, width), BF)],
        moved=2 << 20,
    )(order, *parts, grad, kept, scale, gain_row)


def stack_copies(parts, target, sems, at):
    copies, row = [], 0
    for k, part in enumerate(parts):
        rows = part.shape[0]
        copies.append(pltpu.make_async_copy(part, target.at[pl.ds(row, rows)], sems.at[at + k]))
        row += rows
    return copies


def start_copies(pick_ref, groups):
    if len(groups) == 1:
        for copy in groups[0]:
            copy.start()
        return
    for span, copies in enumerate(groups):

        @pl.when(pick_ref[0] == span)
        def begin():
            for copy in copies:
                copy.start()


def turn_heads(projected, cosine, sine, heads, back=False):
    outs = []
    for h in range(heads):
        v = projected[:, h * HD : (h + 1) * HD]
        turned = pltpu.roll(v, HD // 2, 1) * sine
        outs.append(v * cosine - turned if back else v * cosine + turned)
    return outs


def project(rows_ref, qkv, copies, cosine, sine, heads_ref, total):
    width = rows_ref.shape[1]
    step = width // CHUNKS
    total[...] = jnp.zeros_like(total)
    for k in range(CHUNKS):
        copies[k].wait()
        at = pl.ds(k * step, step)
        total[...] += dot(rows_ref[:, at], qkv[at, :])
    count = total.shape[1] // HD
    turned = turn_heads(total, cosine[...], sine[...], count - 1)
    for h in range(count - 1):
        heads_ref[:, h * HD : (h + 1) * HD] = turned[h].astype(BF)
    heads_ref[:, (count - 1) * HD :] = total[:, (count - 1) * HD :].astype(BF)


def stack_query(ref, b, rows, groups):
    return jnp.concatenate(
        [ref[b * rows : (b + 1) * rows, g * HD : (g + 1) * HD] for g in range(groups)], axis=0
    )


def probabilities(query, key, keep):
    scores = turned_dot(query, key) * (1.0 / math.sqrt(HD))
    exponents = jnp.exp(jnp.where(keep > 0.0, scores, -1e30))
    return exponents / jnp.sum(exponents, axis=-1, keepdims=True)


def load_rows(index, parts, rows_ref, sems, first):
    rows = rows_ref.shape[0] // len(parts)
    return [
        pltpu.make_async_copy(
            src if index is None else src.at[index],
            rows_ref.at[pl.ds(k * rows, rows)],
            sems.at[first + k],
        )
        for k, src in enumerate(parts)
    ]


def layer_call(kind, rows_in, index, tables, pick, qkv_sets, out_sets, saved=None, normed=None):
    n_rows = len(rows_in)
    width = rows_in[0].shape[-1]
    rows = n_rows * rows_in[0].shape[-2]
    half = rows // 2
    which, tables = tables[0], tables[1:]
    spans = len(qkv_sets)
    q_wide = qkv_sets[0][0].shape[1]
    o_wide = out_sets[0][0].shape[1] if out_sets else 0
    groups = q_wide // HD - 2
    n_qkv = len(qkv_sets[0])
    n_out = len(out_sets[0]) if out_sets else 0
    step = width // CHUNKS

    def body(*refs):
        refs = list(refs)
        pick_ref, row_refs = refs[0], refs[1 : 1 + n_rows]
        table_refs, refs = refs[1 + n_rows : 4 + n_rows], refs[4 + n_rows :]
        qkv_refs = [refs[s * n_qkv : (s + 1) * n_qkv] for s in range(spans)]
        refs = refs[spans * n_qkv :]
        out_refs = [refs[s * n_out : (s + 1) * n_out] for s in range(spans)]
        refs = refs[spans * n_out :]
        if kind == "backward":
            heads, normed_refs = refs[0], refs[1 : 1 + n_rows]
            refs = refs[1 + n_rows :]
        n_results = {"forward": 2, "project": 1, "backward": 3}[kind]
        results, refs = refs[:n_results], refs[n_results:]
        rows_ref, qkv, total, sems, cosine, sine, keep = refs[:7]
        refs = refs[7:]
        row_copies = load_rows(index, row_refs, rows_ref, sems, 0)
        table_copies = [
            pltpu.make_async_copy(src.at[which], dst, sems.at[n_rows + k])
            for k, (src, dst) in enumerate(zip(table_refs, (cosine, sine, keep)))
        ]
        sem_more, sem_qkv = n_rows + 3, 2 * n_rows + 3
        qkv_copies = [stack_copies(parts, qkv, sems, sem_qkv) for parts in qkv_refs]
        if n_out:
            out, mixed = refs[:2]
            out_copies = [stack_copies(parts, out, sems, sem_qkv + n_qkv) for parts in out_refs]
        for copy in row_copies:
            copy.start()
        if kind == "backward":
            start_copies(pick_ref, out_copies)
            start_copies(pick_ref, qkv_copies)
            d_heads, normed_ref = refs[2:]
            more = load_rows(normed[1], normed_refs, normed_ref, sems, sem_more)
            for copy in more:
                copy.start()
        else:
            start_copies(pick_ref, qkv_copies)
            if n_out:
                start_copies(pick_ref, out_copies)
        for copy in table_copies:
            copy.start()
        for copy in row_copies + table_copies:
            copy.wait()

        if kind == "project":
            project(rows_ref, qkv, qkv_copies[0], cosine, sine, results[0], total)
            return

        if kind == "forward":
            heads = refs[2]
            project(rows_ref, qkv, qkv_copies[0], cosine, sine, heads, total)
            for b in range(2):
                at = slice(b * half, (b + 1) * half)
                query = stack_query(heads, b, half, groups)
                kept = jnp.concatenate([keep[at, :]] * groups, axis=0)
                probs = probabilities(query, heads[at, groups * HD : (groups + 1) * HD], kept)
                got = dot(probs.astype(BF), heads[at, (groups + 1) * HD :]).astype(BF)
                for g in range(groups):
                    mixed[at, g * HD : (g + 1) * HD] = got[g * half : (g + 1) * half]
            for copy in out_copies[0]:
                copy.wait()

            def give(k, carry):
                at = pl.ds(pl.multiple_of(k * step, step), step)
                term = turned_dot(mixed[...], out[at, :]).astype(BF)
                results[0][:, at] = term[:half]
                results[1][:, at] = term[half:]
                return carry

            lax.fori_loop(0, CHUNKS, give, 0)
            return

        for copy in out_copies[0]:
            copy.wait()
        total[:, :o_wide] = jnp.zeros((rows, o_wide), F32)

        def add(k, carry):
            at = pl.ds(pl.multiple_of(k * step, step), step)
            total[:, :o_wide] += dot(rows_ref[:, at], out[at, :])
            return carry

        lax.fori_loop(0, CHUNKS, add, 0)
        mixed[...] = total[:, :o_wide].astype(BF)
        for b in range(2):
            at = slice(b * half, (b + 1) * half)
            query = stack_query(heads, b, half, groups)
            push = stack_query(mixed, b, half, groups)
            key = heads[at, groups * HD : (groups + 1) * HD]
            value = heads[at, (groups + 1) * HD :]
            kept = jnp.concatenate([keep[at, :]] * groups, axis=0)
            probs = probabilities(query, key, kept)
            d_probs = turned_dot(push, value)
            centre = jnp.sum(d_probs * probs, axis=-1, keepdims=True)
            d_scores = (probs * (d_probs - centre) * (1.0 / math.sqrt(HD))).astype(BF)
            over_rows = (((0,), (0,)), ((), ()))
            d_value = lax.dot_general(probs.astype(BF), push, over_rows, preferred_element_type=F32)
            d_key = lax.dot_general(d_scores, query, over_rows, preferred_element_type=F32)
            d_query = dot(d_scores, key)
            c, s = cosine[at, :], sine[at, :]
            for g in range(groups):
                piece = d_query[g * half : (g + 1) * half]
                d_heads[at, g * HD : (g + 1) * HD] = turn_heads(piece, c, s, 1, True)[0].astype(BF)
            d_heads[at, groups * HD : (groups + 1) * HD] = turn_heads(d_key, c, s, 1, True)[0].astype(BF)
            d_heads[at, (groups + 1) * HD :] = d_value.astype(BF)
        for copy in qkv_copies[0]:
            copy.wait()
        for copy in more:
            copy.wait()

        def give_back(k, carry):
            at = pl.ds(pl.multiple_of(k * step, step), step)
            term = turned_dot(d_heads[...], qkv[at, :])
            results[2][:, at] = jnp.sum(
                term * normed_ref[:, at].astype(F32), axis=0, keepdims=True
            )
            term = term.astype(BF)
            results[0][:, at] = term[:half]
            results[1][:, at] = term[half:]
            return carry

        lax.fori_loop(0, CHUNKS, give_back, 0)

    outs = {
        "forward": (shape((half, width)),) * 2,
        "project": shape((rows, q_wide)),
        "backward": (shape((half, width)),) * 2 + (shape((1, width), F32),),
    }[kind]
    scratch = [
        pltpu.VMEM((rows, width), BF),
        pltpu.VMEM((width, q_wide), BF),
        pltpu.VMEM((rows, q_wide), F32),
        pltpu.SemaphoreType.DMA((2 * n_rows + 3 + n_qkv + n_out,)),
    ] + [pltpu.VMEM((rows, table.shape[-1]), F32) for table in tables]
    if n_out:
        scratch += [pltpu.VMEM((width, o_wide), BF), pltpu.VMEM((rows, o_wide), BF)]
        scratch += [pltpu.VMEM((rows, q_wide), BF)]
    args = [pick, *rows_in, *tables]
    specs = [SM] + [HB] * (n_rows + 3)
    for parts in list(qkv_sets) + list(out_sets):
        args += parts
        specs += [HB] * len(parts)
    if kind == "backward":
        args += [saved, *normed[0]]
        specs += [VM] + [HB] * n_rows
        scratch += [pltpu.VMEM((rows, width), BF)]
    flops = 2 * rows * width * (q_wide + o_wide)
    return kernel_call(body, outs, specs, scratch, flops=flops, moved=14 << 20)(*args)


def all_tables(ids, z):
    count = ids.shape[-1]
    block = count // 4
    row = jnp.arange(count, dtype=jnp.int32)
    own = (z + jnp.array(RING, jnp.int32)) % 4
    index = (own[:, None] * block + jnp.arange(block, dtype=jnp.int32)).reshape(count)
    picked = (index[:, None] == row).astype(F32)
    ids = ids.astype(F32)
    relative = jnp.sum(ids[:, :, None, :] * picked, axis=-1)
    starts = jnp.sum((ids[:, :, None, :] < relative[:, :, :, None]).astype(F32), axis=-1)
    positions = index.astype(F32) - starts
    halfway = HD // 2
    frequency = jnp.exp(jnp.arange(halfway, dtype=F32) * (-2.0 * math.log(ROPE_BASE) / HD))
    angles = positions[..., None] * frequency
    cosine, sine = jnp.cos(angles), jnp.sin(angles)
    cosine = jnp.concatenate([cosine, cosine], axis=-1).reshape(4, 2 * count, HD)
    sine = jnp.concatenate([-sine, sine], axis=-1).reshape(4, 2 * count, HD)
    kept = (relative[..., :, None] == relative[..., None, :]) & (index[:, None] >= index[None, :])
    return cosine, sine, kept.astype(F32).reshape(4, 2 * count, count)


def sum_gains(part):
    order = chip_order()[1]
    part = part + shift(part, "z", 2)
    part = part + shift(part, "z", 1)
    part = part + chip_move(part, SIBLING)
    block = part.shape[1] // 16
    part = jnp.take(part.reshape(2, 16, block), order, axis=1).reshape(part.shape)
    part = part + shift(part, "y", 2)
    part = part + shift(part, "y", 1)
    part = part + chip_move(part, BESIDE)
    other = chip_move(part, ACROSS)
    return jnp.where(lax.axis_index("s") == lax.axis_index("xh"), part, other)


def chip_order():
    y, x = lax.axis_index("y"), lax.axis_index("xh") * 2 + lax.axis_index("xl")
    ring, near = jnp.array(RING, jnp.int32), jnp.array(NEAR, jnp.int32)
    place = ((y + ring) % 4)[:, None] * 4 + jnp.bitwise_xor(x, near)[None, :]
    every = jnp.arange(4, dtype=jnp.int32)
    ring_back, near_back = jnp.array(RING_BACK, jnp.int32), jnp.array(RING_BACK, jnp.int32)
    back_y = jnp.sum(
        jnp.where(((every - y) % 4)[:, None] == every[None, :], ring_back[None, :], 0), axis=1
    )
    back_x = jnp.sum(
        jnp.where(jnp.bitwise_xor(every, x)[:, None] == every[None, :], near_back[None, :], 0),
        axis=1,
    )
    back = back_y[:, None] * 4 + back_x[None, :]
    return place.reshape(16).astype(jnp.int32), back.reshape(16).astype(jnp.int32)


def per_device(
    fwd_state, bwd_state, stash, gains, w_query, w_key, w_value, w_out, fwd_segments, bwd_segments
):
    a, core, z = lax.axis_index("xh"), lax.axis_index("s"), lax.axis_index("z")
    match = core == a
    one = lambda v: v.astype(jnp.int32).reshape(1)
    place, back = chip_order()
    across = jnp.array([4 * y + (x ^ 1) for y in range(4) for x in range(4)], jnp.int32)

    kept0, home0, kept1, home1 = split_weights(
        one(a), w_query[0], w_key[0], w_value[0], w_out[0]
    )
    home1, guest1 = chip_move(home1, HOME), chip_move(kept1, GUEST)
    local = jnp.concatenate([fwd_state, bwd_state, stash[0]], axis=0)
    gains_sibling = chip_move(gains[0], SIBLING)
    own_ids = jnp.stack([fwd_segments[:, 0], bwd_segments[:, 0]])
    partner_ids = chip_move(own_ids, ACROSS)
    q1, o1 = join_slots(one(match), kept1, home1, guest1)

    came = (home1, guest1)
    guest_rows = chip_move(after(local, *came), GUEST)
    home0, guest0 = chip_move(after(home0, *came), HOME), chip_move(after(kept0, *came), GUEST)
    q1_x, o1_x = beside(q1), beside(o1)
    q1_b, q1_a = y_both(q1)
    o1_b, o1_a = y_both(o1)
    ids = jnp.stack(
        [jnp.where(match, own_ids, partner_ids), jnp.where(match, partner_ids, own_ids)], axis=2
    )
    ids = jnp.where(a == 0, ids, ids[:, ::-1]).reshape(4, 2, -1)
    all_cosines, all_sines, all_kept = lax.optimization_barrier(all_tables(ids, z))

    came = (q1_x, o1_x, q1_b, q1_a, o1_b, o1_a, guest_rows, home0, guest0)
    scalars = jnp.stack([match.astype(jnp.int32), a.astype(jnp.int32)])
    rows, keep, scale, gain = start_rows(
        scalars, place, local, guest_rows, gains[0], gains_sibling
    )
    q1_xb, q1_xa = y_both(after(q1_x, *came))
    o1_o = shift(after(o1_b, *came), "y", 1)
    o1_bx, o1_ax = beside(after(o1_b, *came)), beside(after(o1_a, *came))
    rows_b, rows_a = gather_near(after(rows, *came))
    q0, o0 = join_slots(one(match), kept0, home0, guest0)
    rows_s = chip_move(after(rows, *came), SIBLING)

    came = (q1_xb, q1_xa, o1_o, o1_bx, o1_ax, rows_b, rows_a, rows_s)
    came = came + (all_cosines, all_sines, all_kept)
    q1_o, q1_ox = shift(after(q1_b, *came), "y", 1), shift(after(q1_xa, *came), "y", -1)
    o1_ox = beside(after(o1_o, *came))
    o0_b, o0_a = y_both(after(o0, *came))
    q0_x = beside(after(q0, *came))
    rows_o = shift(after(rows_b, *came), "z", 1)
    rows_bs, rows_as = (chip_move(after(v, *came), SIBLING) for v in (rows_b, rows_a))

    came = (q1_o, q1_ox, o1_ox, o0_b, o0_a, q0_x, rows_o, rows_bs, rows_as)
    rows_os = chip_move(after(rows_o, *came), SIBLING)
    q0_b, q0_a = y_both(after(q0, *came))
    q0_xb, q0_xa = y_both(after(q0_x, *came))
    o0_o = shift(after(o0_a, *came), "y", -1)
    o0_x, o0_bx, o0_ax = (beside(after(v, *came)) for v in (o0, o0_b, o0_a))
    entering = (rows, rows_b, rows_a, rows_o, rows_s, rows_bs, rows_as, rows_os)

    came = (q0_b, q0_a, q0_xb, q0_xa, o0_o, o0_x, o0_bx, o0_ax)
    q0_o, q0_ox = shift(after(q0_b, *came), "y", 1), shift(after(q0_xa, *came), "y", -1)
    o0_ox = beside(after(o0_o, *came))

    qkv_parts = [
        [q0, q0_x, q0_b, q0_xb, q0_a, q0_xa, q0_o, q0_ox],
        [q1, q1_x, q1_b, q1_xb, q1_a, q1_xa, q1_o, q1_ox],
    ]
    out_parts = [
        [o0, o0_x, o0_b, o0_bx, o0_a, o0_ax, o0_o, o0_ox],
        [o1, o1_x, o1_b, o1_bx, o1_a, o1_ax, o1_o, o1_ox],
    ]
    gain_late = jnp.where(a == 0, gain[1:2], gain[0:1])
    gain_bwd = (gain[1:2], gain_late)

    tables = [(k, all_cosines, all_sines, all_kept) for k in range(4)]

    late = one(jnp.where(a == 0, 1, 0))
    state, grad = keep[0], keep[1]
    fwd_in, fwd_at = entering, 0
    cotangent, cot_at = entering, 1
    stash_in = ((entering, 2), (entering, 3))
    sets = (qkv_parts, out_parts)
    gain_sum = []
    for tick in range(2):
        spans_fwd, spans_bwd = (([0], [1]), ([0, 1], [0, 1]))[tick]
        qkv_fwd, out_fwd = ([table[s] for s in spans_fwd] for table in sets)
        qkv_bwd, out_bwd = ([table[s] for s in spans_bwd] for table in sets)
        mine, other = layer_call("forward", fwd_in, fwd_at, tables[tick], late, qkv_fwd, out_fwd)
        stash_rows, stash_at = stash_in[tick]
        heads = layer_call("project", stash_rows, stash_at, tables[2 + tick], late, qkv_bwd, [])
        b_mine, b_other, gain_part = layer_call(
            "backward",
            cotangent,
            cot_at,
            tables[2 + tick],
            late,
            qkv_bwd,
            out_bwd,
            saved=heads,
            normed=stash_in[tick],
        )
        gain_sum.append(gain_part / gain_bwd[tick])
        order = across if tick == 0 else back
        pushed = scatter_rows(b_mine, b_other)
        grad = finish_backward(
            order, pushed, grad, keep[2 + tick], scale[2 + tick], gain_bwd[tick]
        )
        state = finish_forward(order, scatter_rows(mine, other), state)
        if tick == 0:
            state, grad = chip_move(state, ACROSS), chip_move(grad, ACROSS)
            fwd_in, fwd_at = gather_rows(norm_rows(state, gain_late)), None
            cotangent, cot_at = gather_rows(grad), None

    state_out, grad_out = chip_move(state, HOME), chip_move(grad, HOME)
    on_first = jnp.where(a == 1, 1.0, 0.0)
    gain_rows = jnp.concatenate(
        [gain_sum[1] * on_first, gain_sum[0] + gain_sum[1] * (1.0 - on_first)], axis=0
    )
    gain_total = sum_gains(gain_rows)
    return (state_out[None], grad_out[None], gain_total[None])


def solution(mesh):
    grid = Mesh(mesh.devices.reshape(4, 2, 2, 2, 4), ("y", "xh", "xl", "s", "z"))
    dp = ("y", "xh", "xl")
    in_specs = (
        P("s", dp + ("z",), None),
        P("s", dp + ("z",), None),
        P("s", None, dp + ("z",), None),
        P("s", None, None),
        P("s", None, dp, "z"),
        P("s", None, dp, "z"),
        P("s", None, dp, "z"),
        P("s", None, "z", dp),
        P(None, dp, None),
        P(None, dp, None),
    )
    out_specs = (
        P("s", dp + ("z",), None),
        P("s", dp + ("z",), None),
        P("s", None, None),
    )

    return jax.shard_map(
        per_device, mesh=grid, in_specs=in_specs, out_specs=out_specs, check_vma=False
    )
```

```python
import math

import jax
import jax.numpy as jnp
from jax import lax
from jax.experimental import pallas as pl
from jax.experimental.pallas import tpu as pltpu
from jax.sharding import Mesh, PartitionSpec as P

HD = 128
ROPE_BASE = 1000000.0
BF = jnp.bfloat16
F32 = jnp.float32


CHIP = ("xh", "xl", "s")


def spot(xh, xl, core):
    return (xh * 2 + xl) * 2 + core


PLACES = [(xh, xl, core) for xh in (0, 1) for xl in (0, 1) for core in (0, 1)]
SIBLING = [(spot(a, l, c), spot(a, l, 1 - c)) for a, l, c in PLACES]
ACROSS = [(spot(a, l, c), spot(1 - a, 1 - l, c)) for a, l, c in PLACES]
BESIDE = [(spot(a, l, c), spot(a, 1 - l, c)) for a, l, c in PLACES]
HOME = [
    (spot(a, l, c), spot(a, l, 1 - c) if c == a else spot(1 - a, 1 - l, c)) for a, l, c in PLACES
]
GUEST = [(spot(a, l, c), spot(1 - a, 1 - l, 1 - c)) for a, l, c in PLACES if c != a]


def chip_move(value, pairs):
    return lax.ppermute(value, CHIP, pairs)


def shift(value, axis, steps):
    count = lax.axis_size(axis)
    return lax.ppermute(value, axis, [(i, (i + steps) % count) for i in range(count)])


RING = (0, 3, 1, 2)
RING_BACK = (0, 2, 3, 1)


NEAR = (0, 3, 1, 2)
VM = pl.BlockSpec(memory_space=pltpu.VMEM)
SM = pl.BlockSpec(memory_space=pltpu.SMEM)
HB = pl.BlockSpec(memory_space=pl.ANY)
CHUNKS = 8


def shape(dims, kind=BF):
    return jax.ShapeDtypeStruct(dims, kind)


def kernel_call(body, outs, in_specs, scratch=(), flops=0, moved=0):
    return pl.pallas_call(
        body,
        out_shape=outs,
        in_specs=in_specs,
        out_specs=jax.tree.map(lambda unused: VM, outs),
        scratch_shapes=list(scratch),
        cost_estimate=pl.CostEstimate(flops=flops, bytes_accessed=moved, transcendentals=0),
    )


def turned_dot(left, right):
    return lax.dot_general(left, right, (((1,), (1,)), ((), ())), preferred_element_type=F32)


def dot(left, right):
    return jnp.dot(left, right, preferred_element_type=F32)


def split_weights(a, w_query, w_key, w_value, w_out):
    block = w_query.shape[1]
    q_cols, k_cols, o_rows = w_query.shape[2] // 2, w_key.shape[2] // 2, w_out.shape[1] // 2
    wide = q_cols + 2 * k_cols + o_rows

    def body(a_ref, q_ref, k_ref, v_ref, o_ref, *outs):
        for span in range(2):
            for which in range(2):
                half = a_ref[0] if which == 0 else 1 - a_ref[0]
                out = outs[span * 2 + which]
                q_at = pl.multiple_of(half * q_cols, q_cols)
                k_at = pl.multiple_of(half * k_cols, k_cols)
                o_at = pl.multiple_of(half * o_rows, o_rows)
                out[:, :q_cols] = q_ref[span, :, pl.ds(q_at, q_cols)]
                out[:, q_cols : q_cols + k_cols] = k_ref[span, :, pl.ds(k_at, k_cols)]
                out[:, q_cols + k_cols : q_cols + 2 * k_cols] = v_ref[span, :, pl.ds(k_at, k_cols)]
                out[:, q_cols + 2 * k_cols :] = o_ref[span, pl.ds(o_at, o_rows), :].T

    outs = tuple(shape((block, wide)) for _ in range(4))
    return kernel_call(body, outs, [SM] + [VM] * 4, moved=10 << 20)(
        a, w_query, w_key, w_value, w_out
    )


def join_slots(match, kept, home, guest):
    block, wide = kept.shape
    cut = wide - wide * 2 // 5

    def body(match_ref, kept_ref, home_ref, guest_ref, qkv_ref, out_ref):
        def put(at, value_ref):
            qkv_ref[pl.ds(at, block), :] = value_ref[:, :cut]
            out_ref[pl.ds(at, block), :] = value_ref[:, cut:]

        @pl.when(match_ref[0] == 1)
        def own():
            put(0, kept_ref)
            put(block, home_ref)

        @pl.when(match_ref[0] == 0)
        def moved():
            put(0, home_ref)
            put(block, guest_ref)

    outs = (shape((2 * block, cut)), shape((2 * block, wide - cut)))
    return kernel_call(body, outs, [SM] + [VM] * 3, moved=3 << 20)(match, kept, home, guest)


def y_both(value):
    return shift(value, "y", 1), shift(value, "y", -1)


def beside(value):
    return chip_move(value, BESIDE)


def reorder(order_ref, width, block, take_from, put_to):
    for k in range(width // block):
        at = pl.multiple_of(order_ref[k] * block, block)
        put_to(k * block, take_from(at))


def start_rows(scalars, order, local, guest, gains, gains_sibling):
    kinds, rows, width = local.shape
    block = width // 16

    def body(s_ref, order_ref, local_ref, guest_ref, g_ref, h_ref, out, keep, scale, gain):
        match, a = s_ref[0] == 1, s_ref[1]

        def take_gain(at):
            return jnp.where(match, g_ref[:, pl.ds(at, block)], h_ref[:, pl.ds(at, block)])

        def put_gain(at, value):
            gain[:, at : at + block] = value.astype(F32)

        reorder(order_ref, width, block, take_gain, put_gain)
        late = jnp.where(a == 0, gain[1:2, :], gain[0:1, :])
        for kind in range(4):

            def take_rows(at):
                return jnp.where(
                    match, local_ref[kind, :, pl.ds(at, block)], guest_ref[kind, :, pl.ds(at, block)]
                )

            def put_rows(at, value):
                keep[kind, :, at : at + block] = value

            reorder(order_ref, width, block, take_rows, put_rows)
            value = keep[kind]
            if kind == 1:
                out[kind] = value
                continue
            value = value.astype(F32)
            by = lax.rsqrt(jnp.mean(value * value, axis=1, keepdims=True) + 1e-06)
            factor = (gain[0:1, :], None, gain[1:2, :], late)[kind]
            out[kind] = (value * by * factor).astype(BF)
            scale[kind] = jnp.broadcast_to(by, (rows, 128))

    outs = (
        shape((kinds, rows, width)),
        shape((kinds, rows, width)),
        shape((kinds, rows, 128), F32),
        shape((2, width), F32),
    )
    return kernel_call(body, outs, [SM, SM] + [VM] * 4, moved=6 << 20)(
        scalars, order, local, guest, gains, gains_sibling
    )


def norm_rows(state, gain_row):
    def body(state_ref, gain_ref, out_ref):
        value = state_ref[...].astype(F32)
        by = lax.rsqrt(jnp.mean(value * value, axis=1, keepdims=True) + 1e-06)
        out_ref[...] = (value * by * gain_ref[...]).astype(BF)

    return kernel_call(body, shape(state.shape), [VM, VM], moved=1 << 19)(state, gain_row)


def gather_near(value):
    return shift(value, "z", 1), shift(value, "z", -1)


def gather_rows(value):
    near = gather_near(value)
    far = shift(near[1], "z", -1)
    parts = (value, *near, far)
    return parts + tuple(chip_move(part, SIBLING) for part in parts)


def scatter_rows(mine, other):
    came = chip_move(other, SIBLING)
    rows, width = mine.shape
    block = rows // 4

    def body(mine_ref, came_ref, own, one, two, three):
        for k, out in enumerate((own, one, two, three)):
            at = pl.ds(k * block, block)
            total = mine_ref[at, :].astype(F32) + came_ref[at, :].astype(F32)
            out[...] = total.astype(out.dtype)

    outs = (shape((block, width), F32),) + (shape((block, width)),) * 3
    own, one, two, three = kernel_call(body, outs, [VM, VM], moved=4 << 20)(mine, came)
    return own, shift(one, "z", -1), shift(two, "z", 1), shift(three, "z", 2)


def finish_forward(order, parts, state):
    rows, width = state.shape
    block = width // 16

    def body(order_ref, own, one, two, three, state_ref, out_ref):
        def total(at):
            at = pl.ds(at, block)
            value = own[:, at] + one[:, at].astype(F32) + two[:, at].astype(F32)
            value = value + three[:, at].astype(F32) + state_ref[:, at].astype(F32)
            return value.astype(BF)

        def put(at, value):
            out_ref[:, at : at + block] = value

        reorder(order_ref, width, block, total, put)

    return kernel_call(body, shape((rows, width)), [SM] + [VM] * 5, moved=2 << 20)(
        order, *parts, state
    )


def finish_backward(order, parts, grad, kept, scale, gain_row):
    rows, width = grad.shape
    block = width // 16

    def body(order_ref, own, one, two, three, grad_ref, kept_ref, scale_ref, gain_ref, out_ref, hold):
        by = scale_ref[:, :1]
        pushed = own[...] + one[...].astype(F32) + two[...].astype(F32) + three[...].astype(F32)
        pushed = pushed * gain_ref[...]
        value = kept_ref[...].astype(F32)
        lean = jnp.mean(value * pushed, axis=1, keepdims=True) * (by * by * by)
        hold[...] = (grad_ref[...].astype(F32) + pushed * by - value * lean).astype(BF)

        def put(at, piece):
            out_ref[:, at : at + block] = piece

        reorder(order_ref, width, block, lambda at: hold[:, pl.ds(at, block)], put)

    return kernel_call(
        body,
        shape((rows, width)),
        [SM] + [VM] * 8,
        scratch=[pltpu.VMEM((rows, width), BF)],
        moved=2 << 20,
    )(order, *parts, grad, kept, scale, gain_row)


def stack_copies(parts, target, sems, at):
    copies, row = [], 0
    for k, part in enumerate(parts):
        rows = part.shape[0]
        copies.append(pltpu.make_async_copy(part, target.at[pl.ds(row, rows)], sems.at[at + k]))
        row += rows
    return copies


def start_copies(pick_ref, groups):
    if len(groups) == 1:
        for copy in groups[0]:
            copy.start()
        return
    for span, copies in enumerate(groups):

        @pl.when(pick_ref[0] == span)
        def begin():
            for copy in copies:
                copy.start()


def turn_heads(projected, cosine, sine, heads, back=False):
    outs = []
    for h in range(heads):
        v = projected[:, h * HD : (h + 1) * HD]
        turned = pltpu.roll(v, HD // 2, 1) * sine
        outs.append(v * cosine - turned if back else v * cosine + turned)
    return outs


def project(rows_ref, qkv, copies, cosine, sine, heads_ref, total):
    width = rows_ref.shape[1]
    step = width // CHUNKS
    total[...] = jnp.zeros_like(total)
    for k in range(CHUNKS):
        copies[k].wait()
        at = pl.ds(k * step, step)
        total[...] += dot(rows_ref[:, at], qkv[at, :])
    count = total.shape[1] // HD
    turned = turn_heads(total, cosine[...], sine[...], count - 1)
    for h in range(count - 1):
        heads_ref[:, h * HD : (h + 1) * HD] = turned[h].astype(BF)
    heads_ref[:, (count - 1) * HD :] = total[:, (count - 1) * HD :].astype(BF)


def stack_query(ref, b, rows, groups):
    return jnp.concatenate(
        [ref[b * rows : (b + 1) * rows, g * HD : (g + 1) * HD] for g in range(groups)], axis=0
    )


def probabilities(query, key, keep):
    scores = turned_dot(query, key) * (1.0 / math.sqrt(HD))
    exponents = jnp.exp(jnp.where(keep > 0.0, scores, -1e30))
    return exponents / jnp.sum(exponents, axis=-1, keepdims=True)


def load_rows(index, parts, rows_ref, sems, first):
    rows = rows_ref.shape[0] // len(parts)
    return [
        pltpu.make_async_copy(
            src if index is None else src.at[index],
            rows_ref.at[pl.ds(k * rows, rows)],
            sems.at[first + k],
        )
        for k, src in enumerate(parts)
    ]


def layer_call(kind, rows_in, index, tables, pick, qkv_sets, out_sets, saved=None, normed=None):
    n_rows = len(rows_in)
    width = rows_in[0].shape[-1]
    rows = n_rows * rows_in[0].shape[-2]
    half = rows // 2
    which, tables = tables[0], tables[1:]
    spans = len(qkv_sets)
    q_wide = qkv_sets[0][0].shape[1]
    o_wide = out_sets[0][0].shape[1] if out_sets else 0
    groups = q_wide // HD - 2
    n_qkv = len(qkv_sets[0])
    n_out = len(out_sets[0]) if out_sets else 0
    step = width // CHUNKS

    def body(*refs):
        refs = list(refs)
        pick_ref, row_refs = refs[0], refs[1 : 1 + n_rows]
        table_refs, refs = refs[1 + n_rows : 4 + n_rows], refs[4 + n_rows :]
        qkv_refs = [refs[s * n_qkv : (s + 1) * n_qkv] for s in range(spans)]
        refs = refs[spans * n_qkv :]
        out_refs = [refs[s * n_out : (s + 1) * n_out] for s in range(spans)]
        refs = refs[spans * n_out :]
        if kind == "backward":
            heads, normed_refs = refs[0], refs[1 : 1 + n_rows]
            refs = refs[1 + n_rows :]
        n_results = {"forward": 2, "project": 1, "backward": 3}[kind]
        results, refs = refs[:n_results], refs[n_results:]
        rows_ref, qkv, total, sems, cosine, sine, keep = refs[:7]
        refs = refs[7:]
        row_copies = load_rows(index, row_refs, rows_ref, sems, 0)
        table_copies = [
            pltpu.make_async_copy(src.at[which], dst, sems.at[n_rows + k])
            for k, (src, dst) in enumerate(zip(table_refs, (cosine, sine, keep)))
        ]
        sem_more, sem_qkv = n_rows + 3, 2 * n_rows + 3
        qkv_copies = [stack_copies(parts, qkv, sems, sem_qkv) for parts in qkv_refs]
        if n_out:
            out, mixed = refs[:2]
            out_copies = [stack_copies(parts, out, sems, sem_qkv + n_qkv) for parts in out_refs]
        for copy in row_copies + table_copies:
            copy.start()
        if kind == "backward":
            start_copies(pick_ref, out_copies)
            start_copies(pick_ref, qkv_copies)
            d_heads, normed_ref = refs[2:]
            more = load_rows(normed[1], normed_refs, normed_ref, sems, sem_more)
            for copy in more:
                copy.start()
        else:
            start_copies(pick_ref, qkv_copies)
            if n_out:
                start_copies(pick_ref, out_copies)
        for copy in row_copies + table_copies:
            copy.wait()

        if kind == "project":
            project(rows_ref, qkv, qkv_copies[0], cosine, sine, results[0], total)
            return

        if kind == "forward":
            heads = refs[2]
            project(rows_ref, qkv, qkv_copies[0], cosine, sine, heads, total)
            for b in range(2):
                at = slice(b * half, (b + 1) * half)
                query = stack_query(heads, b, half, groups)
                kept = jnp.concatenate([keep[at, :]] * groups, axis=0)
                probs = probabilities(query, heads[at, groups * HD : (groups + 1) * HD], kept)
                got = dot(probs.astype(BF), heads[at, (groups + 1) * HD :]).astype(BF)
                for g in range(groups):
                    mixed[at, g * HD : (g + 1) * HD] = got[g * half : (g + 1) * half]
            for copy in out_copies[0]:
                copy.wait()

            def give(k, carry):
                at = pl.ds(pl.multiple_of(k * step, step), step)
                term = turned_dot(mixed[...], out[at, :]).astype(BF)
                results[0][:, at] = term[:half]
                results[1][:, at] = term[half:]
                return carry

            lax.fori_loop(0, CHUNKS, give, 0)
            return

        total[:, :o_wide] = jnp.zeros((rows, o_wide), F32)
        for k in range(CHUNKS):
            out_copies[0][k].wait()
            at = pl.ds(k * step, step)
            total[:, :o_wide] += dot(rows_ref[:, at], out[at, :])
        mixed[...] = total[:, :o_wide].astype(BF)
        for b in range(2):
            at = slice(b * half, (b + 1) * half)
            query = stack_query(heads, b, half, groups)
            push = stack_query(mixed, b, half, groups)
            key = heads[at, groups * HD : (groups + 1) * HD]
            value = heads[at, (groups + 1) * HD :]
            kept = jnp.concatenate([keep[at, :]] * groups, axis=0)
            probs = probabilities(query, key, kept)
            d_probs = turned_dot(push, value)
            centre = jnp.sum(d_probs * probs, axis=-1, keepdims=True)
            d_scores = (probs * (d_probs - centre) * (1.0 / math.sqrt(HD))).astype(BF)
            over_rows = (((0,), (0,)), ((), ()))
            d_value = lax.dot_general(probs.astype(BF), push, over_rows, preferred_element_type=F32)
            d_key = lax.dot_general(d_scores, query, over_rows, preferred_element_type=F32)
            d_query = dot(d_scores, key)
            c, s = cosine[at, :], sine[at, :]
            for g in range(groups):
                piece = d_query[g * half : (g + 1) * half]
                d_heads[at, g * HD : (g + 1) * HD] = turn_heads(piece, c, s, 1, True)[0].astype(BF)
            d_heads[at, groups * HD : (groups + 1) * HD] = turn_heads(d_key, c, s, 1, True)[0].astype(BF)
            d_heads[at, (groups + 1) * HD :] = d_value.astype(BF)
        for copy in qkv_copies[0]:
            copy.wait()
        for copy in more:
            copy.wait()

        def give_back(k, carry):
            at = pl.ds(pl.multiple_of(k * step, step), step)
            term = turned_dot(d_heads[...], qkv[at, :])
            results[2][:, at] = jnp.sum(
                term * normed_ref[:, at].astype(F32), axis=0, keepdims=True
            )
            term = term.astype(BF)
            results[0][:, at] = term[:half]
            results[1][:, at] = term[half:]
            return carry

        lax.fori_loop(0, CHUNKS, give_back, 0)

    outs = {
        "forward": (shape((half, width)),) * 2,
        "project": shape((rows, q_wide)),
        "backward": (shape((half, width)),) * 2 + (shape((1, width), F32),),
    }[kind]
    scratch = [
        pltpu.VMEM((rows, width), BF),
        pltpu.VMEM((width, q_wide), BF),
        pltpu.VMEM((rows, q_wide), F32),
        pltpu.SemaphoreType.DMA((2 * n_rows + 3 + n_qkv + n_out,)),
    ] + [pltpu.VMEM((rows, table.shape[-1]), F32) for table in tables]
    if n_out:
        scratch += [pltpu.VMEM((width, o_wide), BF), pltpu.VMEM((rows, o_wide), BF)]
        scratch += [pltpu.VMEM((rows, q_wide), BF)]
    args = [pick, *rows_in, *tables]
    specs = [SM] + [HB] * (n_rows + 3)
    for parts in list(qkv_sets) + list(out_sets):
        args += parts
        specs += [HB] * len(parts)
    if kind == "backward":
        args += [saved, *normed[0]]
        specs += [VM] + [HB] * n_rows
        scratch += [pltpu.VMEM((rows, width), BF)]
    flops = 2 * rows * width * (q_wide + o_wide)
    return kernel_call(body, outs, specs, scratch, flops=flops, moved=14 << 20)(*args)


def all_tables(ids, z):
    count = ids.shape[-1]
    block = count // 4
    row = jnp.arange(count, dtype=jnp.int32)
    own = (z + jnp.array(RING, jnp.int32)) % 4
    index = (own[:, None] * block + jnp.arange(block, dtype=jnp.int32)).reshape(count)
    picked = (index[:, None] == row).astype(F32)
    ids = ids.astype(F32)
    relative = jnp.sum(ids[:, :, None, :] * picked, axis=-1)
    starts = jnp.sum((ids[:, :, None, :] < relative[:, :, :, None]).astype(F32), axis=-1)
    positions = index.astype(F32) - starts
    halfway = HD // 2
    frequency = jnp.exp(jnp.arange(halfway, dtype=F32) * (-2.0 * math.log(ROPE_BASE) / HD))
    angles = positions[..., None] * frequency
    cosine, sine = jnp.cos(angles), jnp.sin(angles)
    cosine = jnp.concatenate([cosine, cosine], axis=-1).reshape(4, 2 * count, HD)
    sine = jnp.concatenate([-sine, sine], axis=-1).reshape(4, 2 * count, HD)
    kept = (relative[..., :, None] == relative[..., None, :]) & (index[:, None] >= index[None, :])
    return cosine, sine, kept.astype(F32).reshape(4, 2 * count, count)


def sum_gains(part):
    order = chip_order()[1]
    part = part + shift(part, "z", 2)
    part = part + shift(part, "z", 1)
    part = part + chip_move(part, SIBLING)
    block = part.shape[1] // 16
    part = jnp.take(part.reshape(2, 16, block), order, axis=1).reshape(part.shape)
    part = part + shift(part, "y", 2)
    part = part + shift(part, "y", 1)
    part = part + chip_move(part, BESIDE)
    other = chip_move(part, ACROSS)
    return jnp.where(lax.axis_index("s") == lax.axis_index("xh"), part, other)


def chip_order():
    y, x = lax.axis_index("y"), lax.axis_index("xh") * 2 + lax.axis_index("xl")
    ring, near = jnp.array(RING, jnp.int32), jnp.array(NEAR, jnp.int32)
    place = ((y + ring) % 4)[:, None] * 4 + jnp.bitwise_xor(x, near)[None, :]
    every = jnp.arange(4, dtype=jnp.int32)
    ring_back, near_back = jnp.array(RING_BACK, jnp.int32), jnp.array(RING_BACK, jnp.int32)
    back_y = jnp.sum(
        jnp.where(((every - y) % 4)[:, None] == every[None, :], ring_back[None, :], 0), axis=1
    )
    back_x = jnp.sum(
        jnp.where(jnp.bitwise_xor(every, x)[:, None] == every[None, :], near_back[None, :], 0),
        axis=1,
    )
    back = back_y[:, None] * 4 + back_x[None, :]
    return place.reshape(16).astype(jnp.int32), back.reshape(16).astype(jnp.int32)


def per_device(
    fwd_state, bwd_state, stash, gains, w_query, w_key, w_value, w_out, fwd_segments, bwd_segments
):
    a, core, z = lax.axis_index("xh"), lax.axis_index("s"), lax.axis_index("z")
    match = core == a
    one = lambda v: v.astype(jnp.int32).reshape(1)
    place, back = chip_order()
    across = jnp.array([4 * y + (x ^ 1) for y in range(4) for x in range(4)], jnp.int32)

    kept0, home0, kept1, home1 = split_weights(
        one(a), w_query[0], w_key[0], w_value[0], w_out[0]
    )
    home1 = chip_move(home1, HOME)
    guest1 = chip_move(kept1, GUEST)
    local = jnp.concatenate([fwd_state, bwd_state, stash[0]], axis=0)
    gains_sibling = chip_move(gains[0], SIBLING)
    own_ids = jnp.stack([fwd_segments[:, 0], bwd_segments[:, 0]])
    partner_ids = chip_move(own_ids, ACROSS)
    q1, o1 = join_slots(one(match), kept1, home1, guest1)

    q1_x, o1_x = beside(q1), beside(o1)
    q1_b, q1_a = y_both(q1)
    o1_b, o1_a = y_both(o1)
    guest_rows = chip_move(local, GUEST)
    home0 = chip_move(home0, HOME)
    guest0 = chip_move(kept0, GUEST)
    ids = jnp.stack(
        [jnp.where(match, own_ids, partner_ids), jnp.where(match, partner_ids, own_ids)],
        axis=2,
    )
    ids = jnp.where(a == 0, ids, ids[:, ::-1]).reshape(4, 2, -1)
    all_cosines, all_sines, all_kept = lax.optimization_barrier(all_tables(ids, z))
    scalars = jnp.stack([match.astype(jnp.int32), a.astype(jnp.int32)])
    rows, keep, scale, gain = start_rows(scalars, place, local, guest_rows, gains[0], gains_sibling)
    o1_o = shift(o1_b, "y", 1)
    o1_bx, o1_ax = beside(o1_b), beside(o1_a)
    q1_xb, q1_xa = y_both(q1_x)
    q1_o = shift(q1_b, "y", 1)
    q0, o0 = join_slots(one(match), kept0, home0, guest0)
    o0_b, o0_a = y_both(o0)
    q0_x = beside(q0)
    rows_b, rows_a = gather_near(rows)
    rows_s = chip_move(rows, SIBLING)
    q1_ox = shift(q1_xa, "y", -1)
    q0_b, q0_a = y_both(q0)
    o1_ox, o0_x = beside(o1_o), beside(o0)
    rows_o = shift(rows_b, "z", 1)
    rows_bs, rows_as = chip_move(rows_b, SIBLING), chip_move(rows_a, SIBLING)
    o0_o = shift(o0_a, "y", -1)
    o0_bx, o0_ax = beside(o0_b), beside(o0_a)
    q0_xb, q0_xa = y_both(q0_x)
    q0_o = shift(q0_b, "y", 1)
    rows_os = chip_move(rows_o, SIBLING)
    q0_ox = shift(q0_xa, "y", -1)
    o0_ox = beside(o0_o)
    entering = (rows, rows_b, rows_a, rows_o, rows_s, rows_bs, rows_as, rows_os)

    qkv_parts = [
        [q0, q0_x, q0_b, q0_xb, q0_a, q0_xa, q0_o, q0_ox],
        [q1, q1_x, q1_b, q1_xb, q1_a, q1_xa, q1_o, q1_ox],
    ]
    out_parts = [
        [o0, o0_x, o0_b, o0_bx, o0_a, o0_ax, o0_o, o0_ox],
        [o1, o1_x, o1_b, o1_bx, o1_a, o1_ax, o1_o, o1_ox],
    ]
    gain_late = jnp.where(a == 0, gain[1:2], gain[0:1])
    gain_bwd = (gain[1:2], gain_late)

    tables = [(k, all_cosines, all_sines, all_kept) for k in range(4)]

    late = one(jnp.where(a == 0, 1, 0))
    state, grad = keep[0], keep[1]
    fwd_in, fwd_at = entering, 0
    cotangent, cot_at = entering, 1
    stash_in = ((entering, 2), (entering, 3))
    sets = (qkv_parts, out_parts)
    gain_sum = []
    for tick in range(2):
        spans_fwd, spans_bwd = (([0], [1]), ([0, 1], [0, 1]))[tick]
        qkv_fwd, out_fwd = ([table[s] for s in spans_fwd] for table in sets)
        qkv_bwd, out_bwd = ([table[s] for s in spans_bwd] for table in sets)
        mine, other = layer_call("forward", fwd_in, fwd_at, tables[tick], late, qkv_fwd, out_fwd)
        stash_rows, stash_at = stash_in[tick]
        heads = layer_call("project", stash_rows, stash_at, tables[2 + tick], late, qkv_bwd, [])
        b_mine, b_other, gain_part = layer_call(
            "backward",
            cotangent,
            cot_at,
            tables[2 + tick],
            late,
            qkv_bwd,
            out_bwd,
            saved=heads,
            normed=stash_in[tick],
        )
        gain_sum.append(gain_part / gain_bwd[tick])
        order = across if tick == 0 else back
        pushed = scatter_rows(b_mine, b_other)
        grad = finish_backward(order, pushed, grad, keep[2 + tick], scale[2 + tick], gain_bwd[tick])
        state = finish_forward(order, scatter_rows(mine, other), state)
        if tick == 0:
            state = chip_move(state, ACROSS)
            grad = chip_move(grad, ACROSS)
            fwd_in, fwd_at = gather_rows(norm_rows(state, gain_late)), None
            cotangent, cot_at = gather_rows(grad), None

    state_out = chip_move(state, HOME)
    grad_out = chip_move(grad, HOME)
    on_first = jnp.where(a == 1, 1.0, 0.0)
    gain_rows = jnp.concatenate(
        [gain_sum[1] * on_first, gain_sum[0] + gain_sum[1] * (1.0 - on_first)], axis=0
    )
    gain_total = sum_gains(gain_rows)
    return (state_out[None], grad_out[None], gain_total[None])


def solution(mesh):
    grid = Mesh(mesh.devices.reshape(4, 2, 2, 2, 4), ("y", "xh", "xl", "s", "z"))
    dp = ("y", "xh", "xl")
    in_specs = (
        P("s", dp + ("z",), None),
        P("s", dp + ("z",), None),
        P("s", None, dp + ("z",), None),
        P("s", None, None),
        P("s", None, dp, "z"),
        P("s", None, dp, "z"),
        P("s", None, dp, "z"),
        P("s", None, "z", dp),
        P(None, dp, None),
        P(None, dp, None),
    )
    out_specs = (
        P("s", dp + ("z",), None),
        P("s", dp + ("z",), None),
        P("s", None, None),
    )

    return jax.shard_map(
        per_device, mesh=grid, in_specs=in_specs, out_specs=out_specs, check_vma=False
    )
```

```python
import math

import jax
import jax.numpy as jnp
from jax import lax
from jax.experimental import pallas as pl
from jax.experimental.pallas import tpu as pltpu
from jax.sharding import Mesh, PartitionSpec as P

HD = 128
ROPE_BASE = 1000000.0
BF = jnp.bfloat16
F32 = jnp.float32


CHIP = ("xh", "xl", "s")


def spot(xh, xl, core):
    return (xh * 2 + xl) * 2 + core


PLACES = [(xh, xl, core) for xh in (0, 1) for xl in (0, 1) for core in (0, 1)]
SIBLING = [(spot(a, l, c), spot(a, l, 1 - c)) for a, l, c in PLACES]
ACROSS = [(spot(a, l, c), spot(1 - a, 1 - l, c)) for a, l, c in PLACES]
BESIDE = [(spot(a, l, c), spot(a, 1 - l, c)) for a, l, c in PLACES]
HOME = [
    (spot(a, l, c), spot(a, l, 1 - c) if c == a else spot(1 - a, 1 - l, c)) for a, l, c in PLACES
]
GUEST = [(spot(a, l, c), spot(1 - a, 1 - l, 1 - c)) for a, l, c in PLACES if c != a]


def chip_move(value, pairs):
    return lax.ppermute(value, CHIP, pairs)


def shift(value, axis, steps):
    count = lax.axis_size(axis)
    return lax.ppermute(value, axis, [(i, (i + steps) % count) for i in range(count)])


RING = (0, 3, 1, 2)
RING_BACK = (0, 2, 3, 1)


NEAR = (0, 3, 1, 2)
VM = pl.BlockSpec(memory_space=pltpu.VMEM)
SM = pl.BlockSpec(memory_space=pltpu.SMEM)
HB = pl.BlockSpec(memory_space=pltpu.HBM)
CHUNKS = 8


def shape(dims, kind=BF):
    return jax.ShapeDtypeStruct(dims, kind)


def kernel_call(body, outs, in_specs, scratch=(), flops=0, moved=0, out_spec=VM):
    return pl.pallas_call(
        body,
        out_shape=outs,
        in_specs=in_specs,
        out_specs=jax.tree.map(lambda unused: out_spec, outs),
        scratch_shapes=list(scratch),
        cost_estimate=pl.CostEstimate(flops=flops, bytes_accessed=moved, transcendentals=0),
        compiler_params=pltpu.CompilerParams(vmem_limit_bytes=67043328),
    )


def turned_dot(left, right):
    return lax.dot_general(left, right, (((1,), (1,)), ((), ())), preferred_element_type=F32)


def dot(left, right):
    return jnp.dot(left, right, preferred_element_type=F32)


def split_weights(a, w_query, w_key, w_value, w_out):
    block = w_query.shape[1]
    q_cols, k_cols, o_rows = w_query.shape[2] // 2, w_key.shape[2] // 2, w_out.shape[1] // 2
    wide = q_cols + 2 * k_cols + o_rows

    def body(a_ref, q_ref, k_ref, v_ref, o_ref, *outs):
        for span in range(2):
            for which in range(2):
                half = a_ref[0] if which == 0 else 1 - a_ref[0]
                out = outs[span * 2 + which]
                q_at = pl.multiple_of(half * q_cols, q_cols)
                k_at = pl.multiple_of(half * k_cols, k_cols)
                o_at = pl.multiple_of(half * o_rows, o_rows)
                out[:, :q_cols] = q_ref[span, :, pl.ds(q_at, q_cols)]
                out[:, q_cols : q_cols + k_cols] = k_ref[span, :, pl.ds(k_at, k_cols)]
                out[:, q_cols + k_cols : q_cols + 2 * k_cols] = v_ref[span, :, pl.ds(k_at, k_cols)]
                out[:, q_cols + 2 * k_cols :] = o_ref[span, pl.ds(o_at, o_rows), :].T

    outs = tuple(shape((block, wide)) for _ in range(4))
    return kernel_call(body, outs, [SM] + [VM] * 4, moved=10 << 20)(
        a, w_query, w_key, w_value, w_out
    )


def join_slots(match, kept, home, guest):
    block, wide = kept.shape
    cut = wide - wide * 2 // 5

    def body(match_ref, kept_ref, home_ref, guest_ref, qkv_ref, out_ref):
        def put(at, value_ref):
            qkv_ref[pl.ds(at, block), :] = value_ref[:, :cut]
            out_ref[pl.ds(at, block), :] = value_ref[:, cut:]

        @pl.when(match_ref[0] == 1)
        def own():
            put(0, kept_ref)
            put(block, home_ref)

        @pl.when(match_ref[0] == 0)
        def moved():
            put(0, home_ref)
            put(block, guest_ref)

    outs = (shape((2 * block, cut)), shape((2 * block, wide - cut)))
    return kernel_call(body, outs, [SM] + [VM] * 3, moved=3 << 20)(match, kept, home, guest)


def y_both(value):
    return shift(value, "y", 1), shift(value, "y", -1)


def beside(value):
    return chip_move(value, BESIDE)


def reorder(order_ref, width, block, take_from, put_to):
    for k in range(width // block):
        at = pl.multiple_of(order_ref[k] * block, block)
        put_to(k * block, take_from(at))


def start_rows(scalars, order, local, guest, gains, gains_sibling):
    kinds, rows, width = local.shape
    block = width // 16

    def body(s_ref, order_ref, local_ref, guest_ref, g_ref, h_ref, out, keep, scale, one_ref, late_ref, gain):
        match, a = s_ref[0] == 1, s_ref[1]

        def take_gain(at):
            return jnp.where(match, g_ref[:, pl.ds(at, block)], h_ref[:, pl.ds(at, block)])

        def put_gain(at, value):
            gain[:, at : at + block] = value.astype(F32)

        reorder(order_ref, width, block, take_gain, put_gain)
        late = jnp.where(a == 0, gain[1:2, :], gain[0:1, :])
        one_ref[...] = gain[1:2, :]
        late_ref[...] = late
        for kind in range(4):

            def take_rows(at):
                return jnp.where(
                    match, local_ref[kind, :, pl.ds(at, block)], guest_ref[kind, :, pl.ds(at, block)]
                )

            def put_rows(at, value):
                keep[kind, :, at : at + block] = value

            reorder(order_ref, width, block, take_rows, put_rows)
            value = keep[kind]
            if kind == 1:
                out[kind] = value
                continue
            value = value.astype(F32)
            by = lax.rsqrt(jnp.mean(value * value, axis=1, keepdims=True) + 1e-06)
            factor = (gain[0:1, :], None, gain[1:2, :], late)[kind]
            out[kind] = (value * by * factor).astype(BF)
            scale[kind] = jnp.broadcast_to(by, (rows, 128))

    outs = (
        shape((kinds, rows, width)),
        shape((kinds, rows, width)),
        shape((kinds, rows, 128), F32),
        shape((1, width), F32),
        shape((1, width), F32),
    )
    scratch = [pltpu.VMEM((2, width), F32)]
    return kernel_call(body, outs, [SM, SM] + [VM] * 4, scratch, moved=6 << 20)(
        scalars, order, local, guest, gains, gains_sibling
    )


def norm_rows(state, gain_row):
    def body(state_ref, gain_ref, out_ref):
        value = state_ref[...].astype(F32)
        by = lax.rsqrt(jnp.mean(value * value, axis=1, keepdims=True) + 1e-06)
        out_ref[...] = (value * by * gain_ref[...]).astype(BF)

    return kernel_call(body, shape(state.shape), [VM, VM], moved=1 << 19)(state, gain_row)


def gather_near(value):
    return shift(value, "z", 1), shift(value, "z", -1)


def gather_rows(value):
    near = gather_near(value)
    far = shift(near[1], "z", -1)
    parts = (value, *near, far)
    twins = tuple(chip_move(part, SIBLING) for part in parts[:3])
    return parts + twins + (chip_move(far, SIBLING),)


def scatter_rows(mine, other):
    came = chip_move(other, SIBLING)
    rows, width = mine.shape
    block = rows // 4

    def body(mine_ref, came_ref, own, one, two, three, left, right, wide, narrow, sems):
        loads = {}
        for k in (1, 2, 3, 0):
            at = pl.ds(k * block, block)
            loads[k] = (
                pltpu.make_async_copy(mine_ref.at[at], left.at[at], sems.at[k]),
                pltpu.make_async_copy(came_ref.at[at], right.at[at], sems.at[4 + k]),
            )
            for copy in loads[k]:
                copy.start()
        stores = []
        for k in (1, 2, 3, 0):
            for copy in loads[k]:
                copy.wait()
            at = pl.ds(k * block, block)
            total = left[at, :].astype(F32) + right[at, :].astype(F32)
            held = narrow.at[k - 1] if k else wide
            held[...] = total.astype(held.dtype)
            out = (own, one, two, three)[k]
            stores.append(pltpu.make_async_copy(held, out, sems.at[8 + k]))
            stores[-1].start()
        for copy in stores:
            copy.wait()

    outs = (shape((block, width), F32),) + (shape((block, width)),) * 3
    scratch = [pltpu.VMEM((rows, width), BF), pltpu.VMEM((rows, width), BF)]
    scratch += [pltpu.VMEM((block, width), F32), pltpu.VMEM((3, block, width), BF)]
    scratch += [pltpu.SemaphoreType.DMA((12,))]
    own, one, two, three = kernel_call(
        body, outs, [HB, HB], scratch, moved=4 << 20, out_spec=HB
    )(mine, came)
    return own, shift(one, "z", -1), shift(two, "z", 1), shift(three, "z", 2)


def finish_forward(order, parts, state):
    rows, width = state.shape
    block = width // 16

    def body(order_ref, own, one, two, three, state_ref, out_ref):
        def total(at):
            at = pl.ds(at, block)
            value = own[:, at] + one[:, at].astype(F32) + two[:, at].astype(F32)
            value = value + three[:, at].astype(F32) + state_ref[:, at].astype(F32)
            return value.astype(BF)

        def put(at, value):
            out_ref[:, at : at + block] = value

        reorder(order_ref, width, block, total, put)

    return kernel_call(body, shape((rows, width)), [SM] + [VM] * 5, moved=2 << 20)(
        order, *parts, state
    )


def finish_backward(order, parts, grad, kept, scale, gain_row):
    rows, width = grad.shape
    block = width // 16

    def body(order_ref, own, one, two, three, grad_ref, kept_ref, scale_ref, gain_ref, out_ref, hold):
        by = scale_ref[:, :1]
        pushed = own[...] + one[...].astype(F32) + two[...].astype(F32) + three[...].astype(F32)
        pushed = pushed * gain_ref[...]
        value = kept_ref[...].astype(F32)
        lean = jnp.mean(value * pushed, axis=1, keepdims=True) * (by * by * by)
        hold[...] = (grad_ref[...].astype(F32) + pushed * by - value * lean).astype(BF)

        def put(at, piece):
            out_ref[:, at : at + block] = piece

        reorder(order_ref, width, block, lambda at: hold[:, pl.ds(at, block)], put)

    return kernel_call(
        body,
        shape((rows, width)),
        [SM] + [VM] * 8,
        scratch=[pltpu.VMEM((rows, width), BF)],
        moved=2 << 20,
    )(order, *parts, grad, kept, scale, gain_row)


def stack_copies(parts, target, sems, at):
    copies, row = [], 0
    for k, part in enumerate(parts):
        rows = part.shape[0]
        copies.append(pltpu.make_async_copy(part, target.at[pl.ds(row, rows)], sems.at[at + k]))
        row += rows
    return copies


def start_copies(pick_ref, groups):
    if len(groups) == 1:
        for copy in groups[0]:
            copy.start()
        return
    for span, copies in enumerate(groups):

        @pl.when(pick_ref[0] == span)
        def begin():
            for copy in copies:
                copy.start()


def turn_heads(projected, cosine, sine, heads, back=False):
    outs = []
    for h in range(heads):
        v = projected[:, h * HD : (h + 1) * HD]
        turned = pltpu.roll(v, HD // 2, 1) * sine
        outs.append(v * cosine - turned if back else v * cosine + turned)
    return outs


def project(rows_ref, qkv, copies, cosine, sine, heads_ref, total):
    width = rows_ref.shape[1]
    step = width // CHUNKS
    total[...] = jnp.zeros_like(total)
    for k in range(CHUNKS):
        copies[k].wait()
        at = pl.ds(k * step, step)
        total[...] += dot(rows_ref[:, at], qkv[at, :])
    count = total.shape[1] // HD
    turned = turn_heads(total, cosine[...], sine[...], count - 1)
    for h in range(count - 1):
        heads_ref[:, h * HD : (h + 1) * HD] = turned[h].astype(BF)
    heads_ref[:, (count - 1) * HD :] = total[:, (count - 1) * HD :].astype(BF)


def stack_query(ref, b, rows, groups):
    return jnp.concatenate(
        [ref[b * rows : (b + 1) * rows, g * HD : (g + 1) * HD] for g in range(groups)], axis=0
    )


def probabilities(query, key, keep):
    scores = turned_dot(query, key) * (1.0 / math.sqrt(HD))
    exponents = jnp.exp(jnp.where(keep > 0.0, scores, -1e30))
    return exponents / jnp.sum(exponents, axis=-1, keepdims=True)


def load_rows(index, parts, rows_ref, sems, first):
    rows = rows_ref.shape[0] // len(parts)
    return [
        pltpu.make_async_copy(
            src if index is None else src.at[index],
            rows_ref.at[pl.ds(k * rows, rows)],
            sems.at[first + k],
        )
        for k, src in enumerate(parts)
    ]


def layer_call(kind, rows_in, index, tables, pick, qkv_sets, out_sets, saved=None, normed=None):
    n_rows = len(rows_in)
    width = rows_in[0].shape[-1]
    rows = n_rows * rows_in[0].shape[-2]
    half = rows // 2
    which, tables = tables[0], tables[1:]
    spans = len(qkv_sets)
    q_wide = qkv_sets[0][0].shape[1]
    o_wide = out_sets[0][0].shape[1] if out_sets else 0
    groups = q_wide // HD - 2
    n_qkv = len(qkv_sets[0])
    n_out = len(out_sets[0]) if out_sets else 0
    step = width // CHUNKS

    def body(*refs):
        refs = list(refs)
        pick_ref, row_refs = refs[0], refs[1 : 1 + n_rows]
        table_refs, refs = refs[1 + n_rows : 4 + n_rows], refs[4 + n_rows :]
        qkv_refs = [refs[s * n_qkv : (s + 1) * n_qkv] for s in range(spans)]
        refs = refs[spans * n_qkv :]
        out_refs = [refs[s * n_out : (s + 1) * n_out] for s in range(spans)]
        refs = refs[spans * n_out :]
        if kind == "backward":
            heads, normed_refs = refs[0], refs[1 : 1 + n_rows]
            refs = refs[1 + n_rows :]
        n_results = {"forward": 2, "project": 1, "backward": 3}[kind]
        results, refs = refs[:n_results], refs[n_results:]
        rows_ref, qkv, total, sems, cosine, sine, keep = refs[:7]
        refs = refs[7:]
        row_copies = load_rows(index, row_refs, rows_ref, sems, 0)
        table_copies = [
            pltpu.make_async_copy(src.at[which], dst, sems.at[n_rows + k])
            for k, (src, dst) in enumerate(zip(table_refs, (cosine, sine, keep)))
        ]
        sem_more, sem_qkv = n_rows + 3, 2 * n_rows + 3
        qkv_copies = [stack_copies(parts, qkv, sems, sem_qkv) for parts in qkv_refs]
        if n_out:
            out, mixed = refs[:2]
            out_copies = [stack_copies(parts, out, sems, sem_qkv + n_qkv) for parts in out_refs]
        for copy in row_copies + table_copies:
            copy.start()
        if kind == "backward":
            start_copies(pick_ref, out_copies)
            start_copies(pick_ref, qkv_copies)
            d_heads, normed_ref = refs[2:]
            more = load_rows(normed[1], normed_refs, normed_ref, sems, sem_more)
            for copy in more:
                copy.start()
        else:
            start_copies(pick_ref, qkv_copies)
            if n_out:
                start_copies(pick_ref, out_copies)
        for copy in row_copies + table_copies:
            copy.wait()

        if kind == "project":
            project(rows_ref, qkv, qkv_copies[0], cosine, sine, results[0], total)
            return

        if kind == "forward":
            heads = refs[2]
            project(rows_ref, qkv, qkv_copies[0], cosine, sine, heads, total)
            for b in range(2):
                at = slice(b * half, (b + 1) * half)
                query = stack_query(heads, b, half, groups)
                kept = jnp.concatenate([keep[at, :]] * groups, axis=0)
                probs = probabilities(query, heads[at, groups * HD : (groups + 1) * HD], kept)
                got = dot(probs.astype(BF), heads[at, (groups + 1) * HD :]).astype(BF)
                for g in range(groups):
                    mixed[at, g * HD : (g + 1) * HD] = got[g * half : (g + 1) * half]
            for copy in out_copies[0]:
                copy.wait()

            def give(k, carry):
                at = pl.ds(pl.multiple_of(k * step, step), step)
                term = turned_dot(mixed[...], out[at, :]).astype(BF)
                results[0][:, at] = term[:half]
                results[1][:, at] = term[half:]
                return carry

            lax.fori_loop(0, CHUNKS, give, 0)
            return

        total[:, :o_wide] = jnp.zeros((rows, o_wide), F32)
        for k in range(CHUNKS):
            out_copies[0][k].wait()
            at = pl.ds(k * step, step)
            total[:, :o_wide] += dot(rows_ref[:, at], out[at, :])
        mixed[...] = total[:, :o_wide].astype(BF)
        for b in range(2):
            at = slice(b * half, (b + 1) * half)
            query = stack_query(heads, b, half, groups)
            push = stack_query(mixed, b, half, groups)
            key = heads[at, groups * HD : (groups + 1) * HD]
            value = heads[at, (groups + 1) * HD :]
            kept = jnp.concatenate([keep[at, :]] * groups, axis=0)
            probs = probabilities(query, key, kept)
            d_probs = turned_dot(push, value)
            centre = jnp.sum(d_probs * probs, axis=-1, keepdims=True)
            d_scores = (probs * (d_probs - centre) * (1.0 / math.sqrt(HD))).astype(BF)
            over_rows = (((0,), (0,)), ((), ()))
            d_value = lax.dot_general(probs.astype(BF), push, over_rows, preferred_element_type=F32)
            d_key = lax.dot_general(d_scores, query, over_rows, preferred_element_type=F32)
            d_query = dot(d_scores, key)
            c, s = cosine[at, :], sine[at, :]
            for g in range(groups):
                piece = d_query[g * half : (g + 1) * half]
                d_heads[at, g * HD : (g + 1) * HD] = turn_heads(piece, c, s, 1, True)[0].astype(BF)
            d_heads[at, groups * HD : (groups + 1) * HD] = turn_heads(d_key, c, s, 1, True)[0].astype(BF)
            d_heads[at, (groups + 1) * HD :] = d_value.astype(BF)
        for copy in qkv_copies[0]:
            copy.wait()
        for copy in more:
            copy.wait()

        def give_back(k, carry):
            at = pl.ds(pl.multiple_of(k * step, step), step)
            term = turned_dot(d_heads[...], qkv[at, :])
            results[2][:, at] = jnp.sum(
                term * normed_ref[:, at].astype(F32), axis=0, keepdims=True
            )
            term = term.astype(BF)
            results[0][:, at] = term[:half]
            results[1][:, at] = term[half:]
            return carry

        lax.fori_loop(0, CHUNKS, give_back, 0)

    outs = {
        "forward": (shape((half, width)),) * 2,
        "project": shape((rows, q_wide)),
        "backward": (shape((half, width)),) * 2 + (shape((1, width), F32),),
    }[kind]
    scratch = [
        pltpu.VMEM((rows, width), BF),
        pltpu.VMEM((width, q_wide), BF),
        pltpu.VMEM((rows, q_wide), F32),
        pltpu.SemaphoreType.DMA((2 * n_rows + 3 + n_qkv + n_out,)),
    ] + [pltpu.VMEM((rows, table.shape[-1]), F32) for table in tables]
    if n_out:
        scratch += [pltpu.VMEM((width, o_wide), BF), pltpu.VMEM((rows, o_wide), BF)]
        scratch += [pltpu.VMEM((rows, q_wide), BF)]
    args = [pick, *rows_in, *tables]
    specs = [SM] + [HB] * (n_rows + 3)
    for parts in list(qkv_sets) + list(out_sets):
        args += parts
        specs += [HB] * len(parts)
    if kind == "backward":
        args += [saved, *normed[0]]
        specs += [VM] + [HB] * n_rows
        scratch += [pltpu.VMEM((rows, width), BF)]
    flops = 2 * rows * width * (q_wide + o_wide)
    return kernel_call(body, outs, specs, scratch, flops=flops, moved=14 << 20)(*args)


def all_tables(ids, z):
    count = ids.shape[-1]
    block = count // 4
    row = jnp.arange(count, dtype=jnp.int32)
    own = (z + jnp.array(RING, jnp.int32)) % 4
    index = (own[:, None] * block + jnp.arange(block, dtype=jnp.int32)).reshape(count)
    picked = (index[:, None] == row).astype(F32)
    ids = ids.astype(F32)
    relative = jnp.sum(ids[:, :, None, :] * picked, axis=-1)
    starts = jnp.sum((ids[:, :, None, :] < relative[:, :, :, None]).astype(F32), axis=-1)
    positions = index.astype(F32) - starts
    halfway = HD // 2
    frequency = jnp.exp(jnp.arange(halfway, dtype=F32) * (-2.0 * math.log(ROPE_BASE) / HD))
    angles = positions[..., None] * frequency
    cosine, sine = jnp.cos(angles), jnp.sin(angles)
    cosine = jnp.concatenate([cosine, cosine], axis=-1).reshape(4, 2 * count, HD)
    sine = jnp.concatenate([-sine, sine], axis=-1).reshape(4, 2 * count, HD)
    kept = (relative[..., :, None] == relative[..., None, :]) & (index[:, None] >= index[None, :])
    return cosine, sine, kept.astype(F32).reshape(4, 2 * count, count)


def sum_gains(part):
    order = chip_order()[1]
    part = part + shift(part, "z", 2)
    part = part + shift(part, "z", 1)
    part = part + chip_move(part, SIBLING)
    block = part.shape[1] // 16
    part = jnp.take(part.reshape(2, 16, block), order, axis=1).reshape(part.shape)
    part = part + shift(part, "y", 2)
    part = part + shift(part, "y", 1)
    part = part + chip_move(part, BESIDE)
    other = chip_move(part, ACROSS)
    return jnp.where(lax.axis_index("s") == lax.axis_index("xh"), part, other)


def chip_order():
    y, x = lax.axis_index("y"), lax.axis_index("xh") * 2 + lax.axis_index("xl")
    ring, near = jnp.array(RING, jnp.int32), jnp.array(NEAR, jnp.int32)
    place = ((y + ring) % 4)[:, None] * 4 + jnp.bitwise_xor(x, near)[None, :]
    every = jnp.arange(4, dtype=jnp.int32)
    ring_back, near_back = jnp.array(RING_BACK, jnp.int32), jnp.array(RING_BACK, jnp.int32)
    back_y = jnp.sum(
        jnp.where(((every - y) % 4)[:, None] == every[None, :], ring_back[None, :], 0), axis=1
    )
    back_x = jnp.sum(
        jnp.where(jnp.bitwise_xor(every, x)[:, None] == every[None, :], near_back[None, :], 0),
        axis=1,
    )
    back = back_y[:, None] * 4 + back_x[None, :]
    return place.reshape(16).astype(jnp.int32), back.reshape(16).astype(jnp.int32)


def per_device(
    fwd_state, bwd_state, stash, gains, w_query, w_key, w_value, w_out, fwd_segments, bwd_segments
):
    a, core, z = lax.axis_index("xh"), lax.axis_index("s"), lax.axis_index("z")
    match = core == a
    one = lambda v: v.astype(jnp.int32).reshape(1)
    place, back = chip_order()
    across = jnp.array([4 * y + (x ^ 1) for y in range(4) for x in range(4)], jnp.int32)

    kept0, home0, kept1, home1 = split_weights(
        one(a), w_query[0], w_key[0], w_value[0], w_out[0]
    )
    home1 = chip_move(home1, HOME)
    guest1 = chip_move(kept1, GUEST)
    local = jnp.concatenate([fwd_state, bwd_state, stash[0]], axis=0)
    own_ids = jnp.stack([fwd_segments[:, 0], bwd_segments[:, 0]])
    gains_sibling = chip_move(gains[0], SIBLING)
    partner_ids = chip_move(own_ids, ACROSS)
    q1, o1 = join_slots(one(match), kept1, home1, guest1)

    q1_x, o1_x = beside(q1), beside(o1)
    q1_b, q1_a = y_both(q1)
    o1_b, o1_a = y_both(o1)
    guest_rows = chip_move(local, GUEST)
    home0 = chip_move(home0, HOME)
    guest0 = chip_move(kept0, GUEST)
    ids = jnp.stack(
        [jnp.where(match, own_ids, partner_ids), jnp.where(match, partner_ids, own_ids)],
        axis=2,
    )
    ids = jnp.where(a == 0, ids, ids[:, ::-1]).reshape(4, 2, -1)
    all_cosines, all_sines, all_kept = lax.optimization_barrier(all_tables(ids, z))
    scalars = jnp.stack([match.astype(jnp.int32), a.astype(jnp.int32)])
    rows, keep, scale, gain_one, gain_late = start_rows(
        scalars, place, local, guest_rows, gains[0], gains_sibling
    )
    o1_o = shift(o1_b, "y", 1)
    o1_bx, o1_ax = beside(o1_b), beside(o1_a)
    q1_xb, q1_xa = y_both(q1_x)
    q1_o = shift(q1_b, "y", 1)
    q0, o0 = join_slots(one(match), kept0, home0, guest0)
    o0_b, o0_a = y_both(o0)
    q0_x = beside(q0)
    rows_b, rows_a = gather_near(rows)
    rows_s = chip_move(rows, SIBLING)
    q1_ox = shift(q1_xa, "y", -1)
    q0_b, q0_a = y_both(q0)
    o1_ox, o0_x = beside(o1_o), beside(o0)
    rows_o = shift(rows_b, "z", 1)
    rows_bs, rows_as = chip_move(rows_b, SIBLING), chip_move(rows_a, SIBLING)
    o0_o = shift(o0_a, "y", -1)
    o0_bx, o0_ax = beside(o0_b), beside(o0_a)
    q0_xb, q0_xa = y_both(q0_x)
    q0_o = shift(q0_b, "y", 1)
    rows_os = chip_move(rows_o, SIBLING)
    q0_ox = shift(q0_xa, "y", -1)
    o0_ox = beside(o0_o)
    entering = (rows, rows_b, rows_a, rows_o, rows_s, rows_bs, rows_as, rows_os)

    qkv_parts = [
        [q0, q0_x, q0_b, q0_xb, q0_a, q0_xa, q0_o, q0_ox],
        [q1, q1_x, q1_b, q1_xb, q1_a, q1_xa, q1_o, q1_ox],
    ]
    out_parts = [
        [o0, o0_x, o0_b, o0_bx, o0_a, o0_ax, o0_o, o0_ox],
        [o1, o1_x, o1_b, o1_bx, o1_a, o1_ax, o1_o, o1_ox],
    ]
    gain_bwd = (gain_one, gain_late)

    tables = [(k, all_cosines, all_sines, all_kept) for k in range(4)]

    late = one(jnp.where(a == 0, 1, 0))
    state, grad = keep[0], keep[1]
    fwd_in, fwd_at = entering, 0
    cotangent, cot_at = entering, 1
    stash_in = ((entering, 2), (entering, 3))
    sets = (qkv_parts, out_parts)
    gain_sum = []
    for tick in range(2):
        spans_fwd, spans_bwd = (([0], [1]), ([0, 1], [0, 1]))[tick]
        qkv_fwd, out_fwd = ([table[s] for s in spans_fwd] for table in sets)
        qkv_bwd, out_bwd = ([table[s] for s in spans_bwd] for table in sets)
        mine, other = layer_call("forward", fwd_in, fwd_at, tables[tick], late, qkv_fwd, out_fwd)
        stash_rows, stash_at = stash_in[tick]
        heads = layer_call("project", stash_rows, stash_at, tables[2 + tick], late, qkv_bwd, [])
        b_mine, b_other, gain_part = layer_call(
            "backward",
            cotangent,
            cot_at,
            tables[2 + tick],
            late,
            qkv_bwd,
            out_bwd,
            saved=heads,
            normed=stash_in[tick],
        )
        gain_sum.append(gain_part / gain_bwd[tick])
        order = across if tick == 0 else back
        pushed = scatter_rows(b_mine, b_other)
        grad = finish_backward(order, pushed, grad, keep[2 + tick], scale[2 + tick], gain_bwd[tick])
        state = finish_forward(order, scatter_rows(mine, other), state)
        if tick == 0:
            state = chip_move(state, ACROSS)
            grad = chip_move(grad, ACROSS)
            fwd_in, fwd_at = gather_rows(norm_rows(state, gain_late)), None
            cotangent, cot_at = gather_rows(grad), None

    state_out = chip_move(state, HOME)
    grad_out = chip_move(grad, HOME)
    on_first = jnp.where(a == 1, 1.0, 0.0)
    gain_rows = jnp.concatenate(
        [gain_sum[1] * on_first, gain_sum[0] + gain_sum[1] * (1.0 - on_first)], axis=0
    )
    gain_total = sum_gains(gain_rows)
    return (state_out[None], grad_out[None], gain_total[None])


def solution(mesh):
    grid = Mesh(mesh.devices.reshape(4, 2, 2, 2, 4), ("y", "xh", "xl", "s", "z"))
    dp = ("y", "xh", "xl")
    in_specs = (
        P("s", dp + ("z",), None),
        P("s", dp + ("z",), None),
        P("s", None, dp + ("z",), None),
        P("s", None, None),
        P("s", None, dp, "z"),
        P("s", None, dp, "z"),
        P("s", None, dp, "z"),
        P("s", None, "z", dp),
        P(None, dp, None),
        P(None, dp, None),
    )
    out_specs = (
        P("s", dp + ("z",), None),
        P("s", dp + ("z",), None),
        P("s", None, None),
    )

    return jax.shard_map(
        per_device, mesh=grid, in_specs=in_specs, out_specs=out_specs, check_vma=False
    )
```

```python
import math

import jax
import jax.numpy as jnp
from jax import lax
from jax.experimental import pallas as pl
from jax.experimental.pallas import tpu as pltpu
from jax.sharding import Mesh, PartitionSpec as P

HD = 128
ROPE_BASE = 1000000.0
BF = jnp.bfloat16
F32 = jnp.float32


CHIP = ("xh", "xl", "s")


def spot(xh, xl, core):
    return (xh * 2 + xl) * 2 + core


PLACES = [(xh, xl, core) for xh in (0, 1) for xl in (0, 1) for core in (0, 1)]
SIBLING = [(spot(a, l, c), spot(a, l, 1 - c)) for a, l, c in PLACES]
ACROSS = [(spot(a, l, c), spot(1 - a, 1 - l, c)) for a, l, c in PLACES]
OPPOSITE = [(spot(a, l, c), spot(1 - a, l, c)) for a, l, c in PLACES]
BESIDE = [(spot(a, l, c), spot(a, 1 - l, c)) for a, l, c in PLACES]
HOME = [
    (spot(a, l, c), spot(a, l, 1 - c) if c == a else spot(1 - a, 1 - l, c)) for a, l, c in PLACES
]
GUEST = [(spot(a, l, c), spot(1 - a, 1 - l, 1 - c)) for a, l, c in PLACES if c != a]


def chip_move(value, pairs):
    return lax.ppermute(value, CHIP, pairs)


def shift(value, axis, steps):
    count = lax.axis_size(axis)
    return lax.ppermute(value, axis, [(i, (i + steps) % count) for i in range(count)])


RING = (0, 3, 1, 2)
RING_BACK = (0, 2, 3, 1)


NEAR = (0, 3, 1, 2)
VM = pl.BlockSpec(memory_space=pltpu.VMEM)
SM = pl.BlockSpec(memory_space=pltpu.SMEM)
HB = pl.BlockSpec(memory_space=pltpu.HBM)
CHUNKS = 8


def shape(dims, kind=BF):
    return jax.ShapeDtypeStruct(dims, kind)


def kernel_call(body, outs, in_specs, scratch=(), flops=0, moved=0, out_spec=VM):
    return pl.pallas_call(
        body,
        out_shape=outs,
        in_specs=in_specs,
        out_specs=jax.tree.map(lambda unused: out_spec, outs),
        scratch_shapes=list(scratch),
        cost_estimate=pl.CostEstimate(flops=flops, bytes_accessed=moved, transcendentals=0),
        compiler_params=pltpu.CompilerParams(vmem_limit_bytes=67043328),
    )


def turned_dot(left, right):
    return lax.dot_general(left, right, (((1,), (1,)), ((), ())), preferred_element_type=F32)


def dot(left, right):
    return jnp.dot(left, right, preferred_element_type=F32)


def split_weights(a, w_query, w_key, w_value, w_out):
    block = w_query.shape[1]
    q_cols, k_cols, o_rows = w_query.shape[2] // 2, w_key.shape[2] // 2, w_out.shape[1] // 2
    wide = q_cols + 2 * k_cols + o_rows

    def body(a_ref, q_ref, k_ref, v_ref, o_ref, *outs):
        for span in range(2):
            for which in range(2):
                half = a_ref[0] if which == 0 else 1 - a_ref[0]
                out = outs[span * 2 + which]
                q_at = pl.multiple_of(half * q_cols, q_cols)
                k_at = pl.multiple_of(half * k_cols, k_cols)
                o_at = pl.multiple_of(half * o_rows, o_rows)
                out[:, :q_cols] = q_ref[span, :, pl.ds(q_at, q_cols)]
                out[:, q_cols : q_cols + k_cols] = k_ref[span, :, pl.ds(k_at, k_cols)]
                out[:, q_cols + k_cols : q_cols + 2 * k_cols] = v_ref[span, :, pl.ds(k_at, k_cols)]
                out[:, q_cols + 2 * k_cols :] = o_ref[span, pl.ds(o_at, o_rows), :].T

    outs = tuple(shape((block, wide)) for _ in range(4))
    return kernel_call(body, outs, [SM] + [VM] * 4, moved=10 << 20)(
        a, w_query, w_key, w_value, w_out
    )


def join_slots(match, kept, home, guest):
    block, wide = kept.shape
    cut = wide - wide * 2 // 5

    def body(match_ref, kept_ref, home_ref, guest_ref, qkv_ref, out_ref):
        def put(at, value_ref):
            qkv_ref[pl.ds(at, block), :] = value_ref[:, :cut]
            out_ref[pl.ds(at, block), :] = value_ref[:, cut:]

        @pl.when(match_ref[0] == 1)
        def own():
            put(0, kept_ref)
            put(block, home_ref)

        @pl.when(match_ref[0] == 0)
        def moved():
            put(0, home_ref)
            put(block, guest_ref)

    outs = (shape((2 * block, cut)), shape((2 * block, wide - cut)))
    return kernel_call(body, outs, [SM] + [VM] * 3, moved=3 << 20)(match, kept, home, guest)


def y_both(value):
    return shift(value, "y", 1), shift(value, "y", -1)


def beside(value):
    return chip_move(value, BESIDE)


def reorder(order_ref, width, block, take_from, put_to):
    for k in range(width // block):
        at = pl.multiple_of(order_ref[k] * block, block)
        put_to(k * block, take_from(at))


def start_rows(scalars, order, local, guest, gains, gains_sibling):
    kinds, rows, width = local.shape
    block = width // 16

    def body(s_ref, order_ref, local_ref, guest_ref, g_ref, h_ref, out, keep, scale, one_ref, late_ref, gain):
        match, a = s_ref[0] == 1, s_ref[1]

        def take_gain(at):
            return jnp.where(match, g_ref[:, pl.ds(at, block)], h_ref[:, pl.ds(at, block)])

        def put_gain(at, value):
            gain[:, at : at + block] = value.astype(F32)

        reorder(order_ref, width, block, take_gain, put_gain)
        late = jnp.where(a == 0, gain[1:2, :], gain[0:1, :])
        one_ref[...] = gain[1:2, :]
        late_ref[...] = late
        for kind in range(4):

            def take_rows(at):
                return jnp.where(
                    match, local_ref[kind, :, pl.ds(at, block)], guest_ref[kind, :, pl.ds(at, block)]
                )

            def put_rows(at, value):
                keep[kind, :, at : at + block] = value

            reorder(order_ref, width, block, take_rows, put_rows)
            value = keep[kind]
            if kind == 1:
                out[kind] = value
                continue
            value = value.astype(F32)
            by = lax.rsqrt(jnp.mean(value * value, axis=1, keepdims=True) + 1e-06)
            factor = (gain[0:1, :], None, gain[1:2, :], late)[kind]
            out[kind] = (value * by * factor).astype(BF)
            scale[kind] = jnp.broadcast_to(by, (rows, 128))

    outs = (
        shape((kinds, rows, width)),
        shape((kinds, rows, width)),
        shape((kinds, rows, 128), F32),
        shape((1, width), F32),
        shape((1, width), F32),
    )
    scratch = [pltpu.VMEM((2, width), F32)]
    return kernel_call(body, outs, [SM, SM] + [VM] * 4, scratch, moved=6 << 20)(
        scalars, order, local, guest, gains, gains_sibling
    )


def norm_rows(state, gain_row):
    def body(state_ref, gain_ref, out_ref):
        value = state_ref[...].astype(F32)
        by = lax.rsqrt(jnp.mean(value * value, axis=1, keepdims=True) + 1e-06)
        out_ref[...] = (value * by * gain_ref[...]).astype(BF)

    return kernel_call(body, shape(state.shape), [VM, VM], moved=1 << 19)(state, gain_row)


def gather_near(value):
    return shift(value, "z", 1), shift(value, "z", -1)


def gather_rows(value):
    near = gather_near(value)
    far = shift(near[1], "z", -1)
    parts = (value, *near, far)
    twins = tuple(chip_move(part, SIBLING) for part in parts[:3])
    return parts + twins + (chip_move(far, SIBLING),)


def scatter_rows(mine, other):
    came = chip_move(other, SIBLING)
    rows, width = mine.shape
    block = rows // 4

    def body(mine_ref, came_ref, own, one, two, three, left, right, wide, narrow, sems):
        loads = {}
        for k in (1, 2, 3, 0):
            at = pl.ds(k * block, block)
            loads[k] = (
                pltpu.make_async_copy(mine_ref.at[at], left.at[at], sems.at[k]),
                pltpu.make_async_copy(came_ref.at[at], right.at[at], sems.at[4 + k]),
            )
            for copy in loads[k]:
                copy.start()
        stores = []
        for k in (1, 2, 3, 0):
            for copy in loads[k]:
                copy.wait()
            at = pl.ds(k * block, block)
            total = left[at, :].astype(F32) + right[at, :].astype(F32)
            held = narrow.at[k - 1] if k else wide
            held[...] = total.astype(held.dtype)
            out = (own, one, two, three)[k]
            stores.append(pltpu.make_async_copy(held, out, sems.at[8 + k]))
            stores[-1].start()
        for copy in stores:
            copy.wait()

    outs = (shape((block, width), F32),) + (shape((block, width)),) * 3
    scratch = [pltpu.VMEM((rows, width), BF), pltpu.VMEM((rows, width), BF)]
    scratch += [pltpu.VMEM((block, width), F32), pltpu.VMEM((3, block, width), BF)]
    scratch += [pltpu.SemaphoreType.DMA((12,))]
    own, one, two, three = kernel_call(
        body, outs, [HB, HB], scratch, moved=4 << 20, out_spec=HB
    )(mine, came)
    return own, shift(one, "z", -1), shift(two, "z", 1), shift(three, "z", 2)


def finish_forward(order, parts, state):
    rows, width = state.shape
    block = width // 16

    def body(order_ref, own, one, two, three, state_ref, out_ref):
        def total(at):
            at = pl.ds(at, block)
            value = own[:, at] + one[:, at].astype(F32) + two[:, at].astype(F32)
            value = value + three[:, at].astype(F32) + state_ref[:, at].astype(F32)
            return value.astype(BF)

        def put(at, value):
            out_ref[:, at : at + block] = value

        reorder(order_ref, width, block, total, put)

    return kernel_call(body, shape((rows, width)), [SM] + [VM] * 5, moved=2 << 20)(
        order, *parts, state
    )


def finish_backward(order, parts, grad, kept, scale, gain_row):
    rows, width = grad.shape
    block = width // 16

    def body(order_ref, own, one, two, three, grad_ref, kept_ref, scale_ref, gain_ref, out_ref, hold):
        by = scale_ref[:, :1]
        pushed = own[...] + one[...].astype(F32) + two[...].astype(F32) + three[...].astype(F32)
        pushed = pushed * gain_ref[...]
        value = kept_ref[...].astype(F32)
        lean = jnp.mean(value * pushed, axis=1, keepdims=True) * (by * by * by)
        hold[...] = (grad_ref[...].astype(F32) + pushed * by - value * lean).astype(BF)

        def put(at, piece):
            out_ref[:, at : at + block] = piece

        reorder(order_ref, width, block, lambda at: hold[:, pl.ds(at, block)], put)

    return kernel_call(
        body,
        shape((rows, width)),
        [SM] + [VM] * 8,
        scratch=[pltpu.VMEM((rows, width), BF)],
        moved=2 << 20,
    )(order, *parts, grad, kept, scale, gain_row)


def stack_copies(parts, target, sems, at):
    copies, row = [], 0
    for k, part in enumerate(parts):
        rows = part.shape[0]
        copies.append(pltpu.make_async_copy(part, target.at[pl.ds(row, rows)], sems.at[at + k]))
        row += rows
    return copies


def start_copies(pick_ref, groups):
    if len(groups) == 1:
        for copy in groups[0]:
            copy.start()
        return
    for span, copies in enumerate(groups):

        @pl.when(pick_ref[0] == span)
        def begin():
            for copy in copies:
                copy.start()


def turn_heads(projected, cosine, sine, heads, back=False):
    outs = []
    for h in range(heads):
        v = projected[:, h * HD : (h + 1) * HD]
        turned = pltpu.roll(v, HD // 2, 1) * sine
        outs.append(v * cosine - turned if back else v * cosine + turned)
    return outs


def project(rows_ref, qkv, copies, cosine, sine, heads_ref, total):
    width = rows_ref.shape[1]
    step = width // CHUNKS
    total[...] = jnp.zeros_like(total)
    for k in range(CHUNKS):
        copies[k].wait()
        at = pl.ds(k * step, step)
        total[...] += dot(rows_ref[:, at], qkv[at, :])
    count = total.shape[1] // HD
    turned = turn_heads(total, cosine[...], sine[...], count - 1)
    for h in range(count - 1):
        heads_ref[:, h * HD : (h + 1) * HD] = turned[h].astype(BF)
    heads_ref[:, (count - 1) * HD :] = total[:, (count - 1) * HD :].astype(BF)


def stack_query(ref, b, rows, groups):
    return jnp.concatenate(
        [ref[b * rows : (b + 1) * rows, g * HD : (g + 1) * HD] for g in range(groups)], axis=0
    )


def probabilities(query, key, keep):
    scores = turned_dot(query, key) * (1.0 / math.sqrt(HD))
    exponents = jnp.exp(jnp.where(keep > 0.0, scores, -1e30))
    return exponents / jnp.sum(exponents, axis=-1, keepdims=True)


def load_rows(index, parts, rows_ref, sems, first):
    rows = rows_ref.shape[0] // len(parts)
    return [
        pltpu.make_async_copy(
            src if index is None else src.at[index],
            rows_ref.at[pl.ds(k * rows, rows)],
            sems.at[first + k],
        )
        for k, src in enumerate(parts)
    ]


def layer_call(kind, rows_in, index, tables, pick, qkv_sets, out_sets, saved=None, normed=None):
    n_rows = len(rows_in)
    width = rows_in[0].shape[-1]
    rows = n_rows * rows_in[0].shape[-2]
    half = rows // 2
    which, tables = tables[0], tables[1:]
    spans = len(qkv_sets)
    q_wide = qkv_sets[0][0].shape[1]
    o_wide = out_sets[0][0].shape[1] if out_sets else 0
    groups = q_wide // HD - 2
    n_qkv = len(qkv_sets[0])
    n_out = len(out_sets[0]) if out_sets else 0
    step = width // CHUNKS

    def body(*refs):
        refs = list(refs)
        pick_ref, row_refs = refs[0], refs[1 : 1 + n_rows]
        table_refs, refs = refs[1 + n_rows : 4 + n_rows], refs[4 + n_rows :]
        qkv_refs = [refs[s * n_qkv : (s + 1) * n_qkv] for s in range(spans)]
        refs = refs[spans * n_qkv :]
        out_refs = [refs[s * n_out : (s + 1) * n_out] for s in range(spans)]
        refs = refs[spans * n_out :]
        if kind == "backward":
            heads, normed_refs = refs[0], refs[1 : 1 + n_rows]
            refs = refs[1 + n_rows :]
        n_results = {"forward": 2, "project": 1, "backward": 3}[kind]
        results, refs = refs[:n_results], refs[n_results:]
        rows_ref, qkv, total, sems, cosine, sine, keep = refs[:7]
        refs = refs[7:]
        row_copies = load_rows(index, row_refs, rows_ref, sems, 0)
        table_copies = [
            pltpu.make_async_copy(src.at[which], dst, sems.at[n_rows + k])
            for k, (src, dst) in enumerate(zip(table_refs, (cosine, sine, keep)))
        ]
        sem_more, sem_qkv = n_rows + 3, 2 * n_rows + 3
        qkv_copies = [stack_copies(parts, qkv, sems, sem_qkv) for parts in qkv_refs]
        if n_out:
            out, mixed = refs[:2]
            out_copies = [stack_copies(parts, out, sems, sem_qkv + n_qkv) for parts in out_refs]
        for copy in row_copies + table_copies:
            copy.start()
        if kind == "backward":
            start_copies(pick_ref, out_copies)
            start_copies(pick_ref, qkv_copies)
            d_heads, normed_ref = refs[2:]
            more = load_rows(normed[1], normed_refs, normed_ref, sems, sem_more)
            for copy in more:
                copy.start()
        else:
            start_copies(pick_ref, qkv_copies)
            if n_out:
                start_copies(pick_ref, out_copies)
        for copy in row_copies + table_copies:
            copy.wait()

        if kind == "project":
            project(rows_ref, qkv, qkv_copies[0], cosine, sine, results[0], total)
            return

        if kind == "forward":
            heads = refs[2]
            project(rows_ref, qkv, qkv_copies[0], cosine, sine, heads, total)
            for b in range(2):
                at = slice(b * half, (b + 1) * half)
                query = stack_query(heads, b, half, groups)
                kept = jnp.concatenate([keep[at, :]] * groups, axis=0)
                probs = probabilities(query, heads[at, groups * HD : (groups + 1) * HD], kept)
                got = dot(probs.astype(BF), heads[at, (groups + 1) * HD :]).astype(BF)
                for g in range(groups):
                    mixed[at, g * HD : (g + 1) * HD] = got[g * half : (g + 1) * half]
            for copy in out_copies[0]:
                copy.wait()

            def give(k, carry):
                at = pl.ds(pl.multiple_of(k * step, step), step)
                term = turned_dot(mixed[...], out[at, :]).astype(BF)
                results[0][:, at] = term[:half]
                results[1][:, at] = term[half:]
                return carry

            lax.fori_loop(0, CHUNKS, give, 0)
            return

        total[:, :o_wide] = jnp.zeros((rows, o_wide), F32)
        for k in range(CHUNKS):
            out_copies[0][k].wait()
            at = pl.ds(k * step, step)
            total[:, :o_wide] += dot(rows_ref[:, at], out[at, :])
        mixed[...] = total[:, :o_wide].astype(BF)
        for b in range(2):
            at = slice(b * half, (b + 1) * half)
            query = stack_query(heads, b, half, groups)
            push = stack_query(mixed, b, half, groups)
            key = heads[at, groups * HD : (groups + 1) * HD]
            value = heads[at, (groups + 1) * HD :]
            kept = jnp.concatenate([keep[at, :]] * groups, axis=0)
            probs = probabilities(query, key, kept)
            d_probs = turned_dot(push, value)
            centre = jnp.sum(d_probs * probs, axis=-1, keepdims=True)
            d_scores = (probs * (d_probs - centre) * (1.0 / math.sqrt(HD))).astype(BF)
            over_rows = (((0,), (0,)), ((), ()))
            d_value = lax.dot_general(probs.astype(BF), push, over_rows, preferred_element_type=F32)
            d_key = lax.dot_general(d_scores, query, over_rows, preferred_element_type=F32)
            d_query = dot(d_scores, key)
            c, s = cosine[at, :], sine[at, :]
            for g in range(groups):
                piece = d_query[g * half : (g + 1) * half]
                d_heads[at, g * HD : (g + 1) * HD] = turn_heads(piece, c, s, 1, True)[0].astype(BF)
            d_heads[at, groups * HD : (groups + 1) * HD] = turn_heads(d_key, c, s, 1, True)[0].astype(BF)
            d_heads[at, (groups + 1) * HD :] = d_value.astype(BF)
        for copy in qkv_copies[0]:
            copy.wait()
        for copy in more:
            copy.wait()

        def give_back(k, carry):
            at = pl.ds(pl.multiple_of(k * step, step), step)
            term = turned_dot(d_heads[...], qkv[at, :])
            results[2][:, at] = jnp.sum(
                term * normed_ref[:, at].astype(F32), axis=0, keepdims=True
            )
            term = term.astype(BF)
            results[0][:, at] = term[:half]
            results[1][:, at] = term[half:]
            return carry

        lax.fori_loop(0, CHUNKS, give_back, 0)

    outs = {
        "forward": (shape((half, width)),) * 2,
        "project": shape((rows, q_wide)),
        "backward": (shape((half, width)),) * 2 + (shape((1, width), F32),),
    }[kind]
    scratch = [
        pltpu.VMEM((rows, width), BF),
        pltpu.VMEM((width, q_wide), BF),
        pltpu.VMEM((rows, q_wide), F32),
        pltpu.SemaphoreType.DMA((2 * n_rows + 3 + n_qkv + n_out,)),
    ] + [pltpu.VMEM((rows, table.shape[-1]), F32) for table in tables]
    if n_out:
        scratch += [pltpu.VMEM((width, o_wide), BF), pltpu.VMEM((rows, o_wide), BF)]
        scratch += [pltpu.VMEM((rows, q_wide), BF)]
    args = [pick, *rows_in, *tables]
    specs = [SM] + [HB] * (n_rows + 3)
    for parts in list(qkv_sets) + list(out_sets):
        args += parts
        specs += [HB] * len(parts)
    if kind == "backward":
        args += [saved, *normed[0]]
        specs += [VM] + [HB] * n_rows
        scratch += [pltpu.VMEM((rows, width), BF)]
    flops = 2 * rows * width * (q_wide + o_wide)
    return kernel_call(body, outs, specs, scratch, flops=flops, moved=14 << 20)(*args)


def all_tables(ids, z):
    count = ids.shape[-1]
    block = count // 4
    row = jnp.arange(count, dtype=jnp.int32)
    own = (z + jnp.array(RING, jnp.int32)) % 4
    index = (own[:, None] * block + jnp.arange(block, dtype=jnp.int32)).reshape(count)
    picked = (index[:, None] == row).astype(F32)
    ids = ids.astype(F32)
    relative = jnp.sum(ids[:, :, None, :] * picked, axis=-1)
    starts = jnp.sum((ids[:, :, None, :] < relative[:, :, :, None]).astype(F32), axis=-1)
    positions = index.astype(F32) - starts
    halfway = HD // 2
    frequency = jnp.exp(jnp.arange(halfway, dtype=F32) * (-2.0 * math.log(ROPE_BASE) / HD))
    angles = positions[..., None] * frequency
    cosine, sine = jnp.cos(angles), jnp.sin(angles)
    cosine = jnp.concatenate([cosine, cosine], axis=-1).reshape(4, 2 * count, HD)
    sine = jnp.concatenate([-sine, sine], axis=-1).reshape(4, 2 * count, HD)
    kept = (relative[..., :, None] == relative[..., None, :]) & (index[:, None] >= index[None, :])
    return cosine, sine, kept.astype(F32).reshape(4, 2 * count, count)


def sum_gains(part):
    order = chip_order()[1]
    part = part + shift(part, "z", 2)
    part = part + shift(part, "z", 1)
    part = part + chip_move(part, SIBLING)
    block = part.shape[1] // 16
    part = jnp.take(part.reshape(2, 16, block), order, axis=1).reshape(part.shape)
    part = part + shift(part, "y", 2)
    part = part + shift(part, "y", 1)
    same = part + chip_move(part, BESIDE)
    other = chip_move(part, ACROSS) + chip_move(part, OPPOSITE)
    return jnp.where(lax.axis_index("s") == lax.axis_index("xh"), same, other)


def chip_order():
    y, x = lax.axis_index("y"), lax.axis_index("xh") * 2 + lax.axis_index("xl")
    ring, near = jnp.array(RING, jnp.int32), jnp.array(NEAR, jnp.int32)
    place = ((y + ring) % 4)[:, None] * 4 + jnp.bitwise_xor(x, near)[None, :]
    every = jnp.arange(4, dtype=jnp.int32)
    ring_back, near_back = jnp.array(RING_BACK, jnp.int32), jnp.array(RING_BACK, jnp.int32)
    back_y = jnp.sum(
        jnp.where(((every - y) % 4)[:, None] == every[None, :], ring_back[None, :], 0), axis=1
    )
    back_x = jnp.sum(
        jnp.where(jnp.bitwise_xor(every, x)[:, None] == every[None, :], near_back[None, :], 0),
        axis=1,
    )
    back = back_y[:, None] * 4 + back_x[None, :]
    return place.reshape(16).astype(jnp.int32), back.reshape(16).astype(jnp.int32)


def per_device(
    fwd_state, bwd_state, stash, gains, w_query, w_key, w_value, w_out, fwd_segments, bwd_segments
):
    a, core, z = lax.axis_index("xh"), lax.axis_index("s"), lax.axis_index("z")
    match = core == a
    one = lambda v: v.astype(jnp.int32).reshape(1)
    place, back = chip_order()
    across = jnp.array([4 * y + (x ^ 1) for y in range(4) for x in range(4)], jnp.int32)

    kept0, home0, kept1, home1 = split_weights(
        one(a), w_query[0], w_key[0], w_value[0], w_out[0]
    )
    home1 = chip_move(home1, HOME)
    guest1 = chip_move(kept1, GUEST)
    local = jnp.concatenate([fwd_state, bwd_state, stash[0]], axis=0)
    own_ids = jnp.stack([fwd_segments[:, 0], bwd_segments[:, 0]])
    gains_sibling = chip_move(gains[0], SIBLING)
    partner_ids = chip_move(own_ids, ACROSS)
    q1, o1 = join_slots(one(match), kept1, home1, guest1)

    q1_x, o1_x = beside(q1), beside(o1)
    q1_b, q1_a = y_both(q1)
    o1_b, o1_a = y_both(o1)
    guest_rows = chip_move(local, GUEST)
    home0 = chip_move(home0, HOME)
    guest0 = chip_move(kept0, GUEST)
    ids = jnp.stack(
        [jnp.where(match, own_ids, partner_ids), jnp.where(match, partner_ids, own_ids)],
        axis=2,
    )
    ids = jnp.where(a == 0, ids, ids[:, ::-1]).reshape(4, 2, -1)
    all_cosines, all_sines, all_kept = lax.optimization_barrier(all_tables(ids, z))
    scalars = jnp.stack([match.astype(jnp.int32), a.astype(jnp.int32)])
    rows, keep, scale, gain_one, gain_late = start_rows(
        scalars, place, local, guest_rows, gains[0], gains_sibling
    )
    o1_o = shift(o1_b, "y", 1)
    o1_bx, o1_ax = beside(o1_b), beside(o1_a)
    q1_xb, q1_xa = y_both(q1_x)
    q1_o = shift(q1_b, "y", 1)
    q0, o0 = join_slots(one(match), kept0, home0, guest0)
    o0_b, o0_a = y_both(o0)
    q0_x = beside(q0)
    rows_b, rows_a = gather_near(rows)
    rows_s = chip_move(rows, SIBLING)
    q1_ox = shift(q1_xa, "y", -1)
    q0_b, q0_a = y_both(q0)
    o1_ox, o0_x = beside(o1_o), beside(o0)
    rows_o = shift(rows_b, "z", 1)
    rows_bs, rows_as = chip_move(rows_b, SIBLING), chip_move(rows_a, SIBLING)
    o0_o = shift(o0_a, "y", -1)
    o0_bx, o0_ax = beside(o0_b), beside(o0_a)
    q0_xb, q0_xa = y_both(q0_x)
    q0_o = shift(q0_b, "y", 1)
    rows_os = chip_move(rows_o, SIBLING)
    q0_ox = shift(q0_xa, "y", -1)
    o0_ox = beside(o0_o)
    entering = (rows, rows_b, rows_a, rows_o, rows_s, rows_bs, rows_as, rows_os)

    qkv_parts = [
        [q0, q0_x, q0_b, q0_xb, q0_a, q0_xa, q0_o, q0_ox],
        [q1, q1_x, q1_b, q1_xb, q1_a, q1_xa, q1_o, q1_ox],
    ]
    out_parts = [
        [o0, o0_x, o0_b, o0_bx, o0_a, o0_ax, o0_o, o0_ox],
        [o1, o1_x, o1_b, o1_bx, o1_a, o1_ax, o1_o, o1_ox],
    ]
    gain_bwd = (gain_one, gain_late)

    tables = [(k, all_cosines, all_sines, all_kept) for k in range(4)]

    late = one(jnp.where(a == 0, 1, 0))
    state, grad = keep[0], keep[1]
    fwd_in, fwd_at = entering, 0
    cotangent, cot_at = entering, 1
    stash_in = ((entering, 2), (entering, 3))
    sets = (qkv_parts, out_parts)
    gain_sum = []
    for tick in range(2):
        spans_fwd, spans_bwd = (([0], [1]), ([0, 1], [0, 1]))[tick]
        qkv_fwd, out_fwd = ([table[s] for s in spans_fwd] for table in sets)
        qkv_bwd, out_bwd = ([table[s] for s in spans_bwd] for table in sets)
        mine, other = layer_call("forward", fwd_in, fwd_at, tables[tick], late, qkv_fwd, out_fwd)
        stash_rows, stash_at = stash_in[tick]
        heads = layer_call("project", stash_rows, stash_at, tables[2 + tick], late, qkv_bwd, [])
        b_mine, b_other, gain_part = layer_call(
            "backward",
            cotangent,
            cot_at,
            tables[2 + tick],
            late,
            qkv_bwd,
            out_bwd,
            saved=heads,
            normed=stash_in[tick],
        )
        gain_sum.append(gain_part / gain_bwd[tick])
        order = across if tick == 0 else back
        pushed = scatter_rows(b_mine, b_other)
        grad = finish_backward(order, pushed, grad, keep[2 + tick], scale[2 + tick], gain_bwd[tick])
        state = finish_forward(order, scatter_rows(mine, other), state)
        if tick == 0:
            state = chip_move(state, ACROSS)
            grad = chip_move(grad, ACROSS)
            fwd_in, fwd_at = gather_rows(norm_rows(state, gain_late)), None
            cotangent, cot_at = gather_rows(grad), None

    state_out = chip_move(state, HOME)
    grad_out = chip_move(grad, HOME)
    on_first = jnp.where(a == 1, 1.0, 0.0)
    gain_rows = jnp.concatenate(
        [gain_sum[1] * on_first, gain_sum[0] + gain_sum[1] * (1.0 - on_first)], axis=0
    )
    gain_total = sum_gains(gain_rows)
    return (state_out[None], grad_out[None], gain_total[None])


def solution(mesh):
    grid = Mesh(mesh.devices.reshape(4, 2, 2, 2, 4), ("y", "xh", "xl", "s", "z"))
    dp = ("y", "xh", "xl")
    in_specs = (
        P("s", dp + ("z",), None),
        P("s", dp + ("z",), None),
        P("s", None, dp + ("z",), None),
        P("s", None, None),
        P("s", None, dp, "z"),
        P("s", None, dp, "z"),
        P("s", None, dp, "z"),
        P("s", None, "z", dp),
        P(None, dp, None),
        P(None, dp, None),
    )
    out_specs = (
        P("s", dp + ("z",), None),
        P("s", dp + ("z",), None),
        P("s", None, None),
    )

    return jax.shard_map(
        per_device, mesh=grid, in_specs=in_specs, out_specs=out_specs, check_vma=False
    )
```

```python
import math

import jax
import jax.numpy as jnp
from jax import lax
from jax.experimental import pallas as pl
from jax.experimental.pallas import tpu as pltpu
from jax.sharding import Mesh, PartitionSpec as P

HD = 128
ROPE_BASE = 1000000.0
BF = jnp.bfloat16
F32 = jnp.float32


CHIP = ("xh", "xl", "s")


def spot(xh, xl, core):
    return (xh * 2 + xl) * 2 + core


PLACES = [(xh, xl, core) for xh in (0, 1) for xl in (0, 1) for core in (0, 1)]
SIBLING = [(spot(a, l, c), spot(a, l, 1 - c)) for a, l, c in PLACES]
ACROSS = [(spot(a, l, c), spot(1 - a, 1 - l, c)) for a, l, c in PLACES]
BESIDE = [(spot(a, l, c), spot(a, 1 - l, c)) for a, l, c in PLACES]
HOME = [
    (spot(a, l, c), spot(a, l, 1 - c) if c == a else spot(1 - a, 1 - l, c)) for a, l, c in PLACES
]
GUEST = [(spot(a, l, c), spot(1 - a, 1 - l, 1 - c)) for a, l, c in PLACES if c != a]


def chip_move(value, pairs):
    return lax.ppermute(value, CHIP, pairs)


def shift(value, axis, steps):
    count = lax.axis_size(axis)
    return lax.ppermute(value, axis, [(i, (i + steps) % count) for i in range(count)])


RING = (0, 3, 1, 2)
RING_BACK = (0, 2, 3, 1)


NEAR = (0, 3, 1, 2)
VM = pl.BlockSpec(memory_space=pltpu.VMEM)
SM = pl.BlockSpec(memory_space=pltpu.SMEM)
HB = pl.BlockSpec(memory_space=pltpu.HBM)
CHUNKS = 8


def shape(dims, kind=BF):
    return jax.ShapeDtypeStruct(dims, kind)


def kernel_call(body, outs, in_specs, scratch=(), flops=0, moved=0, out_spec=VM):
    return pl.pallas_call(
        body,
        out_shape=outs,
        in_specs=in_specs,
        out_specs=jax.tree.map(lambda unused: out_spec, outs),
        scratch_shapes=list(scratch),
        cost_estimate=pl.CostEstimate(flops=flops, bytes_accessed=moved, transcendentals=0),
        compiler_params=pltpu.CompilerParams(vmem_limit_bytes=67043328),
    )


def turned_dot(left, right):
    return lax.dot_general(left, right, (((1,), (1,)), ((), ())), preferred_element_type=F32)


def dot(left, right):
    return jnp.dot(left, right, preferred_element_type=F32)


def split_weights(a, w_query, w_key, w_value, w_out):
    block = w_query.shape[1]
    q_cols, k_cols, o_rows = w_query.shape[2] // 2, w_key.shape[2] // 2, w_out.shape[1] // 2
    wide = q_cols + 2 * k_cols + o_rows

    def body(a_ref, q_ref, k_ref, v_ref, o_ref, *outs):
        for span in range(2):
            for which in range(2):
                half = a_ref[0] if which == 0 else 1 - a_ref[0]
                out = outs[span * 2 + which]
                q_at = pl.multiple_of(half * q_cols, q_cols)
                k_at = pl.multiple_of(half * k_cols, k_cols)
                o_at = pl.multiple_of(half * o_rows, o_rows)
                out[:, :q_cols] = q_ref[span, :, pl.ds(q_at, q_cols)]
                out[:, q_cols : q_cols + k_cols] = k_ref[span, :, pl.ds(k_at, k_cols)]
                out[:, q_cols + k_cols : q_cols + 2 * k_cols] = v_ref[span, :, pl.ds(k_at, k_cols)]
                out[:, q_cols + 2 * k_cols :] = o_ref[span, pl.ds(o_at, o_rows), :].T

    outs = tuple(shape((block, wide)) for _ in range(4))
    return kernel_call(body, outs, [SM] + [VM] * 4, moved=10 << 20)(
        a, w_query, w_key, w_value, w_out
    )


def join_slots(match, kept, home, guest):
    block, wide = kept.shape
    cut = wide - wide * 2 // 5

    def body(match_ref, kept_ref, home_ref, guest_ref, qkv_ref, out_ref):
        def put(at, value_ref):
            qkv_ref[pl.ds(at, block), :] = value_ref[:, :cut]
            out_ref[pl.ds(at, block), :] = value_ref[:, cut:]

        @pl.when(match_ref[0] == 1)
        def own():
            put(0, kept_ref)
            put(block, home_ref)

        @pl.when(match_ref[0] == 0)
        def moved():
            put(0, home_ref)
            put(block, guest_ref)

    outs = (shape((2 * block, cut)), shape((2 * block, wide - cut)))
    return kernel_call(body, outs, [SM] + [VM] * 3, moved=3 << 20)(match, kept, home, guest)


def y_both(value):
    return shift(value, "y", 1), shift(value, "y", -1)


def beside(value):
    return chip_move(value, BESIDE)


def reorder(order_ref, width, block, take_from, put_to):
    for k in range(width // block):
        at = pl.multiple_of(order_ref[k] * block, block)
        put_to(k * block, take_from(at))


def start_rows(scalars, order, local, guest, gains, gains_sibling):
    kinds, rows, width = local.shape
    block = width // 16

    def body(s_ref, order_ref, local_ref, guest_ref, g_ref, h_ref, out, *outs):
        keep, scale, (one_ref, late_ref, gain) = outs[:4], (None, None) + outs[4:6], outs[6:]
        match, a = s_ref[0] == 1, s_ref[1]

        def take_gain(at):
            return jnp.where(match, g_ref[:, pl.ds(at, block)], h_ref[:, pl.ds(at, block)])

        def put_gain(at, value):
            gain[:, at : at + block] = value.astype(F32)

        reorder(order_ref, width, block, take_gain, put_gain)
        late = jnp.where(a == 0, gain[1:2, :], gain[0:1, :])
        one_ref[...] = gain[1:2, :]
        late_ref[...] = late
        for kind in range(4):

            def take_rows(at):
                return jnp.where(
                    match, local_ref[kind, :, pl.ds(at, block)], guest_ref[kind, :, pl.ds(at, block)]
                )

            def put_rows(at, value):
                keep[kind][:, at : at + block] = value

            reorder(order_ref, width, block, take_rows, put_rows)
            value = keep[kind][...]
            if kind == 1:
                out[kind] = value
                continue
            value = value.astype(F32)
            by = lax.rsqrt(jnp.mean(value * value, axis=1, keepdims=True) + 1e-06)
            factor = (gain[0:1, :], None, gain[1:2, :], late)[kind]
            out[kind] = (value * by * factor).astype(BF)
            if kind > 1:
                scale[kind][...] = jnp.broadcast_to(by, (rows, 128))

    outs = (shape((kinds, rows, width)),) + (shape((rows, width)),) * kinds
    outs += (shape((rows, 128), F32),) * 2 + (shape((1, width), F32),) * 2
    scratch = [pltpu.VMEM((2, width), F32)]
    return kernel_call(body, outs, [SM, SM] + [VM] * 4, scratch, moved=6 << 20)(
        scalars, order, local, guest, gains, gains_sibling
    )


def norm_rows(state, gain_row):
    def body(state_ref, gain_ref, out_ref):
        value = state_ref[...].astype(F32)
        by = lax.rsqrt(jnp.mean(value * value, axis=1, keepdims=True) + 1e-06)
        out_ref[...] = (value * by * gain_ref[...]).astype(BF)

    return kernel_call(body, shape(state.shape), [VM, VM], moved=1 << 19)(state, gain_row)


def gather_near(value):
    return shift(value, "z", 1), shift(value, "z", -1)


def gather_rows(value):
    near = gather_near(value)
    far = shift(near[1], "z", -1)
    parts = (value, *near, far)
    twins = tuple(chip_move(part, SIBLING) for part in parts[:3])
    return parts + twins + (chip_move(far, SIBLING),)


def scatter_rows(mine, other):
    came = chip_move(other, SIBLING)
    rows, width = mine.shape
    block = rows // 4

    def body(mine_ref, came_ref, own, one, two, three, left, right, wide, narrow, sems):
        loads = {}
        for k in (1, 2, 3, 0):
            at = pl.ds(k * block, block)
            loads[k] = (
                pltpu.make_async_copy(mine_ref.at[at], left.at[at], sems.at[k]),
                pltpu.make_async_copy(came_ref.at[at], right.at[at], sems.at[4 + k]),
            )
            for copy in loads[k]:
                copy.start()
        stores = []
        for k in (1, 2, 3, 0):
            for copy in loads[k]:
                copy.wait()
            at = pl.ds(k * block, block)
            total = left[at, :].astype(F32) + right[at, :].astype(F32)
            held = narrow.at[k - 1] if k else wide
            held[...] = total.astype(held.dtype)
            out = (own, one, two, three)[k]
            stores.append(pltpu.make_async_copy(held, out, sems.at[8 + k]))
            stores[-1].start()
        for copy in stores:
            copy.wait()

    outs = (shape((block, width), F32),) + (shape((block, width)),) * 3
    scratch = [pltpu.VMEM((rows, width), BF), pltpu.VMEM((rows, width), BF)]
    scratch += [pltpu.VMEM((block, width), F32), pltpu.VMEM((3, block, width), BF)]
    scratch += [pltpu.SemaphoreType.DMA((12,))]
    own, one, two, three = kernel_call(
        body, outs, [HB, HB], scratch, moved=4 << 20, out_spec=HB
    )(mine, came)
    return own, shift(one, "z", -1), shift(two, "z", 1), shift(three, "z", 2)


def finish_forward(order, parts, state):
    rows, width = state.shape
    block = width // 16

    def body(order_ref, own, one, two, three, state_ref, out_ref):
        def total(at):
            at = pl.ds(at, block)
            value = own[:, at] + one[:, at].astype(F32) + two[:, at].astype(F32)
            value = value + three[:, at].astype(F32) + state_ref[:, at].astype(F32)
            return value.astype(BF)

        def put(at, value):
            out_ref[:, at : at + block] = value

        reorder(order_ref, width, block, total, put)

    return kernel_call(body, shape((rows, width)), [SM] + [VM] * 5, moved=2 << 20)(
        order, *parts, state
    )


def finish_backward(order, parts, grad, kept, scale, gain_row):
    rows, width = grad.shape
    block = width // 16

    def body(order_ref, own, one, two, three, grad_ref, kept_ref, scale_ref, gain_ref, out_ref, hold):
        by = scale_ref[:, :1]
        pushed = own[...] + one[...].astype(F32) + two[...].astype(F32) + three[...].astype(F32)
        pushed = pushed * gain_ref[...]
        value = kept_ref[...].astype(F32)
        lean = jnp.mean(value * pushed, axis=1, keepdims=True) * (by * by * by)
        hold[...] = (grad_ref[...].astype(F32) + pushed * by - value * lean).astype(BF)

        def put(at, piece):
            out_ref[:, at : at + block] = piece

        reorder(order_ref, width, block, lambda at: hold[:, pl.ds(at, block)], put)

    return kernel_call(
        body,
        shape((rows, width)),
        [SM] + [VM] * 8,
        scratch=[pltpu.VMEM((rows, width), BF)],
        moved=2 << 20,
    )(order, *parts, grad, kept, scale, gain_row)


def stack_copies(parts, target, sems, at):
    copies, row = [], 0
    for k, part in enumerate(parts):
        rows = part.shape[0]
        copies.append(pltpu.make_async_copy(part, target.at[pl.ds(row, rows)], sems.at[at + k]))
        row += rows
    return copies


def start_copies(pick_ref, groups):
    if len(groups) == 1:
        for copy in groups[0]:
            copy.start()
        return
    for span, copies in enumerate(groups):

        @pl.when(pick_ref[0] == span)
        def begin():
            for copy in copies:
                copy.start()


def turn_heads(projected, cosine, sine, heads, back=False):
    outs = []
    for h in range(heads):
        v = projected[:, h * HD : (h + 1) * HD]
        turned = pltpu.roll(v, HD // 2, 1) * sine
        outs.append(v * cosine - turned if back else v * cosine + turned)
    return outs


def project(rows_ref, qkv, copies, cosine, sine, heads_ref, total):
    width = rows_ref.shape[1]
    step = width // CHUNKS
    total[...] = jnp.zeros_like(total)
    for k in range(CHUNKS):
        copies[k].wait()
        at = pl.ds(k * step, step)
        total[...] += dot(rows_ref[:, at], qkv[at, :])
    count = total.shape[1] // HD
    turned = turn_heads(total, cosine[...], sine[...], count - 1)
    for h in range(count - 1):
        heads_ref[:, h * HD : (h + 1) * HD] = turned[h].astype(BF)
    heads_ref[:, (count - 1) * HD :] = total[:, (count - 1) * HD :].astype(BF)


def stack_query(ref, b, rows, groups):
    return jnp.concatenate(
        [ref[b * rows : (b + 1) * rows, g * HD : (g + 1) * HD] for g in range(groups)], axis=0
    )


def probabilities(query, key, keep):
    scores = turned_dot(query, key) * (1.0 / math.sqrt(HD))
    exponents = jnp.exp(jnp.where(keep > 0.0, scores, -1e30))
    return exponents / jnp.sum(exponents, axis=-1, keepdims=True)


def load_rows(index, parts, rows_ref, sems, first):
    rows = rows_ref.shape[0] // len(parts)
    return [
        pltpu.make_async_copy(
            src if index is None else src.at[index],
            rows_ref.at[pl.ds(k * rows, rows)],
            sems.at[first + k],
        )
        for k, src in enumerate(parts)
    ]


def layer_call(kind, rows_in, index, tables, pick, qkv_sets, out_sets, saved=None, normed=None):
    n_rows = len(rows_in)
    width = rows_in[0].shape[-1]
    rows = n_rows * rows_in[0].shape[-2]
    half = rows // 2
    which, tables = tables[0], tables[1:]
    spans = len(qkv_sets)
    q_wide = qkv_sets[0][0].shape[1]
    o_wide = out_sets[0][0].shape[1] if out_sets else 0
    groups = q_wide // HD - 2
    n_qkv = len(qkv_sets[0])
    n_out = len(out_sets[0]) if out_sets else 0
    step = width // CHUNKS

    def body(*refs):
        refs = list(refs)
        pick_ref, row_refs = refs[0], refs[1 : 1 + n_rows]
        table_refs, refs = refs[1 + n_rows : 4 + n_rows], refs[4 + n_rows :]
        qkv_refs = [refs[s * n_qkv : (s + 1) * n_qkv] for s in range(spans)]
        refs = refs[spans * n_qkv :]
        out_refs = [refs[s * n_out : (s + 1) * n_out] for s in range(spans)]
        refs = refs[spans * n_out :]
        if kind == "backward":
            heads, normed_refs = refs[0], refs[1 : 1 + n_rows]
            refs = refs[1 + n_rows :]
        n_results = {"forward": 2, "project": 1, "backward": 3}[kind]
        results, refs = refs[:n_results], refs[n_results:]
        rows_ref, qkv, total, sems, cosine, sine, keep = refs[:7]
        refs = refs[7:]
        row_copies = load_rows(index, row_refs, rows_ref, sems, 0)
        table_copies = [
            pltpu.make_async_copy(src.at[which], dst, sems.at[n_rows + k])
            for k, (src, dst) in enumerate(zip(table_refs, (cosine, sine, keep)))
        ]
        sem_more, sem_qkv = n_rows + 3, 2 * n_rows + 3
        qkv_copies = [stack_copies(parts, qkv, sems, sem_qkv) for parts in qkv_refs]
        if n_out:
            out, mixed = refs[:2]
            out_copies = [stack_copies(parts, out, sems, sem_qkv + n_qkv) for parts in out_refs]
        for copy in row_copies + table_copies:
            copy.start()
        if kind == "backward":
            start_copies(pick_ref, out_copies)
            start_copies(pick_ref, qkv_copies)
            d_heads, normed_ref = refs[2:]
            more = load_rows(normed[1], normed_refs, normed_ref, sems, sem_more)
            for copy in more:
                copy.start()
        else:
            start_copies(pick_ref, qkv_copies)
            if n_out:
                start_copies(pick_ref, out_copies)
        for copy in row_copies + table_copies:
            copy.wait()

        if kind == "project":
            project(rows_ref, qkv, qkv_copies[0], cosine, sine, results[0], total)
            return

        if kind == "forward":
            heads = refs[2]
            project(rows_ref, qkv, qkv_copies[0], cosine, sine, heads, total)
            for b in range(2):
                at = slice(b * half, (b + 1) * half)
                query = stack_query(heads, b, half, groups)
                kept = jnp.concatenate([keep[at, :]] * groups, axis=0)
                probs = probabilities(query, heads[at, groups * HD : (groups + 1) * HD], kept)
                got = dot(probs.astype(BF), heads[at, (groups + 1) * HD :]).astype(BF)
                for g in range(groups):
                    mixed[at, g * HD : (g + 1) * HD] = got[g * half : (g + 1) * half]
            for copy in out_copies[0]:
                copy.wait()

            def give(k, carry):
                at = pl.ds(pl.multiple_of(k * step, step), step)
                term = turned_dot(mixed[...], out[at, :]).astype(BF)
                results[0][:, at] = term[:half]
                results[1][:, at] = term[half:]
                return carry

            lax.fori_loop(0, CHUNKS, give, 0)
            return

        total[:, :o_wide] = jnp.zeros((rows, o_wide), F32)
        for k in range(CHUNKS):
            out_copies[0][k].wait()
            at = pl.ds(k * step, step)
            total[:, :o_wide] += dot(rows_ref[:, at], out[at, :])
        mixed[...] = total[:, :o_wide].astype(BF)
        for b in range(2):
            at = slice(b * half, (b + 1) * half)
            query = stack_query(heads, b, half, groups)
            push = stack_query(mixed, b, half, groups)
            key = heads[at, groups * HD : (groups + 1) * HD]
            value = heads[at, (groups + 1) * HD :]
            kept = jnp.concatenate([keep[at, :]] * groups, axis=0)
            probs = probabilities(query, key, kept)
            d_probs = turned_dot(push, value)
            centre = jnp.sum(d_probs * probs, axis=-1, keepdims=True)
            d_scores = (probs * (d_probs - centre) * (1.0 / math.sqrt(HD))).astype(BF)
            over_rows = (((0,), (0,)), ((), ()))
            d_value = lax.dot_general(probs.astype(BF), push, over_rows, preferred_element_type=F32)
            d_key = lax.dot_general(d_scores, query, over_rows, preferred_element_type=F32)
            d_query = dot(d_scores, key)
            c, s = cosine[at, :], sine[at, :]
            for g in range(groups):
                piece = d_query[g * half : (g + 1) * half]
                d_heads[at, g * HD : (g + 1) * HD] = turn_heads(piece, c, s, 1, True)[0].astype(BF)
            d_heads[at, groups * HD : (groups + 1) * HD] = turn_heads(d_key, c, s, 1, True)[0].astype(BF)
            d_heads[at, (groups + 1) * HD :] = d_value.astype(BF)
        for copy in qkv_copies[0]:
            copy.wait()
        for copy in more:
            copy.wait()

        def give_back(k, carry):
            at = pl.ds(pl.multiple_of(k * step, step), step)
            term = turned_dot(d_heads[...], qkv[at, :])
            results[2][:, at] = jnp.sum(
                term * normed_ref[:, at].astype(F32), axis=0, keepdims=True
            )
            term = term.astype(BF)
            results[0][:, at] = term[:half]
            results[1][:, at] = term[half:]
            return carry

        lax.fori_loop(0, CHUNKS, give_back, 0)

    outs = {
        "forward": (shape((half, width)),) * 2,
        "project": shape((rows, q_wide)),
        "backward": (shape((half, width)),) * 2 + (shape((1, width), F32),),
    }[kind]
    scratch = [
        pltpu.VMEM((rows, width), BF),
        pltpu.VMEM((width, q_wide), BF),
        pltpu.VMEM((rows, q_wide), F32),
        pltpu.SemaphoreType.DMA((2 * n_rows + 3 + n_qkv + n_out,)),
    ] + [pltpu.VMEM((rows, table.shape[-1]), F32) for table in tables]
    if n_out:
        scratch += [pltpu.VMEM((width, o_wide), BF), pltpu.VMEM((rows, o_wide), BF)]
        scratch += [pltpu.VMEM((rows, q_wide), BF)]
    args = [pick, *rows_in, *tables]
    specs = [SM] + [HB] * (n_rows + 3)
    for parts in list(qkv_sets) + list(out_sets):
        args += parts
        specs += [HB] * len(parts)
    if kind == "backward":
        args += [saved, *normed[0]]
        specs += [VM] + [HB] * n_rows
        scratch += [pltpu.VMEM((rows, width), BF)]
    flops = 2 * rows * width * (q_wide + o_wide)
    return kernel_call(body, outs, specs, scratch, flops=flops, moved=14 << 20)(*args)


def all_tables(ids, z):
    count = ids.shape[-1]
    block = count // 4
    row = jnp.arange(count, dtype=jnp.int32)
    own = (z + jnp.array(RING, jnp.int32)) % 4
    index = (own[:, None] * block + jnp.arange(block, dtype=jnp.int32)).reshape(count)
    picked = (index[:, None] == row).astype(F32)
    ids = ids.astype(F32)
    relative = jnp.sum(ids[:, :, None, :] * picked, axis=-1)
    starts = jnp.sum((ids[:, :, None, :] < relative[:, :, :, None]).astype(F32), axis=-1)
    positions = index.astype(F32) - starts
    halfway = HD // 2
    frequency = jnp.exp(jnp.arange(halfway, dtype=F32) * (-2.0 * math.log(ROPE_BASE) / HD))
    angles = positions[..., None] * frequency
    cosine, sine = jnp.cos(angles), jnp.sin(angles)
    cosine = jnp.concatenate([cosine, cosine], axis=-1).reshape(4, 2 * count, HD)
    sine = jnp.concatenate([-sine, sine], axis=-1).reshape(4, 2 * count, HD)
    kept = (relative[..., :, None] == relative[..., None, :]) & (index[:, None] >= index[None, :])
    return cosine, sine, kept.astype(F32).reshape(4, 2 * count, count)


def sum_gains(part):
    order = chip_order()[1]
    part = part + shift(part, "z", 2)
    part = part + shift(part, "z", 1)
    part = part + chip_move(part, SIBLING)
    block = part.shape[1] // 16
    part = jnp.take(part.reshape(2, 16, block), order, axis=1).reshape(part.shape)
    part = part + shift(part, "y", 2)
    part = part + shift(part, "y", 1)
    part = part + chip_move(part, BESIDE)
    other = chip_move(part, ACROSS)
    return jnp.where(lax.axis_index("s") == lax.axis_index("xh"), part, other)


def chip_order():
    y, x = lax.axis_index("y"), lax.axis_index("xh") * 2 + lax.axis_index("xl")
    ring, near = jnp.array(RING, jnp.int32), jnp.array(NEAR, jnp.int32)
    place = ((y + ring) % 4)[:, None] * 4 + jnp.bitwise_xor(x, near)[None, :]
    every = jnp.arange(4, dtype=jnp.int32)
    ring_back, near_back = jnp.array(RING_BACK, jnp.int32), jnp.array(RING_BACK, jnp.int32)
    back_y = jnp.sum(
        jnp.where(((every - y) % 4)[:, None] == every[None, :], ring_back[None, :], 0), axis=1
    )
    back_x = jnp.sum(
        jnp.where(jnp.bitwise_xor(every, x)[:, None] == every[None, :], near_back[None, :], 0),
        axis=1,
    )
    back = back_y[:, None] * 4 + back_x[None, :]
    return place.reshape(16).astype(jnp.int32), back.reshape(16).astype(jnp.int32)


def per_device(
    fwd_state, bwd_state, stash, gains, w_query, w_key, w_value, w_out, fwd_segments, bwd_segments
):
    a, core, z = lax.axis_index("xh"), lax.axis_index("s"), lax.axis_index("z")
    match = core == a
    one = lambda v: v.astype(jnp.int32).reshape(1)
    place, back = chip_order()
    across = jnp.array([4 * y + (x ^ 1) for y in range(4) for x in range(4)], jnp.int32)

    kept0, home0, kept1, home1 = split_weights(
        one(a), w_query[0], w_key[0], w_value[0], w_out[0]
    )
    home1 = chip_move(home1, HOME)
    guest1 = chip_move(kept1, GUEST)
    local = jnp.concatenate([fwd_state, bwd_state, stash[0]], axis=0)
    own_ids = jnp.stack([fwd_segments[:, 0], bwd_segments[:, 0]])
    gains_sibling = chip_move(gains[0], SIBLING)
    partner_ids = chip_move(own_ids, ACROSS)
    q1, o1 = join_slots(one(match), kept1, home1, guest1)

    q1_x, o1_x = beside(q1), beside(o1)
    q1_b, q1_a = y_both(q1)
    o1_b, o1_a = y_both(o1)
    guest_rows = chip_move(local, GUEST)
    home0 = chip_move(home0, HOME)
    guest0 = chip_move(kept0, GUEST)
    ids = jnp.stack(
        [jnp.where(match, own_ids, partner_ids), jnp.where(match, partner_ids, own_ids)],
        axis=2,
    )
    ids = jnp.where(a == 0, ids, ids[:, ::-1]).reshape(4, 2, -1)
    all_cosines, all_sines, all_kept = lax.optimization_barrier(all_tables(ids, z))
    scalars = jnp.stack([match.astype(jnp.int32), a.astype(jnp.int32)])
    rows, state, grad, *stash_rows = start_rows(
        scalars, place, local, guest_rows, gains[0], gains_sibling
    )
    stash_rows, stash_scale, (gain_one, gain_late) = stash_rows[:2], stash_rows[2:4], stash_rows[4:]
    o1_o = shift(o1_b, "y", 1)
    o1_bx, o1_ax = beside(o1_b), beside(o1_a)
    q1_xb, q1_xa = y_both(q1_x)
    q1_o = shift(q1_b, "y", 1)
    q0, o0 = join_slots(one(match), kept0, home0, guest0)
    o0_b, o0_a = y_both(o0)
    q0_x = beside(q0)
    rows_b, rows_a = gather_near(rows)
    rows_s = chip_move(rows, SIBLING)
    q1_ox = shift(q1_xa, "y", -1)
    q0_b, q0_a = y_both(q0)
    o1_ox, o0_x = beside(o1_o), beside(o0)
    rows_o = shift(rows_b, "z", 1)
    rows_bs, rows_as = chip_move(rows_b, SIBLING), chip_move(rows_a, SIBLING)
    o0_o = shift(o0_a, "y", -1)
    o0_bx, o0_ax = beside(o0_b), beside(o0_a)
    q0_xb, q0_xa = y_both(q0_x)
    q0_o = shift(q0_b, "y", 1)
    rows_os = chip_move(rows_o, SIBLING)
    q0_ox = shift(q0_xa, "y", -1)
    o0_ox = beside(o0_o)
    entering = (rows, rows_b, rows_a, rows_o, rows_s, rows_bs, rows_as, rows_os)

    qkv_parts = [
        [q0, q0_x, q0_b, q0_xb, q0_a, q0_xa, q0_o, q0_ox],
        [q1, q1_x, q1_b, q1_xb, q1_a, q1_xa, q1_o, q1_ox],
    ]
    out_parts = [
        [o0, o0_x, o0_b, o0_bx, o0_a, o0_ax, o0_o, o0_ox],
        [o1, o1_x, o1_b, o1_bx, o1_a, o1_ax, o1_o, o1_ox],
    ]
    gain_bwd = (gain_one, gain_late)

    tables = [(k, all_cosines, all_sines, all_kept) for k in range(4)]

    late = one(jnp.where(a == 0, 1, 0))
    fwd_in, fwd_at = entering, 0
    cotangent, cot_at = entering, 1
    stash_in = ((entering, 2), (entering, 3))
    sets = (qkv_parts, out_parts)
    gain_sum = []
    for tick in range(2):
        spans_fwd, spans_bwd = (([0], [1]), ([0, 1], [0, 1]))[tick]
        qkv_fwd, out_fwd = ([table[s] for s in spans_fwd] for table in sets)
        qkv_bwd, out_bwd = ([table[s] for s in spans_bwd] for table in sets)
        mine, other = layer_call("forward", fwd_in, fwd_at, tables[tick], late, qkv_fwd, out_fwd)
        entering_stash, stash_at = stash_in[tick]
        heads = layer_call("project", entering_stash, stash_at, tables[2 + tick], late, qkv_bwd, [])
        b_mine, b_other, gain_part = layer_call(
            "backward",
            cotangent,
            cot_at,
            tables[2 + tick],
            late,
            qkv_bwd,
            out_bwd,
            saved=heads,
            normed=stash_in[tick],
        )
        gain_sum.append(gain_part / gain_bwd[tick])
        order = across if tick == 0 else back
        pushed = scatter_rows(b_mine, b_other)
        grad = finish_backward(
            order, pushed, grad, stash_rows[tick], stash_scale[tick], gain_bwd[tick]
        )
        state = finish_forward(order, scatter_rows(mine, other), state)
        if tick == 0:
            state = chip_move(state, ACROSS)
            grad = chip_move(grad, ACROSS)
            fwd_in, fwd_at = gather_rows(norm_rows(state, gain_late)), None
            cotangent, cot_at = gather_rows(grad), None

    state_out = chip_move(state, HOME)
    grad_out = chip_move(grad, HOME)
    on_first = jnp.where(a == 1, 1.0, 0.0)
    gain_rows = jnp.concatenate(
        [gain_sum[1] * on_first, gain_sum[0] + gain_sum[1] * (1.0 - on_first)], axis=0
    )
    gain_total = sum_gains(gain_rows)
    return (state_out[None], grad_out[None], gain_total[None])


def solution(mesh):
    grid = Mesh(mesh.devices.reshape(4, 2, 2, 2, 4), ("y", "xh", "xl", "s", "z"))
    dp = ("y", "xh", "xl")
    in_specs = (
        P("s", dp + ("z",), None),
        P("s", dp + ("z",), None),
        P("s", None, dp + ("z",), None),
        P("s", None, None),
        P("s", None, dp, "z"),
        P("s", None, dp, "z"),
        P("s", None, dp, "z"),
        P("s", None, "z", dp),
        P(None, dp, None),
        P(None, dp, None),
    )
    out_specs = (
        P("s", dp + ("z",), None),
        P("s", dp + ("z",), None),
        P("s", None, None),
    )

    return jax.shard_map(
        per_device, mesh=grid, in_specs=in_specs, out_specs=out_specs, check_vma=False
    )
```
